32 devices in a mesh: fsdp: 2 (over y), ctx: 4 (over z), tp: 4 (over x, core).
Axes of the slice: x: 2, y: 2, z: 4, core: 2. Of those that a mesh axis runs over, the one named last changes fastest.
Arguments:
- tokens: bfloat16 [4, 4, 1024, 1024], P(None, 'fsdp', 'ctx', 'tp'), may hold values from -6 to 6
- skip_tokens: bfloat16 [4, 4, 1024, 1024], P(None, 'fsdp', 'ctx', 'tp'), may hold values from -6 to 6
- merger_weight: bfloat16 [1024, 2, 1024], P(('fsdp', 'ctx'), None, 'tp'), may hold values from -0.125 to 0.125
- merger_bias: float32 [1024], P(('fsdp', 'ctx', 'tp')), may hold values from -3 to 3
- first_gain: float32 [1024], P(('fsdp', 'ctx', 'tp')), may hold values from 0.25 to 1.75
- first_shift: float32 [1024], P(('fsdp', 'ctx', 'tp')), may hold values from -2 to 2
- attend_weight: bfloat16 [1024, 3, 1024], P(('fsdp', 'ctx'), None, 'tp'), may hold values from -0.25 to 0.25
- output_weight: bfloat16 [1024, 1024], P(('fsdp', 'ctx'), 'tp'), may hold values from -0.75 to 0.75
- output_bias: float32 [1024], P(('fsdp', 'ctx', 'tp')), may hold values from -2 to 2
- second_gain: float32 [1024], P(('fsdp', 'ctx', 'tp')), may hold values from 0.25 to 1.75
- second_shift: float32 [1024], P(('fsdp', 'ctx', 'tp')), may hold values from -2 to 2
- expand_weight: bfloat16 [1024, 4096], P(('fsdp', 'ctx'), 'tp'), may hold values from -0.1875 to 0.1875
- widen_bias: float32 [4096], P(('fsdp', 'ctx', 'tp')), may hold values from -3 to 3
- shrink_weight: bfloat16 [1024, 4096], P(('fsdp', 'ctx'), 'tp'), may hold values from -0.125 to 0.125
- shrink_bias: float32 [1024], P(('fsdp', 'ctx', 'tp')), may hold values from -2 to 2
- live_slots: int32 [4, 4], P(None, 'fsdp'), may hold values from 0 to 1, as said below
- cotangent: bfloat16 [4, 4, 1024, 1024], P(None, 'fsdp', ('ctx', 'tp')), may hold values from -6 to 6
Outputs:
- layer_out: bfloat16 [4, 4, 1024, 1024], P(None, 'fsdp', ('ctx', 'tp'))
- grad_tokens: float32 [4, 4, 1024, 1024], P(None, 'fsdp', 'ctx', 'tp')
- grad_skip: float32 [4, 4, 1024, 1024], P(None, 'fsdp', 'ctx', 'tp')
- weight_merger: float32 [1024, 2, 1024], P(('fsdp', 'ctx'), None, 'tp')
- bias_merger: float32 [1024], P(('fsdp', 'ctx', 'tp'))
- gain_first: float32 [1024], P(('fsdp', 'ctx', 'tp'))
- shift_first: float32 [1024], P(('fsdp', 'ctx', 'tp'))
- weight_attend: float32 [1024, 3, 1024], P(('fsdp', 'ctx'), None, 'tp')
- weight_output: float32 [1024, 1024], P(('fsdp', 'ctx'), 'tp')
- bias_output: float32 [1024], P(('fsdp', 'ctx', 'tp'))
- gain_second: float32 [1024], P(('fsdp', 'ctx', 'tp'))
- shift_second: float32 [1024], P(('fsdp', 'ctx', 'tp'))
- weight_expand: float32 [1024, 4096], P(('fsdp', 'ctx'), 'tp')
- bias_expand: float32 [4096], P(('fsdp', 'ctx', 'tp'))
- weight_shrink: float32 [1024, 4096], P(('fsdp', 'ctx'), 'tp')
- bias_shrink: float32 [1024], P(('fsdp', 'ctx', 'tp'))
The draws below stay inside these ranges and needn't reach their ends.
Inputs may be any that keep to these rules, and one draw needn't show every extreme that they name: `live_slots`: in every micro-batch but the last exactly one of the 4 slots is empty (0), in the last exactly two; the empty slots lie anywhere.
All inputs are finite; a program needn't handle non-finite values.
Results may differ from the reference program's by a relative error of at most 0.017.
Values may be sent and summed in bfloat16 or wider, within the bound.
No kernel may reach another device: no remote copies, remote signals or barrier semaphores. Data moves between devices by JAX's collectives and lax.ppermute only.
A program may use at most 256 MiB of HBM per device.

```python
import jax
import jax.numpy as jnp
from jax import lax

D = 1024
HEADS = 16
HD = 64
FF = 4096
L = 1024
MICRO_BATCHES = 4
SEQS = 4


def draw_live_slots(key, part):
    orders = []
    for batch_index in range(MICRO_BATCHES):
        orders.append(jax.random.permutation(jax.random.fold_in(key, batch_index + 11), SEQS))
    sorted_order = jnp.stack(orders, axis=0)
    blank_buffers = jnp.where(jnp.arange(MICRO_BATCHES)[:, None] == MICRO_BATCHES - 1, 2, 1)
    return (sorted_order >= blank_buffers).astype(jnp.int32)


def shard_levels(stream_key, dims, cuts, smallest, high):
    loudness, own = 1.0, jax.random.fold_in(stream_key, 6)
    for position, parts in cuts:
        draws = jnp.exp(jax.random.uniform(jax.random.fold_in(own, position), (parts,), jnp.float32, smallest / len(cuts), high / len(cuts)))
        loudness = loudness * jnp.repeat(draws, dims[position] // parts).reshape([-1 if axis == position else 1 for axis in range(len(dims))])
    return loudness


def gaussian(key, shape, scale, bound, cuts=(), kind=jnp.bfloat16):
    array = scale * jax.random.normal(key, shape, jnp.float32)
    if cuts:
        array = array * shard_levels(key, shape, cuts, -0.22, 0.18)
    return jnp.clip(array, -bound, bound).astype(kind)


def setup_inputs(seed: int = 0) -> dict:
    streams_of = jax.random.split(jax.random.key(seed), 18)
    return {
        "tokens": gaussian(streams_of[0], (MICRO_BATCHES, SEQS, L, D), 1.0, 6.0, ((1, 2), (2, 4), (3, 4))),
        "skip_tokens": gaussian(streams_of[1], (MICRO_BATCHES, SEQS, L, D), 1.0, 6.0, ((1, 2), (2, 4), (3, 4))),
        "merger_weight": gaussian(streams_of[2], (D, 2, D), (2 * D) ** -0.5, 0.125, ((0, 8), (2, 4))),
        "merger_bias": gaussian(streams_of[3], (D,), 0.5, 3.0, ((0, 32),), jnp.float32),
        "first_gain": jnp.clip(1.0 + 0.15 * jax.random.normal(streams_of[4], (D,), jnp.float32), 0.25, 1.75),
        "first_shift": gaussian(streams_of[5], (D,), 0.3, 2.0, ((0, 32),), jnp.float32),
        "attend_weight": gaussian(streams_of[6], (D, 3, D), (D // 2) ** -0.5, 0.25, ((0, 8), (2, 4))),
        "output_weight": gaussian(streams_of[7], (D, D), (D // 16) ** -0.5, 0.75, ((0, 8), (1, 4))),
        "output_bias": gaussian(streams_of[8], (D,), 0.3, 2.0, ((0, 32),), jnp.float32),
        "second_gain": jnp.clip(1.0 + 0.15 * jax.random.normal(streams_of[9], (D,), jnp.float32), 0.25, 1.75),
        "second_shift": gaussian(streams_of[10], (D,), 0.3, 2.0, ((0, 32),), jnp.float32),
        "expand_weight": gaussian(streams_of[11], (D, FF), D ** -0.5, 0.1875, ((0, 8), (1, 4))),
        "widen_bias": gaussian(streams_of[12], (FF,), 0.5, 3.0, ((0, 32),), jnp.float32),
        "shrink_weight": gaussian(streams_of[13], (D, FF), (FF // 2) ** -0.5, 0.125, ((0, 8), (1, 4))),
        "shrink_bias": gaussian(streams_of[14], (D,), 0.3, 2.0, ((0, 32),), jnp.float32),
        "live_slots": draw_live_slots(jax.random.fold_in(streams_of[17], 71), 0),
        "cotangent": gaussian(streams_of[16], (MICRO_BATCHES, SEQS, L, D), 1.0, 6.0, ((1, 2), (2, 16))),
    }


@jax.custom_vjp
def low(v):
    return lax.optimization_barrier(v.astype(jnp.bfloat16)).astype(jnp.float32)

@jax.custom_vjp
def low_back(v):
    return v

def low_keep(v):
    return (low(v), None)

def low_pass(kept, grad):
    return (grad,)

def back_keep(v):
    return (v, None)

def back_low(kept, grad):
    return (low(grad),)
low.defvjp(low_keep, low_pass)
low_back.defvjp(back_keep, back_low)
HIGHEST = lax.Precision.HIGHEST
EPSILON = 1e-05

def layer_norm(matrix, scales, shifts):
    center = matrix - lax.optimization_barrier(jnp.mean(matrix, axis=-1, keepdims=True))
    spread = lax.optimization_barrier(jnp.mean(center * center, axis=-1, keepdims=True))
    return center * lax.rsqrt(spread + EPSILON) * scales + shifts

def layer(params, tokens, skip_tokens):
    merger_weight, merger_bias, first_gain, first_shift, attend_weight, output_weight, output_bias, second_gain, second_shift, expand_weight, widen_bias, shrink_weight, shrink_bias = params
    length = tokens.shape[0]
    stacked = jnp.stack([tokens, skip_tokens], axis=1)
    joined = low_back(jnp.einsum('tci,oci->to', stacked, merger_weight, precision=HIGHEST)) + merger_bias
    normed = low(layer_norm(joined, first_gain, first_shift))
    project = jnp.einsum('ti,icj->tcj', normed, attend_weight, precision=HIGHEST)
    queries = low_back(low(project[:, 0])).reshape(length, HEADS, HD)
    key_rows = low_back(low(project[:, 1])).reshape(length, HEADS, HD)
    value_rows = low_back(low(project[:, 2])).reshape(length, HEADS, HD)
    scores = low_back(jnp.einsum('qhd,khd->hqk', queries, key_rows, precision=HIGHEST) * HD ** (-0.5))
    probs_low = low(jax.nn.softmax(scores, axis=-1))
    attended = low_back(low(jnp.einsum('hqk,khd->qhd', probs_low, value_rows, precision=HIGHEST)))
    attended = attended.reshape(length, HEADS * HD)
    second = joined + low_back(jnp.einsum('ti,oi->to', attended, output_weight, precision=HIGHEST)) + output_bias
    normed_two = low(layer_norm(second, second_gain, second_shift))
    widened_hidden = low_back(jnp.einsum('ti,if->tf', normed_two, expand_weight, precision=HIGHEST) + widen_bias)
    activated = low(jax.nn.gelu(widened_hidden, approximate=False))
    return second + low_back(jnp.einsum('tf,of->to', activated, shrink_weight, precision=HIGHEST)) + shrink_bias

def reference(tokens, skip_tokens, merger_weight, merger_bias, first_gain, first_shift, attend_weight, output_weight, output_bias, second_gain, second_shift, expand_weight, widen_bias, shrink_weight, shrink_bias, live_slots, cotangent):
    params = tuple((member.astype(jnp.float32) for member in (merger_weight, merger_bias, first_gain, first_shift, attend_weight, output_weight, output_bias, second_gain, second_shift, expand_weight, widen_bias, shrink_weight, shrink_bias)))
    flat_tokens = tokens.reshape(MICRO_BATCHES * SEQS, L, D)
    flat_skip = skip_tokens.reshape(MICRO_BATCHES * SEQS, L, D)
    flat_cot = cotangent.reshape(MICRO_BATCHES * SEQS, L, D)
    flat_live = live_slots.reshape(MICRO_BATCHES * SEQS)

    def per_slot(running, member):
        one_tokens, one_skip, one_live, one_cot = member
        result, pullback = jax.vjp(layer, params, one_tokens.astype(jnp.float32), one_skip.astype(jnp.float32))
        live_weight = one_live.astype(jnp.float32)
        grads, grad_one, gradient_remaining = pullback(one_cot.astype(jnp.float32) * live_weight)
        running = jax.tree.map(lambda former, latter: former + latter, running, grads)
        return (running, ((result * live_weight).astype(jnp.bfloat16), grad_one, gradient_remaining))
    initial = tuple((jnp.zeros_like(member) for member in params))
    totals, (layer_out, grad_tokens, grad_skip) = lax.scan(per_slot, initial, (flat_tokens, flat_skip, flat_live, flat_cot))
    return (layer_out.reshape(MICRO_BATCHES, SEQS, L, D), grad_tokens.reshape(MICRO_BATCHES, SEQS, L, D), grad_skip.reshape(MICRO_BATCHES, SEQS, L, D), totals[0], totals[1], totals[2], totals[3], totals[4], totals[5], totals[6], totals[7], totals[8], totals[9], totals[10], totals[11], totals[12])
```

```python
import functools

import jax
import jax.numpy as jnp
from jax import lax
from jax.experimental import pallas as pl
from jax.experimental.pallas import tpu as pltpu
from jax.sharding import PartitionSpec as P

HD = 64
EPSILON = 1e-05
F32 = jnp.float32
BF16 = jnp.bfloat16
ALL = ("fsdp", "ctx", "tp")


def dot(form, a, b):
    return jnp.einsum(form, a, b, preferred_element_type=F32)


def attend_forward_body(heads, q_ref, k_ref, v_ref, p_ref, o_ref):
    q = q_ref[0] * jnp.asarray(HD**-0.5, BF16)
    k = k_ref[0]
    v = v_ref[0]
    width = heads * HD
    lanes = lax.broadcasted_iota(jnp.int32, q.shape, 1) // HD
    rows = lax.broadcasted_iota(jnp.int32, (width, q.shape[0]), 0) // HD
    total = jnp.zeros((width, q.shape[0]), F32)
    for h in range(heads):
        q_h = jnp.where(lanes == h, q, jnp.zeros_like(q))
        s = lax.dot_general(k, q_h, (((1,), (1,)), ((), ())), preferred_element_type=F32)
        p = jnp.exp(s - jnp.max(s, axis=0, keepdims=True))
        low = (p * (1.0 / jnp.sum(p, axis=0, keepdims=True))).astype(BF16)
        p_ref[0, h] = low
        o_h = lax.dot_general(v, low, (((0,), (0,)), ((), ())), preferred_element_type=F32)
        total = total + jnp.where(rows == h, o_h, 0.0)
    o_ref[0] = total.T.astype(BF16)


def attend_forward(q, k, v):
    blocks, count, width = q.shape
    keys = k.shape[1]
    per = min(width, 128)
    heads = per // HD
    cols = width // per
    return pl.pallas_call(
        functools.partial(attend_forward_body, heads),
        grid=(blocks, cols),
        in_specs=[
            pl.BlockSpec((1, count, per), lambda t, j: (t, 0, j)),
            pl.BlockSpec((1, keys, per), lambda t, j: (t, 0, j)),
            pl.BlockSpec((1, keys, per), lambda t, j: (t, 0, j)),
        ],
        out_specs=[
            pl.BlockSpec((1, heads, keys, count), lambda t, j: (t, j, 0, 0)),
            pl.BlockSpec((1, count, per), lambda t, j: (t, 0, j)),
        ],
        out_shape=[
            jax.ShapeDtypeStruct((blocks, width // HD, keys, count), BF16),
            jax.ShapeDtypeStruct((blocks, count, width), BF16),
        ],
        compiler_params=pltpu.CompilerParams(vmem_limit_bytes=48 * 1024 * 1024),
        name="attend_forward",
    )(q, k, v)


def attend_backward_body(heads, q_ref, k_ref, v_ref, p_ref, o_ref, g_ref, dq_ref, dk_ref, dv_ref):
    q = q_ref[0] * jnp.asarray(HD**-0.5, BF16)
    k = k_ref[0]
    v = v_ref[0]
    g = g_ref[0]
    width = heads * HD
    count = q.shape[0]
    keys = k.shape[0]
    lanes = lax.broadcasted_iota(jnp.int32, q.shape, 1) // HD
    rows = lax.broadcasted_iota(jnp.int32, (width, count), 0) // HD
    prod = (g.astype(F32) * o_ref[0].astype(F32)).T
    dq = jnp.zeros((width, count), F32)
    dk = jnp.zeros((keys, width), F32)
    dv = jnp.zeros((keys, width), F32)
    for h in range(heads):
        q_h = jnp.where(lanes == h, q, jnp.zeros_like(q))
        g_h = jnp.where(lanes == h, g, jnp.zeros_like(g))
        p = p_ref[0, h]
        dp = lax.dot_general(v, g_h, (((1,), (1,)), ((), ())), preferred_element_type=F32)
        delta = jnp.sum(prod[h * HD : (h + 1) * HD], axis=0, keepdims=True)
        ds = (p.astype(F32) * (dp - delta)).astype(BF16)
        dq_h = lax.dot_general(k, ds, (((0,), (0,)), ((), ())), preferred_element_type=F32)
        dq = dq + jnp.where(rows == h, dq_h, 0.0)
        dk = dk + lax.dot_general(ds, q_h, (((1,), (0,)), ((), ())), preferred_element_type=F32)
        dv = dv + lax.dot_general(p, g_h, (((1,), (0,)), ((), ())), preferred_element_type=F32)
    dq_ref[0] = (dq.T * (HD**-0.5)).astype(BF16)
    dk_ref[0] = dk.astype(BF16)
    dv_ref[0] = dv.astype(BF16)


def attend_backward(q, k, v, p, o, g):
    blocks, count, width = q.shape
    keys = k.shape[1]
    per = min(width, 128)
    heads = per // HD
    cols = width // per
    q_spec = pl.BlockSpec((1, count, per), lambda t, j: (t, 0, j))
    k_spec = pl.BlockSpec((1, keys, per), lambda t, j: (t, 0, j))
    p_spec = pl.BlockSpec((1, heads, keys, count), lambda t, j: (t, j, 0, 0))
    return pl.pallas_call(
        functools.partial(attend_backward_body, heads),
        grid=(blocks, cols),
        in_specs=[q_spec, k_spec, k_spec, p_spec, q_spec, q_spec],
        out_specs=[q_spec, k_spec, k_spec],
        out_shape=[
            jax.ShapeDtypeStruct(q.shape, BF16),
            jax.ShapeDtypeStruct(k.shape, BF16),
            jax.ShapeDtypeStruct(v.shape, BF16),
        ],
        compiler_params=pltpu.CompilerParams(vmem_limit_bytes=48 * 1024 * 1024),
        name="attend_backward",
    )(q, k, v, p, o, g)


def norm_stats(matrix):
    center = matrix - jnp.mean(matrix, axis=-1, keepdims=True)
    spread = jnp.mean(center * center, axis=-1, keepdims=True)
    scale = lax.rsqrt(spread + EPSILON)
    return center * scale, scale


def norm_back(grad, unit, scale, gain):
    z = grad * gain
    inner = z - jnp.mean(z, axis=-1, keepdims=True) - unit * jnp.mean(z * unit, axis=-1, keepdims=True)
    return scale * inner


def gelu_pair(v):
    half = 0.5 * (1.0 + lax.erf(v * (0.5**0.5)))
    slope = half + v * jnp.exp(-0.5 * v * v) * 0.3989422804014327
    return v * half, slope


def pick(array, index, axis):
    return lax.dynamic_index_in_dim(array, index, axis, keepdims=False)


def swap_pairs(size, bit):
    if bit == 0:
        return [(i, i ^ 1) for i in range(size)]
    half = size // 2
    return [(i, (i // 2 + half // 2) % half * 2 + i % 2) for i in range(size)]


def chain_reduce(part, axis, size, rank, lead):
    up_pairs = [(i, i + 1) for i in range(size - 1)]
    down_pairs = [(i + 1, i) for i in range(size - 1)]
    up = down = None
    for step in range(size - 1):
        up_send = pick(part, jnp.clip(size - 1 - step + rank, 0, size - 1), lead)
        down_send = pick(part, jnp.clip(step - (size - 1 - rank), 0, size - 1), lead)
        if step:
            up_send = (up_send.astype(F32) + up.astype(F32)).astype(BF16)
            down_send = (down_send.astype(F32) + down.astype(F32)).astype(BF16)
        up = lax.ppermute(up_send, axis, up_pairs)
        down = lax.ppermute(down_send, axis, down_pairs)
    own = pick(part, rank, lead).astype(F32)
    if size > 1:
        own = own + up.astype(F32) + down.astype(F32)
    return own


def swap_reduce(part, axis, pairs, index, lead):
    got = lax.ppermute(pick(part, 1 - index, lead), axis, pairs)
    return (pick(part, index, lead).astype(F32) + got.astype(F32)).astype(BF16)


def sum_to_owner(grad, sizes, ranks, y_first):
    fs, cs, ts = sizes
    f_rank, c_rank, t_rank = ranks
    rows = grad.shape[1] // (fs * cs)
    part = grad.reshape(ts // 2, 2, fs, cs, rows, grad.shape[2])
    part = swap_reduce(part, "tp", swap_pairs(ts, 0), t_rank % 2, 1)

    def over_x(part):
        if ts == 2:
            return pick(part, 0, 0)
        if ts == 4:
            return swap_reduce(part, "tp", swap_pairs(ts, 1), t_rank // 2, 0)
        raise NotImplementedError

    def over_y(part, lead):
        if fs == 1:
            return pick(part, 0, lead)
        if fs == 2:
            return swap_reduce(part, "fsdp", [(0, 1), (1, 0)], f_rank, lead)
        return chain_reduce(part, "fsdp", fs, f_rank, lead).astype(BF16)

    if y_first:
        part = over_x(over_y(part, 1))
    else:
        part = over_y(over_x(part), 0)
    return chain_reduce(part, "ctx", cs, c_rank, 0)


def on_device(
    sizes,
    tokens,
    skip_tokens,
    merger_weight,
    merger_bias,
    first_gain,
    first_shift,
    attend_weight,
    output_weight,
    output_bias,
    second_gain,
    second_shift,
    expand_weight,
    widen_bias,
    shrink_weight,
    shrink_bias,
    live_slots,
    cotangent,
):
    fs, cs, ts = sizes
    f_rank, c_rank, t_rank = (lax.axis_index(a) for a in ALL)
    ranks = (f_rank, c_rank, t_rank)
    group = cs * ts
    batches, local_seqs, local_len, part_width = tokens.shape
    slots = batches * local_seqs
    share = group // slots
    fine = cotangent.shape[2] // share
    width = cotangent.shape[3]
    count = cs * ts * fine
    device = c_rank * ts + t_rank

    def gather(part):
        full = lax.all_gather(part, ("tp", "fsdp", "ctx"), axis=0, tiled=True)
        return full.reshape(ts, width, part.shape[1])

    merger = gather(merger_weight.reshape(merger_weight.shape[0], -1))
    attend = gather(attend_weight.reshape(attend_weight.shape[0], -1))
    output = gather(output_weight)
    expand = gather(expand_weight)
    shrink = gather(shrink_weight)

    packed = jnp.concatenate(
        [merger_bias, first_gain, first_shift, output_bias, second_gain, second_shift, shrink_bias, widen_bias]
    )
    packed = lax.all_gather(packed, ALL, axis=0, tiled=False)
    small = merger_bias.shape[0]
    vectors = [packed[:, i * small : (i + 1) * small].reshape(-1) for i in range(7)]
    merger_bias, first_gain, first_shift, output_bias, second_gain, second_shift, shrink_bias = vectors
    hidden = expand_weight.shape[1]
    widen_bias = packed[:, 7 * small :].reshape(ts, 1, hidden)

    def to_group(array):
        return lax.all_to_all(array, ("ctx", "tp"), 0, 0, tiled=True)

    def split_rows(array):
        feats = array.shape[-1]
        array = array.reshape(slots, ts, share, fine, feats).transpose(0, 2, 1, 3, 4)
        return array.reshape(group, ts * fine, feats)

    both = to_group(split_rows(jnp.concatenate([tokens, skip_tokens], axis=-1)).reshape(group * ts * fine, -1))
    both = both.reshape(cs, ts, ts * fine, 2 * part_width).transpose(1, 0, 2, 3).reshape(ts, count, 2 * part_width)
    cot = to_group(cotangent.reshape(group * fine, width)).reshape(count, width)
    live = pick(live_slots.reshape(slots), device // share, 0).astype(F32)

    joined = dot("tsi,toi->so", both, merger) + merger_bias
    unit_one, scale_one = norm_stats(joined)
    normed = (unit_one * first_gain + first_shift).astype(BF16)
    project = dot("sd,tdj->tsj", normed, attend).astype(BF16)
    third = project.shape[2] // 3
    queries = project[:, :, :third]
    own_keys = project[:, :, third:]

    def shift_pairs(step):
        return [(i, i // share * share + (i % share + step) % share) for i in range(ts)]

    blocks = [own_keys] + [lax.ppermute(own_keys, "tp", shift_pairs(d)) for d in range(1, share)]
    both_keys = jnp.concatenate(blocks, axis=1)
    key_rows = both_keys[:, :, :third]
    value_rows = both_keys[:, :, third:]
    probs, attended = attend_forward(queries, key_rows, value_rows)
    second = joined + dot("tsi,toi->so", attended, output) + output_bias
    unit_two, scale_two = norm_stats(second)
    normed_two = (unit_two * second_gain + second_shift).astype(BF16)
    expanded = dot("sd,tdf->tsf", normed_two, expand) + widen_bias
    activated, slope = gelu_pair(expanded)
    activated = activated.astype(BF16)
    result = second + dot("tsf,tof->so", activated, shrink) + shrink_bias
    layer_out = (result * live).astype(BF16)
    layer_out = to_group(layer_out.reshape(group * fine, width)).reshape(batches, local_seqs, share * fine, width)

    upstream = cot.astype(F32) * live
    branch_low = upstream.astype(BF16)
    grad_shrink = dot("so,tsf->tof", branch_low, activated).astype(BF16)
    grad_expanded = (dot("so,tof->tsf", branch_low, shrink) * slope).astype(BF16)
    grad_expand = dot("sd,tsf->tdf", normed_two, grad_expanded).astype(BF16)
    grad_normed_two = dot("tsf,tdf->sd", grad_expanded, expand)
    grad_second = upstream + norm_back(grad_normed_two, unit_two, scale_two, second_gain)
    attn_low = grad_second.astype(BF16)
    grad_output = dot("so,tsi->toi", attn_low, attended).astype(BF16)
    grad_attended = dot("so,toi->tsi", attn_low, output).astype(BF16)
    grad_queries, grad_keys, grad_values = attend_backward(
        queries, key_rows, value_rows, probs, attended, grad_attended
    )
    grad_both = jnp.concatenate([grad_keys, grad_values], axis=-1)
    total = grad_both[:, :count].astype(F32)
    for d in range(1, share):
        total = total + lax.ppermute(
            grad_both[:, d * count : (d + 1) * count], "tp", shift_pairs(share - d)
        ).astype(F32)
    grad_project = jnp.concatenate([grad_queries, total.astype(BF16)], axis=-1)
    grad_attend = dot("sd,tsj->tdj", normed, grad_project).astype(BF16)
    grad_normed = dot("tsj,tdj->sd", grad_project, attend)
    grad_joined = grad_second + norm_back(grad_normed, unit_one, scale_one, first_gain)
    joined_low = grad_joined.astype(BF16)
    grad_merger = dot("so,tsi->toi", joined_low, both).astype(BF16)
    grad_inputs = dot("so,toi->tsi", joined_low, merger).astype(BF16)

    out = grad_inputs.reshape(ts, cs, ts * fine, 2 * part_width).transpose(1, 0, 2, 3)
    out = to_group(out.reshape(group * ts * fine, 2 * part_width))
    out = out.reshape(slots, share, ts, fine, 2 * part_width).transpose(0, 2, 1, 3, 4)
    out = out.reshape(batches, local_seqs, local_len, 2 * part_width).astype(F32)

    def rows_sum(array):
        return jnp.sum(array.astype(F32), axis=0)

    sums = [
        rows_sum(grad_joined),
        rows_sum(grad_normed * unit_one),
        rows_sum(grad_normed),
        rows_sum(grad_second),
        rows_sum(grad_normed_two * unit_two),
        rows_sum(grad_normed_two),
        rows_sum(upstream),
    ]
    devices = fs * cs * ts
    vec = jnp.concatenate(
        [v.reshape(devices, small) for v in sums]
        + [jnp.sum(grad_expanded.astype(F32), axis=1).reshape(devices, -1)],
        axis=1,
    )
    vec = jnp.sum(lax.all_to_all(vec, ALL, 0, 0, tiled=True), axis=0)
    vec_out = [vec[i * small : (i + 1) * small] for i in range(7)] + [vec[7 * small :]]

    reduced = [
        sum_to_owner(g, sizes, ranks, y_first)
        for g, y_first in (
            (grad_merger, False),
            (grad_attend, True),
            (grad_output, False),
            (grad_expand, True),
            (grad_shrink, False),
        )
    ]
    return (
        layer_out,
        out[..., :part_width],
        out[..., part_width:],
        reduced[0].reshape(merger_weight.shape),
        vec_out[0],
        vec_out[1],
        vec_out[2],
        reduced[1].reshape(attend_weight.shape),
        reduced[2],
        vec_out[3],
        vec_out[4],
        vec_out[5],
        reduced[3],
        vec_out[7],
        reduced[4],
        vec_out[6],
    )


def solution(mesh):
    sizes = tuple(mesh.shape[a] for a in ALL)
    act = P(None, "fsdp", "ctx", "tp")
    vec = P(ALL)
    flat = P(None, "fsdp", ("ctx", "tp"), None)
    w_three = P(("fsdp", "ctx"), None, "tp")
    w_two = P(("fsdp", "ctx"), "tp")
    return jax.shard_map(
        functools.partial(on_device, sizes),
        mesh=mesh,
        in_specs=(
            act, act, w_three, vec, vec, vec, w_three, w_two, vec, vec, vec, w_two, vec, w_two, vec,
            P(None, "fsdp"), flat,
        ),
        out_specs=(
            flat, act, act, w_three, vec, vec, vec, w_three, w_two, vec, vec, vec, w_two, vec, w_two, vec,
        ),
        check_vma=False,
    )
```

```python
import functools

import jax
import jax.numpy as jnp
from jax import lax
from jax.experimental import pallas as pl
from jax.experimental.pallas import tpu as pltpu
from jax.sharding import PartitionSpec as P

HD = 64
EPSILON = 1e-05
F32 = jnp.float32
BF16 = jnp.bfloat16
ALL = ("fsdp", "ctx", "tp")
PARAMS = pltpu.CompilerParams(vmem_limit_bytes=56 * 1024 * 1024)
CHUNK = 128


def mxu(a, b, a_dim, b_dim):
    return lax.dot_general(a, b, (((a_dim,), (b_dim,)), ((), ())), preferred_element_type=F32)


def whole(shape):
    return pl.BlockSpec(shape, lambda n: (0,) * len(shape))


def call(body, after, *, in_specs, out_specs, out_shape, grid, name, scratch_shapes=()):
    n_in, n_after, n_out = len(in_specs), len(after), len(out_specs)

    def run(*refs):
        outs = refs[n_in + n_after :]
        outs[n_out][...] = jnp.zeros((8, 128), F32)
        body(*refs[:n_in], *outs[:n_out], *outs[n_out + 1 :])

    def apply(*args):
        outs = pl.pallas_call(
            run,
            grid=grid,
            in_specs=[*in_specs, *[pl.BlockSpec(memory_space=pl.ANY)] * n_after],
            out_specs=[*out_specs, pl.BlockSpec((8, 128), lambda n: (0, 0))],
            out_shape=[*out_shape, jax.ShapeDtypeStruct((8, 128), F32)],
            scratch_shapes=scratch_shapes,
            compiler_params=PARAMS,
            cost_estimate=pl.CostEstimate(flops=1, bytes_accessed=1, transcendentals=0),
            name=name,
        )(*args, *after)
        return outs[:-1], outs[-1]

    return apply


def attend_forward_body(share, heads, *refs):
    own, others = refs[0], refs[1:share]
    p_ref, o_ref = refs[share:]
    part = heads * HD
    rows = lax.broadcasted_iota(jnp.int32, (part, own.shape[1]), 0) // HD
    lanes = lax.broadcasted_iota(jnp.int32, (own.shape[1], part), 1) // HD
    q = own[0, :, :part] * jnp.asarray(HD**-0.5, BF16)
    k = jnp.concatenate([r[0, :, part : 2 * part] for r in (own, *others)], axis=0)
    v = jnp.concatenate([r[0, :, 2 * part :] for r in (own, *others)], axis=0)
    total = jnp.zeros((part, q.shape[0]), F32)
    for h in range(heads):
        s = mxu(k, jnp.where(lanes == h, q, jnp.zeros_like(q)), 1, 1)
        p = jnp.exp(s - jnp.max(s, axis=0, keepdims=True))
        low = (p * (1.0 / jnp.sum(p, axis=0, keepdims=True))).astype(BF16)
        p_ref[0, h] = low
        total = total + jnp.where(rows == h, mxu(v, low, 0, 0), 0.0)
    o_ref[0] = total.T.astype(BF16)


def other_specs(share, shape):
    return [pl.BlockSpec(shape, lambda x, d=d: (x ^ (d >> 1), 0, 0)) for d in range(1, share)]


def attend_forward(after, own, others):
    blocks, count, cols = own.shape
    share = 1 + len(others)
    part = cols // 3
    heads = part // HD
    return call(
        functools.partial(attend_forward_body, share, heads),
        after,
        grid=(blocks,),
        in_specs=[pl.BlockSpec((1, count, cols), lambda x: (x, 0, 0))] + other_specs(share, (1, count, cols)),
        out_specs=[
            pl.BlockSpec((1, heads, share * count, count), lambda x: (x, 0, 0, 0)),
            pl.BlockSpec((1, count, part), lambda x: (x, 0, 0)),
        ],
        out_shape=[
            jax.ShapeDtypeStruct((blocks, heads, share * count, count), BF16),
            jax.ShapeDtypeStruct((blocks, count, part), BF16),
        ],
        name="attend_forward",
    )(own, *others)


def attend_backward_body(share, heads, *refs):
    own, others = refs[0], refs[1:share]
    p_ref, o_ref, g_ref = refs[share : share + 3]
    outs = refs[share + 3 :]
    part = heads * HD
    count = own.shape[1]
    q = own[0, :, :part] * jnp.asarray(HD**-0.5, BF16)
    k = jnp.concatenate([r[0, :, part : 2 * part] for r in (own, *others)], axis=0)
    v = jnp.concatenate([r[0, :, 2 * part :] for r in (own, *others)], axis=0)
    g = g_ref[0]
    rows = lax.broadcasted_iota(jnp.int32, (part, count), 0) // HD
    lanes = lax.broadcasted_iota(jnp.int32, (count, part), 1) // HD
    prod = (g.astype(F32) * o_ref[0].astype(F32)).T
    dq = jnp.zeros((part, count), F32)
    dk = jnp.zeros((share * count, part), F32)
    dv = jnp.zeros((share * count, part), F32)
    for h in range(heads):
        q_h = jnp.where(lanes == h, q, jnp.zeros_like(q))
        g_h = jnp.where(lanes == h, g, jnp.zeros_like(g))
        p = p_ref[0, h]
        delta = jnp.sum(prod[h * HD : (h + 1) * HD], axis=0, keepdims=True)
        ds = (p.astype(F32) * (mxu(v, g_h, 1, 1) - delta)).astype(BF16)
        dq = dq + jnp.where(rows == h, mxu(k, ds, 0, 0), 0.0)
        dk = dk + mxu(ds, q_h, 1, 0)
        dv = dv + mxu(p, g_h, 1, 0)
    outs[0][0, :, :part] = (dq.T * (HD**-0.5)).astype(BF16)
    outs[0][0, :, part : 2 * part] = dk[:count].astype(BF16)
    outs[0][0, :, 2 * part :] = dv[:count].astype(BF16)
    for d in range(1, share):
        outs[d][0, :, :part] = dk[d * count : (d + 1) * count].astype(BF16)
        outs[d][0, :, part:] = dv[d * count : (d + 1) * count].astype(BF16)


def attend_backward(after, own, others, probs, attended, grad):
    blocks, count, cols = own.shape
    share = 1 + len(others)
    part = cols // 3
    heads = part // HD
    spec = pl.BlockSpec((1, count, cols), lambda x: (x, 0, 0))
    o_spec = pl.BlockSpec((1, count, part), lambda x: (x, 0, 0))
    p_spec = pl.BlockSpec((1, heads, share * count, count), lambda x: (x, 0, 0, 0))
    return call(
        functools.partial(attend_backward_body, share, heads),
        after,
        grid=(blocks,),
        in_specs=[spec] + other_specs(share, (1, count, cols)) + [p_spec, o_spec, o_spec],
        out_specs=[spec] + other_specs(share, (1, count, 2 * part)),
        out_shape=[jax.ShapeDtypeStruct((blocks, count, cols), BF16)]
        + [jax.ShapeDtypeStruct((blocks, count, 2 * part), BF16)] * (share - 1),
        name="attend_backward",
    )(own, *others, probs, attended, grad)


def tree(w):
    return [h[0] for k in w for x in k for h in x]


def weight_specs(w, shape, index):
    return [
        pl.BlockSpec((None, *shape), lambda n, h=h, lead=lead: (lead, *index(h, n)))
        for k in w
        for x in k
        for h, (_, lead) in enumerate(x)
    ]


def up_body(ks, parts, step, *refs):
    left = refs[0]
    count = len(ks) * 2 * parts
    rows = left.shape[1] // parts
    for i in range(len(ks)):
        for x in range(2):
            total = None
            for h in range(parts):
                term = mxu(left[:, h * rows : (h + 1) * rows], refs[1 + (i * 2 + x) * parts + h][...], 1, 0)
                total = term if total is None else total + term
            step(i, x, total, refs[1 + count :])


def up(after, name, left, weights, width, col, step, extras, outs, tile):
    parts = len(weights[0][0])
    rows = weights[0][0][0][0].shape[1]
    per = width // tile
    count = left.shape[0]
    return call(
        functools.partial(up_body, range(len(weights)), parts, step),
        after,
        grid=(per,),
        in_specs=[whole((count, parts * rows))]
        + weight_specs(weights, (rows, tile), lambda h, n: (0, col * per + n))
        + [pl.BlockSpec((2, e.shape[1], tile), lambda n: (0, 0, n)) for e in extras],
        out_specs=[pl.BlockSpec((2, o[0], tile), lambda n: (0, 0, n)) for o in outs],
        out_shape=[jax.ShapeDtypeStruct((2, o[0], width), o[1]) for o in outs],
        name=name,
    )(left, *tree(weights), *extras)


def plain_step(i, x, total, refs):
    refs[i][x] = total.astype(BF16)


def gelu_step(i, x, total, refs):
    bias, act, slope = refs
    v = total + bias[x]
    half = 0.5 * (1.0 + lax.erf(v * (0.5**0.5)))
    act[x] = (v * half).astype(BF16)
    slope[x] = (half + v * jnp.exp(-0.5 * v * v) * 0.3989422804014327).astype(BF16)


def slope_step(i, x, total, refs):
    slope, grad, sums = refs
    low = (total * slope[x].astype(F32)).astype(BF16)
    grad[x] = low
    sums[x] = jnp.sum(low.astype(F32), axis=0, keepdims=True)


def down_body(parts, per, finish, n_out, *refs):
    lefts = refs[:2]
    weights = refs[2 : 2 + 4 * parts]
    rest = refs[2 + 4 * parts : -1]
    acc = refs[-1]
    n = pl.program_id(0)
    for h in range(parts):

        @pl.when(n // per == h)
        def _():
            total = None
            for k in range(2):
                for x in range(2):
                    term = mxu(lefts[k][x], weights[(k * 2 + x) * parts + h][...], 1, 1)
                    total = term if total is None else total + term
            acc[n] = total

    @pl.when(n == parts * per - 1)
    def _():
        finish(acc, rest)


def down(after, name, lefts, weights, width, col, finish, extras, outs):
    parts = len(weights[0][0])
    rows = weights[0][0][0][0].shape[1]
    tile = min(256, rows)
    per = rows // tile
    count = lefts[0].shape[1]
    return call(
        functools.partial(down_body, parts, per, finish, len(outs)),
        after,
        grid=(parts * per,),
        in_specs=[whole((2, count, width))] * 2
        + weight_specs(weights, (tile, width), lambda h, n: (jnp.clip(n - h * per, 0, per - 1), col))
        + [whole(e.shape) for e in extras],
        out_specs=[whole(o[0]) for o in outs],
        out_shape=[jax.ShapeDtypeStruct(*o) for o in outs],
        scratch_shapes=[pltpu.VMEM((parts * per, count, tile), F32)],
        name=name,
    )(*lefts, *tree(weights), *extras)


def row_mean(tiles):
    total = sum(jnp.sum(t, axis=-1, keepdims=True) for t in tiles)
    return total / sum(t.shape[-1] for t in tiles)


def norm_finish(has_residual, acc, refs):
    refs = list(refs)
    residual = refs.pop(0) if has_residual else None
    rows, total_ref, low_ref, low_t_ref = refs
    tiles, count, width = acc.shape
    for r in range(0, count, CHUNK):
        rr = pl.ds(r, CHUNK)
        total = []
        for i in range(tiles):
            cc = slice(i * width, (i + 1) * width)
            v = acc[i, rr, :] + rows[0:1, cc]
            if residual is not None:
                v = v + residual[rr, cc]
            total_ref[rr, cc] = v
            total.append(v)
        mean = row_mean(total)
        center = [t - mean for t in total]
        scale = lax.rsqrt(row_mean([c * c for c in center]) + EPSILON)
        for i in range(tiles):
            cc = slice(i * width, (i + 1) * width)
            v = center[i] * scale * rows[1:2, cc] + rows[2:3, cc]
            low_ref[rr, cc] = v.astype(BF16)
            low_t_ref[cc, rr] = v.T.astype(BF16)


def norm_back_finish(keep, acc, refs):
    total_ref, up_ref, rows, *outs = refs
    full_ref = outs.pop(0) if keep else None
    low_ref, low_t_ref, sums_ref = outs
    tiles, count, width = acc.shape
    zero = jnp.zeros((1, width), F32)
    sums = [[zero] * tiles for _ in range(4)]
    for r in range(0, count, CHUNK):
        rr = pl.ds(r, CHUNK)
        cuts = [slice(i * width, (i + 1) * width) for i in range(tiles)]
        total = [total_ref[rr, cc] for cc in cuts]
        mean = row_mean(total)
        center = [t - mean for t in total]
        scale = lax.rsqrt(row_mean([c * c for c in center]) + EPSILON)
        unit = [c * scale for c in center]
        grad = [acc[i, rr, :] for i in range(tiles)]
        z = [g * rows[0:1, cc] for g, cc in zip(grad, cuts)]
        z_mean = row_mean(z)
        zu_mean = row_mean([a * b for a, b in zip(z, unit)])
        for i, cc in enumerate(cuts):
            up_now = up_ref[rr, cc].astype(F32)
            v = up_now + scale * (z[i] - z_mean - unit[i] * zu_mean)
            if keep:
                full_ref[rr, cc] = v
            low_ref[rr, cc] = v.astype(BF16)
            low_t_ref[cc, rr] = v.T.astype(BF16)
            for j, s in enumerate((v, grad[i] * unit[i], grad[i], up_now)):
                sums[j][i] = sums[j][i] + jnp.sum(s, axis=0, keepdims=True)
    for j in range(4):
        for i in range(tiles):
            sums_ref[j : j + 1, i * width : (i + 1) * width] = sums[j][i]


def out_finish(acc, refs):
    total_ref, rows, low_ref = refs
    tiles, count, width = acc.shape
    for i in range(tiles):
        cc = slice(i * width, (i + 1) * width)
        v = (acc[i] + total_ref[:, cc] + rows[0:1, cc]) * rows[1:2, cc]
        low_ref[:, cc] = v.astype(BF16)


def weight_grad_body(n_parts, parts, by_x, has_more, *refs):
    lefts = refs[: n_parts * parts]
    rights = refs[n_parts * parts : n_parts * (parts + 1)]
    more = refs[n_parts * (parts + 1) :]
    n_out = 2 if by_x else parts
    outs = more[-n_out:]
    for x in range(2):
        for h in range(parts):
            i, j = (x, h) if by_x else (h, x)
            at = 0
            for p in range(n_parts):
                total = mxu(lefts[p * parts + h][...], rights[p][x], 1, 0)
                cc = slice(at, at + total.shape[1])
                at = cc.stop
                if has_more:
                    total = total + more[i][j, :, cc].astype(F32)
                outs[i][j, :, cc] = total.astype(BF16)


def weight_grad(after, lefts, rights, parts, by_x, more=()):
    depth, count = lefts[0].shape
    rows = depth // parts
    tile = min(256, rows)
    per = rows // tile
    cols = sum(r.shape[2] for r in rights)
    n_out, lead = (2, parts) if by_x else (parts, 2)
    out_spec = pl.BlockSpec((lead, tile, cols), lambda n: (0, n, 0))
    return call(
        functools.partial(weight_grad_body, len(lefts), parts, by_x, bool(more)),
        after,
        grid=(per,),
        in_specs=[
            pl.BlockSpec((tile, count), lambda n, h=h: (h * per + n, 0)) for _ in lefts for h in range(parts)
        ]
        + [whole(r.shape) for r in rights]
        + [out_spec] * len(more),
        out_specs=[out_spec] * n_out,
        out_shape=[jax.ShapeDtypeStruct((lead, rows, cols), BF16)] * n_out,
        name="weight_grad",
    )(*[left for left in lefts for _ in range(parts)], *rights, *more)


def pick(array, index, axis=0):
    return lax.dynamic_index_in_dim(array, index, axis, keepdims=False)


def add(*terms):
    return sum(t.astype(F32) for t in terms).astype(BF16)


class Line:
    def __init__(self):
        self.marks = []

    def gate(self, *arrays):
        leaves, form = jax.tree.flatten(arrays)
        places = [i for i, leaf in enumerate(leaves) if isinstance(leaf, jax.Array)]
        held, self.marks = lax.optimization_barrier(([leaves[i] for i in places], self.marks))
        for i, array in zip(places, held):
            leaves[i] = array
        arrays = jax.tree.unflatten(form, leaves)
        return arrays[0] if len(arrays) == 1 else arrays

    def plain(self, step, *args):
        out = step(*self.gate(args, ())[0])
        self.marks = self.marks + jax.tree.leaves(out)
        return out

    def __call__(self, step, *args):
        args = self.gate(args, ())[0]
        out, mark = step(self.marks, *args)
        self.marks = [mark]
        return out


def on_device(
    sizes,
    tokens,
    skip_tokens,
    merger_weight,
    merger_bias,
    first_gain,
    first_shift,
    attend_weight,
    output_weight,
    output_bias,
    second_gain,
    second_shift,
    expand_weight,
    widen_bias,
    shrink_weight,
    shrink_bias,
    live_slots,
    cotangent,
):
    fs, cs, ts = sizes
    assert ts == 4
    f_rank, c_rank, t_rank = (lax.axis_index(a) for a in ALL)
    group = cs * ts
    devices = fs * group
    batches, local_seqs, local_len, part_width = tokens.shape
    slots = batches * local_seqs
    share = group // slots
    assert share in (1, 2, 4)
    fine = cotangent.shape[2] // share
    width = cotangent.shape[3]
    count = group * fine
    hidden = expand_weight.shape[1]
    rows = width // (fs * cs)
    line = Line()

    def to_group(array):
        return lax.all_to_all(array, ("ctx", "tp"), 0, 0, tiled=True)

    def over_tp(array, flip):
        return lax.ppermute(array, "tp", [(i, i ^ flip) for i in range(ts)])

    def over_ctx(array, d):
        return lax.ppermute(array, "ctx", [(i, (i + d) % cs) for i in range(cs)])

    def over_fsdp(array, d):
        return lax.ppermute(array, "fsdp", [(i, (i + d) % fs) for i in range(fs)])

    def gather_ctx(pair):
        return [pair] + [over_ctx(pair, d) for d in range(1, cs)]

    def stack_parts(*moved):
        return [jnp.concatenate([m[i] for m in moved], axis=0) for i in range(2)]

    def gather_one(moved):
        a, b = line.plain(stack_parts, *moved)
        return a, [over_fsdp(a, h) for h in range(1, fs)], b, over_tp(b, 2)

    def gather_two(a, a_f, b, b_x):
        def stacks(a, a_f, b, b_x):
            return jnp.stack([a, *a_f]), jnp.stack([b, b_x])

        a, b = line.plain(stacks, a, a_f, b, b_x)
        return a, over_tp(a, 2), b, [over_fsdp(b, h) for h in range(1, fs)]

    def gather_three(a, a_x, b, b_f):
        whole_a, whole_b = [], []
        for _ in range(2):
            whole_a.append([[(p, h) for h in range(fs)] for p in (a, a_x)])
            whole_b.append([[(p, x) for p in (b, *b_f)] for x in range(2)])
            a, a_x, b, *b_f = [over_tp(p, 1) for p in (a, a_x, b, *b_f)]
        return whole_a, whole_b

    def chip(blocks):
        return [over_tp(b, 1) for b in blocks]

    def reduce_mid_a(a, move):
        return line.plain(lambda a, m: [add(a[h], m[h]) for h in range(fs)], a, move)

    def reduce_mid_b(b, moves):
        return line.plain(lambda b, m: [add(b[x], *[p[x] for p in m]) for x in range(2)], b, moves)

    def reduce_end(a, a_move, b, b_move):
        def both(a, a_move, b, b_move):
            a = add(a, *a_move).reshape(cs, rows, -1)
            b = add(b, b_move).reshape(cs, rows, -1)
            return [jnp.stack([a[d], b[d]]) for d in range(cs)]

        pieces = line.plain(both, a, a_move, b, b_move)
        return pieces[0], [over_ctx(pieces[d], -d) for d in range(1, cs)]

    def finish(own, moved):
        return sum(p.astype(F32) for p in (own, *moved))

    spread = lambda blocks: [blocks[0][0], blocks[1][0], blocks[0][1], blocks[1][1]]
    owner = jnp.stack(
        [(f_rank - h) % fs * cs + (c_rank - d) % cs for h in range(fs) for d in range(cs)]
    )
    features = lax.broadcasted_iota(jnp.int32, (width, width), 0)
    places = (owner[:, None] * rows + jnp.arange(rows)[None, :]).reshape(1, width)
    permute = (features == places).astype(BF16)

    def relative(array, axis=0):
        return [
            jnp.stack([pick(array, t_rank ^ (2 * x + k), axis) for x in range(2)]) for k in range(2)
        ]

    def absolute(blocks):
        blocks = jnp.stack(spread(blocks))
        return jnp.stack([pick(blocks, t_rank ^ t) for t in range(ts)])

    flat = lambda w: w.reshape(w.shape[0], -1)
    side = merger_weight.shape[1] * merger_weight.shape[2]
    heads_width = output_weight.shape[1]

    def start_att(a, m, o):
        return jnp.stack([flat(a), jnp.concatenate([flat(m), o], axis=1)])

    def split_rows(one, two):
        array = jnp.concatenate([one, two], axis=-1)
        array = array.reshape(slots, ts, share, fine, -1).transpose(0, 2, 1, 3, 4)
        return array.reshape(group * ts * fine, -1)

    small = merger_bias.shape[0]
    att = gather_ctx(line.plain(start_att, attend_weight, merger_weight, output_weight))
    packed = line.plain(
        lambda *v: jnp.broadcast_to(jnp.concatenate(v), (devices, sum(x.shape[0] for x in v))),
        merger_bias, first_gain, first_shift, output_bias, second_gain, second_shift, shrink_bias, widen_bias,
    )
    packed = lax.all_to_all(packed, ALL, 0, 0, tiled=True)
    both = line.plain(split_rows, tokens, skip_tokens)
    ffn = line.plain(lambda a, b: jnp.stack([a, b]), expand_weight, shrink_weight)
    packed = line.gate(packed)
    att = gather_one(att)
    both, ffn = line.gate(both, ffn)
    both = to_group(both)
    ffn = gather_ctx(ffn)
    attend, merger_output = gather_three(*gather_two(*att))

    def vectors_of(packed):
        vectors = packed[:, : 7 * small].reshape(fs * cs, ts, 7, small).transpose(0, 2, 1, 3)
        vectors = vectors.reshape(fs * cs, 7, rows)
        vectors = jnp.stack([pick(vectors, owner[i]) for i in range(fs * cs)], axis=1).reshape(7, width)
        return vectors, relative(packed[:, 7 * small :].reshape(ts, 1, hidden))

    def blocks_of(both):
        both = relative(both.reshape(cs, ts, ts * fine, side), 1)
        return [b.reshape(2, count, side) for b in both]

    vectors, widen = line.plain(vectors_of, packed)
    both = line.plain(blocks_of, both)
    act = (count, width)
    turned = (width, count)

    joined, normed, normed_t = line(
        lambda after, b, w, v: down(
            after, "joined", b, w, side, 0, functools.partial(norm_finish, False), [v[0:3]],
            [(act, F32), (act, BF16), (turned, BF16)],
        ),
        both, merger_output, vectors,
    )
    ffn = gather_one(ffn)
    project = line(
        lambda after, n, w: up(
            after, "project", n, w, 3 * heads_width, 0, plain_step, [], [(count, BF16)] * 2, heads_width
        ),
        normed, attend,
    )
    cot = to_group(line.gate(cotangent).reshape(group * fine, width))
    others = [[over_tp(project[k ^ (d & 1)], d) for d in range(1, share)] for k in range(2)]
    inner = [None, None]
    inner[0] = line(attend_forward, project[0], others[0])
    ffn = gather_two(*ffn)
    inner[1] = line(attend_forward, project[1], others[1])
    probs, attended = zip(*inner)
    second, normed_two, normed_two_t = line(
        lambda after, a, w, r, v: down(
            after, "second", a, w, heads_width, side // heads_width, functools.partial(norm_finish, True), [r, v[3:6]],
            [(act, F32), (act, BF16), (turned, BF16)],
        ),
        attended, merger_output, joined, vectors,
    )
    live = pick(live_slots.reshape(slots), (c_rank * ts + t_rank) // share).astype(F32)

    def arrived(cot, permute):
        ours = (mxu(cot.reshape(count, width), permute, 1, 0) * live).astype(BF16)
        return ours, ours.T

    branch_low, branch_low_t = line.plain(arrived, cot, permute)
    expand, shrink = gather_three(*line.gate(*ffn))

    def hidden_step(after, left, w, b):
        return up(after, "hidden", left, [w], hidden, 0, gelu_step, [b], [(count, BF16)] * 2, 256)

    activated, slope = [None, None], [None, None]
    activated[0], slope[0] = line(hidden_step, normed_two, expand[0], widen[0])
    activated[1], slope[1] = line(hidden_step, normed_two, expand[1], widen[1])

    def grads(by_x):
        return lambda after, lefts, rights, more=(): weight_grad(after, lefts, rights, fs, by_x, more)

    def hidden_back(after, left, w, s):
        return up(
            after, "hidden_back", left, [w], hidden, 0, slope_step, [s], [(count, BF16), (1, F32)], 256
        )

    grad_expanded, wide = [None, None], [None, None]
    other = chip(line(grads(True), [branch_low_t], [activated[1]]))
    grad_expanded[1], wide[1] = line(hidden_back, branch_low, shrink[1], slope[1])
    grad_shrink = line(grads(True), [branch_low_t], [activated[0]], other)
    shrink_move = over_tp(grad_shrink[1], 2)
    grad_expanded[0], wide[0] = line(hidden_back, branch_low, shrink[0], slope[0])
    other = chip(line(grads(False), [normed_two_t], [grad_expanded[1]]))
    grad_second, attn_low, attn_low_t, sums_two = line(
        lambda after, g, w, t, u, v: down(
            after, "second_back", g, w, hidden, 0, functools.partial(norm_back_finish, True), [t, u, v[4:5]],
            [(act, F32), (act, BF16), (turned, BF16), ((4, width), F32)],
        ),
        grad_expanded, expand, second, branch_low, vectors,
    )
    grad_expand = line(grads(False), [normed_two_t], [grad_expanded[0]], other)
    expand_move = [over_fsdp(grad_expand[h], -h) for h in range(1, fs)]
    grad_attended = line(
        lambda after, a, w: up(
            after, "attended_back", a, w, heads_width, side // heads_width, plain_step, [], [(count, BF16)] * 2,
            heads_width // 2,
        ),
        attn_low, merger_output,
    )

    def layer_end(after, a, w, t, v):
        ends = jnp.stack([v[6], jnp.full((width,), live)])
        return down(after, "layer_out", a, w, hidden, 0, out_finish, [t, ends], [(act, BF16)])

    (layer_out,) = line(layer_end, activated, shrink, second, vectors)
    layer_out = line.plain(lambda a, p: mxu(a, p, 1, 1).astype(BF16), layer_out, permute)
    layer_out = to_group(layer_out.reshape(group * fine, width))
    inner = [None, None]
    inner[1] = line(attend_backward, project[1], others[1], probs[1], attended[1], grad_attended[1])
    grad_shrink = reduce_mid_a(grad_shrink[0], shrink_move)
    shrink_move = [over_fsdp(grad_shrink[h], -h) for h in range(1, fs)]
    inner[0] = line(attend_backward, project[0], others[0], probs[0], attended[0], grad_attended[0])
    grad_expand = reduce_mid_b(grad_expand[0], expand_move)
    expand_move = over_tp(grad_expand[1], 2)

    def close(k):
        def total(own, *moves):
            third = own.shape[2] // 3
            return jnp.concatenate([own[:, :, :third], add(own[:, :, third:], *moves)], axis=-1)

        moves = [over_tp(inner[k ^ (d & 1)][d], d) for d in range(1, share)]
        return line.plain(total, inner[k][0], *moves)

    grad_project = [None, None]
    grad_project[1] = close(1)
    other = chip(line(grads(True), [normed_t], [grad_project[1]]))
    grad_project[0] = close(0)
    joined_low, joined_low_t, sums_one = line(
        lambda after, g, w, t, u, v: down(
            after, "first_back", g, w, 3 * heads_width, 0, functools.partial(norm_back_finish, False), [t, u, v[1:2]],
            [(act, BF16), (turned, BF16), ((4, width), F32)],
        ),
        grad_project, attend, joined, grad_second, vectors,
    )
    def vector_sums(one, two, wide):
        sums = jnp.concatenate([one[0:3], two]).reshape(7, fs * cs, rows)
        places = [(f_rank - f) % fs * cs + (c_rank - c) % cs for f in range(fs) for c in range(cs)]
        sums = jnp.stack([pick(sums, p, 1) for p in places])
        sums = sums.reshape(fs * cs, 7, ts, small).transpose(0, 2, 1, 3).reshape(devices, 7 * small)
        return jnp.concatenate([sums, absolute(wide).reshape(devices, -1)], axis=1)

    vec = lax.all_to_all(line.plain(vector_sums, sums_one, sums_two, wide), ALL, 0, 0, tiled=True)
    rest_other = chip(line(grads(False), [joined_low_t, attn_low_t], [both[1], attended[1]]))
    grad_attend = line(grads(True), [normed_t], [grad_project[0]], other)
    attend_move = over_tp(grad_attend[1], 2)
    grad_rest = line(grads(False), [joined_low_t, attn_low_t], [both[0], attended[0]], rest_other)
    rest_move = [over_fsdp(grad_rest[h], -h) for h in range(1, fs)]
    out = line(
        lambda after, a, w: up(after, "inputs_back", a, w, side, 0, plain_step, [], [(count, BF16)] * 2, 256),
        joined_low, merger_output,
    )

    def turn_back(out):
        out = absolute(out).reshape(ts, cs, ts * fine, side)
        return out.transpose(1, 0, 2, 3).reshape(group * ts * fine, side)

    out = to_group(line.plain(turn_back, out))
    ffn = reduce_end(grad_shrink[0], shrink_move, grad_expand[0], expand_move)
    grad_attend = reduce_mid_a(grad_attend[0], attend_move)
    attend_move = [over_fsdp(grad_attend[h], -h) for h in range(1, fs)]
    grad_rest = reduce_mid_b(grad_rest[0], rest_move)
    rest_move = over_tp(grad_rest[1], 2)
    att = reduce_end(grad_attend[0], attend_move, grad_rest[0], rest_move)
    ffn = line.plain(finish, *ffn)

    def unpack(out, layer_out, vec):
        out = out.reshape(slots, share, ts, fine, side).transpose(0, 2, 1, 3, 4)
        out = out.reshape(batches, local_seqs, local_len, side).astype(F32)
        layer_out = layer_out.reshape(batches, local_seqs, share * fine, width)
        return out[..., :part_width], out[..., part_width:], layer_out, jnp.sum(vec, axis=0)

    grad_tokens, grad_skip, layer_out, vec = line.plain(unpack, out, layer_out, vec)
    att = line.plain(finish, *att)
    vec_out = [vec[i * small : (i + 1) * small] for i in range(7)] + [vec[7 * small :]]
    return (
        layer_out,
        grad_tokens,
        grad_skip,
        att[1, :, :side].reshape(merger_weight.shape),
        vec_out[0],
        vec_out[1],
        vec_out[2],
        att[0].reshape(attend_weight.shape),
        att[1, :, side:],
        vec_out[3],
        vec_out[4],
        vec_out[5],
        ffn[1],
        vec_out[7],
        ffn[0],
        vec_out[6],
    )


def solution(mesh):
    sizes = tuple(mesh.shape[a] for a in ALL)
    act = P(None, "fsdp", "ctx", "tp")
    vec = P(ALL)
    flat = P(None, "fsdp", ("ctx", "tp"), None)
    w_three = P(("fsdp", "ctx"), None, "tp")
    w_two = P(("fsdp", "ctx"), "tp")
    return jax.shard_map(
        functools.partial(on_device, sizes),
        mesh=mesh,
        in_specs=(
            act, act, w_three, vec, vec, vec, w_three, w_two, vec, vec, vec, w_two, vec, w_two, vec,
            P(None, "fsdp"), flat,
        ),
        out_specs=(
            flat, act, act, w_three, vec, vec, vec, w_three, w_two, vec, vec, vec, w_two, vec, w_two, vec,
        ),
        check_vma=False,
    )
```

```python
import functools

import jax
import jax.numpy as jnp
from jax import lax
from jax.experimental import pallas as pl
from jax.experimental.pallas import tpu as pltpu
from jax.sharding import PartitionSpec as P

HD = 64
EPSILON = 1e-05
F32 = jnp.float32
BF16 = jnp.bfloat16
ALL = ("fsdp", "ctx", "tp")
PARAMS = pltpu.CompilerParams(vmem_limit_bytes=56 * 1024 * 1024)
CHUNK = 128


def mxu(a, b, a_dim, b_dim):
    return lax.dot_general(a, b, (((a_dim,), (b_dim,)), ((), ())), preferred_element_type=F32)


def whole(shape):
    return pl.BlockSpec(shape, lambda *_: (0,) * len(shape))


def call(body, roles, after, *, in_specs, out_specs, out_shape, grid, name, scratch_shapes=()):
    n_in, n_after, n_out = len(in_specs), len(after), len(out_specs)

    def run(roles_ref, *refs):
        outs = refs[n_in + n_after :]
        outs[n_out][...] = jnp.zeros((8, 128), F32)
        body(roles_ref, *refs[:n_in], *outs[:n_out], *outs[n_out + 1 :])

    def apply(*args):
        outs = pl.pallas_call(
            run,
            grid_spec=pltpu.PrefetchScalarGridSpec(
                num_scalar_prefetch=1,
                grid=grid,
                in_specs=[*in_specs, *[pl.BlockSpec(memory_space=pl.ANY)] * n_after],
                out_specs=[*out_specs, whole((8, 128))],
                scratch_shapes=scratch_shapes,
            ),
            out_shape=[*out_shape, jax.ShapeDtypeStruct((8, 128), F32)],
            compiler_params=PARAMS,
            cost_estimate=pl.CostEstimate(flops=1, bytes_accessed=1, transcendentals=0),
            name=name,
        )(roles, *args, *after)
        return outs[:-1], outs[-1]

    return apply


def attend_forward_body(share, heads, roles, *refs):
    own, others = refs[0], refs[1:share]
    p_ref, o_ref = refs[share:]
    part = heads * HD
    rows = lax.broadcasted_iota(jnp.int32, (part, own.shape[1]), 0) // HD
    lanes = lax.broadcasted_iota(jnp.int32, (own.shape[1], part), 1) // HD
    q = own[0, :, :part] * jnp.asarray(HD**-0.5, BF16)
    k = jnp.concatenate([r[0, :, part : 2 * part] for r in (own, *others)], axis=0)
    v = jnp.concatenate([r[0, :, 2 * part :] for r in (own, *others)], axis=0)
    total = jnp.zeros((part, q.shape[0]), F32)
    for h in range(heads):
        s = mxu(k, jnp.where(lanes == h, q, jnp.zeros_like(q)), 1, 1)
        p = jnp.exp(s - jnp.max(s, axis=0, keepdims=True))
        low = (p * (1.0 / jnp.sum(p, axis=0, keepdims=True))).astype(BF16)
        p_ref[0, h] = low
        total = total + jnp.where(rows == h, mxu(v, low, 0, 0), 0.0)
    o_ref[0] = total.T.astype(BF16)


def other_specs(share, shape):
    return [pl.BlockSpec(shape, lambda x, _, d=d: (x ^ (d >> 1), 0, 0)) for d in range(1, share)]


def attend_forward(roles, after, own, others):
    blocks, count, cols = own.shape
    share = 1 + len(others)
    part = cols // 3
    heads = part // HD
    return call(
        functools.partial(attend_forward_body, share, heads),
        roles,
        after,
        grid=(blocks,),
        in_specs=[pl.BlockSpec((1, count, cols), lambda x, _: (x, 0, 0))] + other_specs(share, (1, count, cols)),
        out_specs=[
            pl.BlockSpec((1, heads, share * count, count), lambda x, _: (x, 0, 0, 0)),
            pl.BlockSpec((1, count, part), lambda x, _: (x, 0, 0)),
        ],
        out_shape=[
            jax.ShapeDtypeStruct((blocks, heads, share * count, count), BF16),
            jax.ShapeDtypeStruct((blocks, count, part), BF16),
        ],
        name="attend_forward",
    )(own, *others)


def attend_backward_body(share, heads, roles, *refs):
    own, others = refs[0], refs[1:share]
    p_ref, o_ref, g_ref = refs[share : share + 3]
    outs = refs[share + 3 :]
    part = heads * HD
    count = own.shape[1]
    q = own[0, :, :part] * jnp.asarray(HD**-0.5, BF16)
    k = jnp.concatenate([r[0, :, part : 2 * part] for r in (own, *others)], axis=0)
    v = jnp.concatenate([r[0, :, 2 * part :] for r in (own, *others)], axis=0)
    g = g_ref[0]
    rows = lax.broadcasted_iota(jnp.int32, (part, count), 0) // HD
    lanes = lax.broadcasted_iota(jnp.int32, (count, part), 1) // HD
    prod = (g.astype(F32) * o_ref[0].astype(F32)).T
    dq = jnp.zeros((part, count), F32)
    dk = jnp.zeros((share * count, part), F32)
    dv = jnp.zeros((share * count, part), F32)
    for h in range(heads):
        q_h = jnp.where(lanes == h, q, jnp.zeros_like(q))
        g_h = jnp.where(lanes == h, g, jnp.zeros_like(g))
        p = p_ref[0, h]
        delta = jnp.sum(prod[h * HD : (h + 1) * HD], axis=0, keepdims=True)
        ds = (p.astype(F32) * (mxu(v, g_h, 1, 1) - delta)).astype(BF16)
        dq = dq + jnp.where(rows == h, mxu(k, ds, 0, 0), 0.0)
        dk = dk + mxu(ds, q_h, 1, 0)
        dv = dv + mxu(p, g_h, 1, 0)
    outs[0][0, :, :part] = (dq.T * (HD**-0.5)).astype(BF16)
    outs[0][0, :, part : 2 * part] = dk[:count].astype(BF16)
    outs[0][0, :, 2 * part :] = dv[:count].astype(BF16)
    for d in range(1, share):
        outs[d][0, :, :part] = dk[d * count : (d + 1) * count].astype(BF16)
        outs[d][0, :, part:] = dv[d * count : (d + 1) * count].astype(BF16)


def attend_backward(roles, after, own, others, probs, attended, grad):
    blocks, count, cols = own.shape
    share = 1 + len(others)
    part = cols // 3
    heads = part // HD
    spec = pl.BlockSpec((1, count, cols), lambda x, _: (x, 0, 0))
    o_spec = pl.BlockSpec((1, count, part), lambda x, _: (x, 0, 0))
    p_spec = pl.BlockSpec((1, heads, share * count, count), lambda x, _: (x, 0, 0, 0))
    return call(
        functools.partial(attend_backward_body, share, heads),
        roles,
        after,
        grid=(blocks,),
        in_specs=[spec] + other_specs(share, (1, count, cols)) + [p_spec, o_spec, o_spec],
        out_specs=[spec] + other_specs(share, (1, count, 2 * part)),
        out_shape=[jax.ShapeDtypeStruct((blocks, count, cols), BF16)]
        + [jax.ShapeDtypeStruct((blocks, count, 2 * part), BF16)] * (share - 1),
        name="attend_backward",
    )(own, *others, probs, attended, grad)


def up_body(ks, parts, step, roles, *refs):
    left = refs[0]
    rest = refs[1 + 2 * len(ks) :]
    rows = left.shape[1] // parts
    for i, k in enumerate(ks):
        w = refs[1 + 2 * i : 3 + 2 * i]

        def term(x, h, at):
            return mxu(left[:, pl.ds(at * rows, rows)], w[x][h], 1, 0)

        if parts == 2:
            role = roles[k]
            one, two = term(0, 1, 1 - role), term(1, 0, role)
            step(i, 0, term(0, 0, 0) + jnp.where(role == 0, one, two), rest)
            step(i, 1, term(1, 1, 1) + jnp.where(role == 0, two, one), rest)
        else:
            for x in range(2):
                step(i, x, sum(term(x, h, h) for h in range(parts)), rest)


def up(roles, after, name, left, weights, ks, width, col, step, extras, outs, tile):
    parts, rows, _ = weights[0][0].shape
    per = width // tile
    count = left.shape[0]
    return call(
        functools.partial(up_body, ks, parts, step),
        roles,
        after,
        grid=(per,),
        in_specs=[whole((count, parts * rows))]
        + [pl.BlockSpec((parts, rows, tile), lambda n, _: (0, 0, col * per + n))] * (2 * len(ks))
        + [pl.BlockSpec((2, e.shape[1], tile), lambda n, _: (0, 0, n)) for e in extras],
        out_specs=[pl.BlockSpec((2, o[0], tile), lambda n, _: (0, 0, n)) for o in outs],
        out_shape=[jax.ShapeDtypeStruct((2, o[0], width), o[1]) for o in outs],
        name=name,
    )(left, *[a for w in weights for a in w], *extras)


def plain_step(i, x, total, refs):
    refs[i][x] = total.astype(BF16)


def gelu_step(i, x, total, refs):
    bias, act, slope = refs
    v = total + bias[x]
    half = 0.5 * (1.0 + lax.erf(v * (0.5**0.5)))
    act[x] = (v * half).astype(BF16)
    slope[x] = (half + v * jnp.exp(-0.5 * v * v) * 0.3989422804014327).astype(BF16)


def slope_step(i, x, total, refs):
    slope, grad, sums = refs
    low = (total * slope[x].astype(F32)).astype(BF16)
    grad[x] = low
    sums[x] = jnp.sum(low.astype(F32), axis=0, keepdims=True)


def down_body(parts, finish, roles, *refs):
    rest = refs[6:-1]
    acc = refs[-1]
    n = pl.program_id(0)
    per = pl.num_programs(0)
    total = [0] * parts
    for k in range(2):
        left, w = refs[k], refs[2 + 2 * k : 4 + 2 * k]

        def term(x, h, at):
            return mxu(left[at], w[x][h], 1, 1)

        if parts == 2:
            role = roles[k]
            one, two = term(0, 1, role), term(1, 0, 1 - role)
            total[0] = total[0] + term(0, 0, 0) + jnp.where(role == 0, two, one)
            total[1] = total[1] + term(1, 1, 1) + jnp.where(role == 0, one, two)
        else:
            for h in range(parts):
                total[h] = total[h] + term(0, h, 0) + term(1, h, 1)
    for h in range(parts):
        acc[h * per + n] = total[h]

    @pl.when(n == per - 1)
    def _():
        finish(acc, rest)


def down(roles, after, name, lefts, weights, width, col, finish, extras, outs):
    parts, rows, _ = weights[0][0].shape
    tile = min(256, rows)
    count = lefts[0].shape[1]
    return call(
        functools.partial(down_body, parts, finish),
        roles,
        after,
        grid=(rows // tile,),
        in_specs=[whole((2, count, width))] * 2
        + [pl.BlockSpec((parts, tile, width), lambda n, _: (0, n, col))] * 4
        + [whole(e.shape) for e in extras],
        out_specs=[whole(o[0]) for o in outs],
        out_shape=[jax.ShapeDtypeStruct(*o) for o in outs],
        scratch_shapes=[pltpu.VMEM((parts * rows // tile, count, tile), F32)],
        name=name,
    )(*lefts, *weights[0], *weights[1], *extras)


def row_mean(tiles):
    total = sum(jnp.sum(t, axis=-1, keepdims=True) for t in tiles)
    return total / sum(t.shape[-1] for t in tiles)


def norm_finish(has_residual, acc, refs):
    refs = list(refs)
    residual = refs.pop(0) if has_residual else None
    rows, total_ref, low_ref, low_t_ref = refs
    tiles, count, width = acc.shape
    for r in range(0, count, CHUNK):
        rr = pl.ds(r, CHUNK)
        total = []
        for i in range(tiles):
            cc = slice(i * width, (i + 1) * width)
            v = acc[i, rr, :] + rows[0:1, cc]
            if residual is not None:
                v = v + residual[rr, cc]
            total_ref[rr, cc] = v
            total.append(v)
        mean = row_mean(total)
        center = [t - mean for t in total]
        scale = lax.rsqrt(row_mean([c * c for c in center]) + EPSILON)
        for i in range(tiles):
            cc = slice(i * width, (i + 1) * width)
            v = center[i] * scale * rows[1:2, cc] + rows[2:3, cc]
            low_ref[rr, cc] = v.astype(BF16)
            low_t_ref[cc, rr] = v.T.astype(BF16)


def norm_back_finish(keep, acc, refs):
    total_ref, up_ref, rows, *outs = refs
    full_ref = outs.pop(0) if keep else None
    low_ref, low_t_ref, sums_ref = outs
    tiles, count, width = acc.shape
    zero = jnp.zeros((1, width), F32)
    sums = [[zero] * tiles for _ in range(4)]
    for r in range(0, count, CHUNK):
        rr = pl.ds(r, CHUNK)
        cuts = [slice(i * width, (i + 1) * width) for i in range(tiles)]
        total = [total_ref[rr, cc] for cc in cuts]
        mean = row_mean(total)
        center = [t - mean for t in total]
        scale = lax.rsqrt(row_mean([c * c for c in center]) + EPSILON)
        unit = [c * scale for c in center]
        grad = [acc[i, rr, :] for i in range(tiles)]
        z = [g * rows[0:1, cc] for g, cc in zip(grad, cuts)]
        z_mean = row_mean(z)
        zu_mean = row_mean([a * b for a, b in zip(z, unit)])
        for i, cc in enumerate(cuts):
            up_now = up_ref[rr, cc].astype(F32)
            v = up_now + scale * (z[i] - z_mean - unit[i] * zu_mean)
            if keep:
                full_ref[rr, cc] = v
            low_ref[rr, cc] = v.astype(BF16)
            low_t_ref[cc, rr] = v.T.astype(BF16)
            for j, s in enumerate((v, grad[i] * unit[i], grad[i], up_now)):
                sums[j][i] = sums[j][i] + jnp.sum(s, axis=0, keepdims=True)
    for j in range(4):
        for i in range(tiles):
            sums_ref[j : j + 1, i * width : (i + 1) * width] = sums[j][i]


def out_finish(acc, refs):
    total_ref, rows, low_ref = refs
    tiles, count, width = acc.shape
    for i in range(tiles):
        cc = slice(i * width, (i + 1) * width)
        v = (acc[i] + total_ref[:, cc] + rows[0:1, cc]) * rows[1:2, cc]
        low_ref[:, cc] = v.astype(BF16)


def weight_grad_body(n_parts, n_more, own, roles, *refs):
    ends = refs[4 * n_parts + n_more :]
    for a in range(2):
        at = 0
        more = [m[a].astype(F32) for m in refs[4 * n_parts : 4 * n_parts + n_more]]
        for p in range(n_parts):
            left, right = refs[4 * p + 2 * a : 4 * p + 2 * a + 2]
            total = mxu(left[...], right[...], 1, 0)
            cc = slice(at, at + total.shape[1])
            at = cc.stop
            if own:
                start = 0
                for m in more:
                    if start <= cc.start and cc.stop <= start + m.shape[1]:
                        total = total + m[:, cc.start - start : cc.stop - start]
                    start += m.shape[1]
                ends[a][:, cc] = total.astype(BF16)
            else:
                ends[0][a, :, cc] = total.astype(BF16)


def weight_grad(roles, after, lefts, rights, parts, k, more=()):
    depth, count = lefts[0].shape
    rows = depth // parts
    tile = min(256, rows)
    per = rows // tile
    cols = sum(r.shape[2] for r in rights)
    own = k == 0
    specs, args = [], []
    for left, right in zip(lefts, rights):
        for a in range(2):
            specs += [
                pl.BlockSpec((tile, count), lambda b, n, p, a=a: ((b + p[k] * (a - b)) * per + n, 0)),
                pl.BlockSpec((None, count, right.shape[2]), lambda b, n, p, a=a: (a + p[k] * (b - a), 0, 0)),
            ]
            args += [left, right]
    pair = lambda width: pl.BlockSpec((2, None, tile, width), lambda b, n, _: (0, b, n, 0))
    if own:
        out_specs = [pl.BlockSpec((None, tile, cols), lambda b, n, _: (b, n, 0))] * 2
        out_shape = [jax.ShapeDtypeStruct((parts, rows, cols), BF16)] * 2
    else:
        out_specs = [pair(cols)]
        out_shape = [jax.ShapeDtypeStruct((2, parts, rows, cols), BF16)]
    return call(
        functools.partial(weight_grad_body, len(lefts), len(more), own),
        roles,
        after,
        grid=(parts, per),
        in_specs=specs + [pair(m.shape[3]) for m in more],
        out_specs=out_specs,
        out_shape=out_shape,
        name="weight_grad",
    )(*args, *more)


def pick(array, index, axis=0):
    return lax.dynamic_index_in_dim(array, index, axis, keepdims=False)


def add(*terms):
    return sum(t.astype(F32) for t in terms).astype(BF16)


class Line:
    def __init__(self, roles):
        self.roles, self.marks = roles, []

    def gate(self, *arrays):
        leaves, form = jax.tree.flatten(arrays)
        places = [i for i, leaf in enumerate(leaves) if isinstance(leaf, jax.Array)]
        held, self.marks = lax.optimization_barrier(([leaves[i] for i in places], self.marks))
        for i, array in zip(places, held):
            leaves[i] = array
        arrays = jax.tree.unflatten(form, leaves)
        return arrays[0] if len(arrays) == 1 else arrays

    def plain(self, step, *args):
        out = step(*self.gate(args, ())[0])
        self.marks = self.marks + jax.tree.leaves(out)
        return out

    def __call__(self, step, *args):
        args = self.gate(args, ())[0]
        out, mark = step(self.roles, self.marks, *args)
        self.marks = [mark]
        return out


def on_device(
    sizes,
    tokens,
    skip_tokens,
    merger_weight,
    merger_bias,
    first_gain,
    first_shift,
    attend_weight,
    output_weight,
    output_bias,
    second_gain,
    second_shift,
    expand_weight,
    widen_bias,
    shrink_weight,
    shrink_bias,
    live_slots,
    cotangent,
):
    fs, cs, ts = sizes
    assert ts == 4
    f_rank, c_rank, t_rank = (lax.axis_index(a) for a in ALL)
    group = cs * ts
    devices = fs * group
    batches, local_seqs, local_len, part_width = tokens.shape
    slots = batches * local_seqs
    share = group // slots
    assert share in (1, 2, 4)
    fine = cotangent.shape[2] // share
    width = cotangent.shape[3]
    count = group * fine
    hidden = expand_weight.shape[1]
    rows = width // (fs * cs)
    role = t_rank % 2 if fs == 2 else 0 * t_rank
    line = Line(jnp.stack([role, (1 - role) if fs == 2 else role]).astype(jnp.int32))

    def to_group(array):
        return lax.all_to_all(array, ("ctx", "tp"), 0, 0, tiled=True)

    def over_tp(array, flip):
        return lax.ppermute(array, "tp", [(i, i ^ flip) for i in range(ts)])

    ring = list(range(0, cs, 2)) + list(range(cs - 1 - cs % 2, 0, -2))

    def over_ctx(array, d):
        return lax.ppermute(array, "ctx", [(ring[i], ring[(i + d) % cs]) for i in range(cs)])

    def ctx_behind(d):
        return jnp.asarray([ring[(ring.index(i) - d) % cs] for i in range(cs)], jnp.int32)[c_rank]

    def over_fsdp(array, d):
        return lax.ppermute(array, "fsdp", [(i, (i + d) % fs) for i in range(fs)])

    def first_pairs(i):
        f, c, t = i // (cs * ts), i // ts % cs, i % ts
        f, t = (f, t ^ 2) if t % 2 else (1 - f, t)
        return (f * cs + c) * ts + t

    def second_pairs(i):
        f, c, t = i // (cs * ts), i // ts % cs, i % ts
        f, t = (1 - f, t) if t % 2 else (f, t ^ 2)
        return (f * cs + c) * ts + t

    def over(array, target):
        return lax.ppermute(array, ALL, [(i, target(i)) for i in range(devices)])

    def gather_ctx(piece):
        return [piece] + [over_ctx(piece, d) for d in range(1, cs)]

    def ring_start(piece):
        return [piece, over_ctx(piece, 1)]

    def ring_step(moved):
        *kept, last = moved
        last = line.gate(last)
        return [*kept, last, over_ctx(last, 1)] if len(moved) < cs else [*kept, last]

    def gather_one(moved):
        own = line.plain(lambda *m: jnp.concatenate(m, axis=0), *moved)
        return own, [over(own, first_pairs)] if fs == 2 else [over_fsdp(own, h) for h in range(1, fs)]

    def gather_two(own, moved):
        first = line.plain(lambda a, m: jnp.stack([a, *m]), own, moved)
        return first, over(first, second_pairs) if fs == 2 else over_tp(first, 2), over_tp(first, 1)

    def gather_three(first, second, other):
        first, second, other = line.gate(first, second, other)
        return [[first, second], [other, over_tp(second, 1)]]

    def reduce_one(sums):
        keep, send = sums
        return keep, over(send, second_pairs) if fs == 2 else over_tp(send, 2)

    def reduce_two(keep, moved):
        sums = line.plain(lambda a, m: [add(a[h], m[h]) for h in range(fs)], keep, moved)
        if fs == 2:
            return sums[0], [over(sums[1], first_pairs)]
        return sums[0], [over_fsdp(sums[h], -h) for h in range(1, fs)]

    def reduce_three(own, moved):
        def pieces(own, moved):
            total = add(own, *moved).reshape(cs, rows, -1)
            return [total[d] for d in range(cs)]

        parts = line.plain(pieces, own, moved)
        return parts, over_ctx(parts[-1], -1)

    def reduce_step(parts, moving):
        *parts, last = line.plain(lambda p, m: [*p[:-2], add(p[-2], m)], parts, moving)
        return [*parts, last], over_ctx(last, -1)

    def reduce_last(parts, moving):
        while len(parts) > 2:
            parts, moving = reduce_step(parts, moving)
        return line.plain(lambda p, m: p.astype(F32) + m.astype(F32), parts[0], moving)

    spread = lambda blocks: [blocks[0][0], blocks[1][0], blocks[0][1], blocks[1][1]]
    owner = jnp.stack(
        [(f_rank - h) % fs * cs + ctx_behind(d) for h in range(fs) for d in range(cs)]
    )
    features = lax.broadcasted_iota(jnp.int32, (width, width), 0)
    places = (owner[:, None] * rows + jnp.arange(rows)[None, :]).reshape(1, width)
    permute = (features == places).astype(BF16)

    def relative(array, axis=0):
        return [
            jnp.stack([pick(array, t_rank ^ (2 * x + k), axis) for x in range(2)]) for k in range(2)
        ]

    def absolute(blocks):
        blocks = jnp.stack(spread(blocks))
        return jnp.stack([pick(blocks, t_rank ^ t) for t in range(ts)])

    flat = lambda w: w.reshape(w.shape[0], -1)
    side = merger_weight.shape[1] * merger_weight.shape[2]
    heads_width = output_weight.shape[1]

    def pack_att(m, o, a):
        return jnp.concatenate([flat(m), o, flat(a)], axis=1)

    def split_rows(one, two):
        array = jnp.concatenate([one, two], axis=-1)
        array = array.reshape(slots, ts, share, fine, -1).transpose(0, 2, 1, 3, 4)
        return array.reshape(group * ts * fine, -1)

    small = merger_bias.shape[0]
    att = gather_ctx(line.plain(pack_att, merger_weight, output_weight, attend_weight))
    packed = line.plain(
        lambda *v: jnp.broadcast_to(jnp.concatenate(v), (devices, sum(x.shape[0] for x in v))),
        merger_bias, first_gain, first_shift, output_bias, second_gain, second_shift, shrink_bias, widen_bias,
    )
    packed = lax.all_to_all(packed, ALL, 0, 0, tiled=True)
    both = line.plain(split_rows, tokens, skip_tokens)
    ffn = line.plain(lambda a, b: jnp.concatenate([a, b], axis=1), expand_weight, shrink_weight)
    packed = line.gate(packed)
    att = gather_one(att)
    ffn = ring_start(line.gate(ffn))
    ffn = ring_step(ffn)
    att = gather_two(*att)
    for _ in range(3, cs):
        ffn = ring_step(ffn)
    both = to_group(line.gate(both))
    ffn = gather_one(ring_step(ffn))

    def vectors_of(packed):
        vectors = packed[:, : 7 * small].reshape(fs * cs, ts, 7, small).transpose(0, 2, 1, 3)
        vectors = vectors.reshape(fs * cs, 7, rows)
        vectors = jnp.stack([pick(vectors, owner[i]) for i in range(fs * cs)], axis=1).reshape(7, width)
        return vectors, relative(packed[:, 7 * small :].reshape(ts, 1, hidden))

    def blocks_of(both):
        both = relative(both.reshape(cs, ts, ts * fine, side), 1)
        return [b.reshape(2, count, side) for b in both]

    vectors, widen = line.plain(vectors_of, packed)
    att = gather_three(*att)
    both = line.plain(blocks_of, both)
    act = (count, width)
    turned = (width, count)
    flows = [(count, BF16)] * 2

    joined, normed, normed_t = line(
        lambda *o: down(
            *o[:2], "joined", o[2], o[3], side, 0, functools.partial(norm_finish, False), [o[4][0:3]],
            [(act, F32), (act, BF16), (turned, BF16)],
        ),
        both, att, vectors,
    )
    ffn = gather_two(*ffn)
    project = line(
        lambda *o: up(*o[:2], "project", *o[2:], (0, 1), 3 * heads_width, 1, plain_step, [], flows, heads_width),
        normed, att,
    )
    cot = to_group(line.gate(cotangent).reshape(group * fine, width))
    others = [[over_tp(project[k ^ (d & 1)], d) for d in range(1, share)] for k in range(2)]
    inner = [line(attend_forward, project[k], others[k]) for k in range(2)]
    probs, attended = zip(*inner)
    second, normed_two, normed_two_t = line(
        lambda *o: down(
            *o[:2], "second", o[2], o[3], heads_width, side // heads_width, functools.partial(norm_finish, True),
            [o[4], o[5][3:6]], [(act, F32), (act, BF16), (turned, BF16)],
        ),
        attended, att, joined, vectors,
    )
    live = pick(live_slots.reshape(slots), (c_rank * ts + t_rank) // share).astype(F32)

    def arrived(cot, permute):
        ours = (mxu(cot.reshape(count, width), permute, 1, 0) * live).astype(BF16)
        return ours, ours.T

    branch_low, branch_low_t = line.plain(arrived, cot, permute)
    ffn = gather_three(*ffn)

    def hidden_step(k):
        return lambda *o: up(*o[:2], "hidden", *o[2:4], (k,), hidden, 0, gelu_step, [o[4]], flows, 256)

    activated, slope = [None, None], [None, None]
    for k in range(2):
        activated[k], slope[k] = line(hidden_step(k), normed_two, ffn[k : k + 1], widen[k])

    def grads(k):
        return lambda roles, after, lefts, rights, more=(): weight_grad(roles, after, lefts, rights, fs, k, more)

    def other_grads(lefts, rights):
        return over_tp(line(grads(1), lefts, rights)[0], 1)

    def hidden_back(k):
        return lambda *o: up(
            *o[:2], "hidden_back", *o[2:4], (k,), hidden, 1, slope_step, [o[4]], [(count, BF16), (1, F32)], 256
        )

    grad_expanded, wide = [None, None], [None, None]
    other = other_grads([branch_low_t], [activated[1]])
    grad_expanded[1], wide[1] = line(hidden_back(1), branch_low, ffn[1:], slope[1])
    shrink_sums = reduce_one(line(grads(0), [branch_low_t], [activated[0]], [other]))
    grad_expanded[0], wide[0] = line(hidden_back(0), branch_low, ffn[:1], slope[0])
    grad_second, attn_low, attn_low_t, sums_two = line(
        lambda *o: down(
            *o[:2], "second_back", o[2], o[3], hidden, 0, functools.partial(norm_back_finish, True),
            [o[4], o[5], o[6][4:5]], [(act, F32), (act, BF16), (turned, BF16), ((4, width), F32)],
        ),
        grad_expanded, ffn, second, branch_low, vectors,
    )
    shrink_sums = reduce_two(*shrink_sums)
    other = other_grads([normed_two_t], [grad_expanded[1]])
    grad_attended = line(
        lambda *o: up(
            *o[:2], "attended_back", *o[2:], (0, 1), heads_width, side // heads_width, plain_step, [], flows,
            heads_width // 2,
        ),
        attn_low, att,
    )
    shrink_sums = reduce_three(*shrink_sums)
    expand_sums = reduce_one(line(grads(0), [normed_two_t], [grad_expanded[0]], [other]))
    inner = [None, None]
    inner[1] = line(attend_backward, project[1], others[1], probs[1], attended[1], grad_attended[1])
    shrink_sums = reduce_step(*shrink_sums)
    inner[0] = line(attend_backward, project[0], others[0], probs[0], attended[0], grad_attended[0])
    shrink_sums = reduce_step(*shrink_sums)
    expand_sums = reduce_two(*expand_sums)

    def close(k):
        def total(own, *moves):
            third = own.shape[2] // 3
            return jnp.concatenate([own[:, :, :third], add(own[:, :, third:], *moves)], axis=-1)

        moves = [over_tp(inner[k ^ (d & 1)][d], d) for d in range(1, share)]
        return line.plain(total, inner[k][0], *moves)

    grad_project = [None, None]
    grad_project[1] = close(1)
    attend_other = other_grads([attn_low_t, normed_t], [attended[1], grad_project[1]])
    grad_project[0] = close(0)
    grad_shrink = reduce_last(*shrink_sums)
    expand_sums = reduce_three(*expand_sums)
    joined_low, joined_low_t, sums_one = line(
        lambda *o: down(
            *o[:2], "first_back", o[2], o[3], 3 * heads_width, 1, functools.partial(norm_back_finish, False),
            [o[4], o[5], o[6][1:2]], [(act, BF16), (turned, BF16), ((4, width), F32)],
        ),
        grad_project, att, joined, grad_second, vectors,
    )
    expand_sums = reduce_step(*expand_sums)
    merger_other = other_grads([joined_low_t], [both[1]])
    out = line(
        lambda *o: up(*o[:2], "inputs_back", *o[2:], (0, 1), side, 0, plain_step, [], flows, 256),
        joined_low, att,
    )
    expand_sums = reduce_step(*expand_sums)
    att_sums = reduce_one(
        line(
            grads(0), [joined_low_t, attn_low_t, normed_t], [both[0], attended[0], grad_project[0]],
            [merger_other, attend_other],
        )
    )

    def turn_back(out):
        out = absolute(out).reshape(ts, cs, ts * fine, side)
        return out.transpose(1, 0, 2, 3).reshape(group * ts * fine, side)

    out = to_group(line.plain(turn_back, out))
    grad_expand = reduce_last(*expand_sums)

    def vector_sums(one, two, wide):
        sums = jnp.concatenate([one[0:3], two]).reshape(7, fs * cs, rows)
        place = jnp.asarray([ring.index(i) for i in range(cs)], jnp.int32)[c_rank]
        places = [(f_rank - f) % fs * cs + (place - ring.index(c)) % cs for f in range(fs) for c in range(cs)]
        sums = jnp.stack([pick(sums, p, 1) for p in places])
        sums = sums.reshape(fs * cs, 7, ts, small).transpose(0, 2, 1, 3).reshape(devices, 7 * small)
        return jnp.concatenate([sums, absolute(wide).reshape(devices, -1)], axis=1)

    vec = line.plain(vector_sums, sums_one, sums_two, wide).reshape(fs, cs, 2, 2, -1)
    moved = over_tp(pick(vec, 1 - t_rank % 2, 3), 1)
    def layer_end(roles, after, a, w, t, v):
        ends = jnp.stack([v[6], jnp.full((width,), live)])
        return down(roles, after, "layer_out", a, w, hidden, 1, out_finish, [t, ends], [(act, BF16)])

    (layer_out,) = line(layer_end, activated, ffn, second, vectors)
    layer_out = line.plain(lambda a, p: mxu(a, p, 1, 1).astype(BF16), layer_out, permute)
    vec = line.plain(lambda v, m: pick(v, t_rank % 2, 3) + m, vec, moved)
    moved = over_tp(pick(vec, 1 - t_rank // 2, 2), 2)
    att_sums = reduce_two(*att_sums)
    vec = line.plain(lambda v, m: pick(v, t_rank // 2, 2) + m, vec, moved)
    moved = [over_fsdp(pick(vec, (f_rank - h) % fs), -h) for h in range(1, fs)]
    att_sums = reduce_three(*att_sums)
    vec = line.plain(lambda v, m: sum(m, pick(v, f_rank)), vec, moved)
    moved = [over_ctx(pick(vec, ctx_behind(d)), -d) for d in range(1, cs)]
    att_sums = reduce_step(*att_sums)
    vec = line.plain(lambda v, m: sum(m, pick(v, c_rank)), vec, moved)
    out = line.gate(out)
    layer_out = to_group(line.gate(layer_out).reshape(group * fine, width))
    grad_att = reduce_last(*att_sums)

    def unpack(out, layer_out):
        out = out.reshape(slots, share, ts, fine, side).transpose(0, 2, 1, 3, 4)
        out = out.reshape(batches, local_seqs, local_len, side).astype(F32)
        layer_out = layer_out.reshape(batches, local_seqs, share * fine, width)
        return out[..., :part_width], out[..., part_width:], layer_out

    grad_tokens, grad_skip, layer_out = line.plain(unpack, out, layer_out)
    cut = side + heads_width
    vec_out = [vec[i * small : (i + 1) * small] for i in range(7)] + [vec[7 * small :]]
    return (
        layer_out,
        grad_tokens,
        grad_skip,
        grad_att[:, :side].reshape(merger_weight.shape),
        vec_out[0],
        vec_out[1],
        vec_out[2],
        grad_att[:, cut:].reshape(attend_weight.shape),
        grad_att[:, side:cut],
        vec_out[3],
        vec_out[4],
        vec_out[5],
        grad_expand,
        vec_out[7],
        grad_shrink,
        vec_out[6],
    )


def solution(mesh):
    sizes = tuple(mesh.shape[a] for a in ALL)
    act = P(None, "fsdp", "ctx", "tp")
    vec = P(ALL)
    flat = P(None, "fsdp", ("ctx", "tp"), None)
    w_three = P(("fsdp", "ctx"), None, "tp")
    w_two = P(("fsdp", "ctx"), "tp")
    return jax.shard_map(
        functools.partial(on_device, sizes),
        mesh=mesh,
        in_specs=(
            act, act, w_three, vec, vec, vec, w_three, w_two, vec, vec, vec, w_two, vec, w_two, vec,
            P(None, "fsdp"), flat,
        ),
        out_specs=(
            flat, act, act, w_three, vec, vec, vec, w_three, w_two, vec, vec, vec, w_two, vec, w_two, vec,
        ),
        check_vma=False,
    )
```

```python
import functools

import jax
import jax.numpy as jnp
from jax import lax
from jax.experimental import pallas as pl
from jax.experimental.pallas import tpu as pltpu
from jax.sharding import PartitionSpec as P

HD = 64
EPSILON = 1e-05
F32 = jnp.float32
BF16 = jnp.bfloat16
ALL = ("fsdp", "ctx", "tp")
PARAMS = pltpu.CompilerParams(vmem_limit_bytes=56 * 1024 * 1024)
CHUNK = 128


def mxu(a, b, a_dim, b_dim):
    return lax.dot_general(a, b, (((a_dim,), (b_dim,)), ((), ())), preferred_element_type=F32)


def whole(shape):
    return pl.BlockSpec(shape, lambda *_: (0,) * len(shape))


def call(body, roles, after, *, in_specs, out_specs, out_shape, grid, name, scratch_shapes=()):
    n_in, n_after, n_out = len(in_specs), len(after), len(out_specs)

    def run(roles_ref, *refs):
        outs = refs[n_in + n_after :]
        outs[n_out][...] = jnp.zeros((8, 128), F32)
        body(roles_ref, *refs[:n_in], *outs[:n_out], *outs[n_out + 1 :])

    def apply(*args):
        outs = pl.pallas_call(
            run,
            grid_spec=pltpu.PrefetchScalarGridSpec(
                num_scalar_prefetch=1,
                grid=grid,
                in_specs=[*in_specs, *[pl.BlockSpec(memory_space=pl.ANY)] * n_after],
                out_specs=[*out_specs, whole((8, 128))],
                scratch_shapes=scratch_shapes,
            ),
            out_shape=[*out_shape, jax.ShapeDtypeStruct((8, 128), F32)],
            compiler_params=PARAMS,
            cost_estimate=pl.CostEstimate(flops=1, bytes_accessed=1, transcendentals=0),
            name=name,
        )(roles, *args, *after)
        return outs[:-1], outs[-1]

    return apply


def attend_forward_body(share, heads, roles, *refs):
    own, others = refs[0], refs[1:share]
    p_ref, o_ref = refs[share:]
    part = heads * HD
    rows = lax.broadcasted_iota(jnp.int32, (part, own.shape[1]), 0) // HD
    lanes = lax.broadcasted_iota(jnp.int32, (own.shape[1], part), 1) // HD
    q = own[0, :, :part] * jnp.asarray(HD**-0.5, BF16)
    k = jnp.concatenate([r[0, :, part : 2 * part] for r in (own, *others)], axis=0)
    v = jnp.concatenate([r[0, :, 2 * part :] for r in (own, *others)], axis=0)
    total = jnp.zeros((part, q.shape[0]), F32)
    for h in range(heads):
        s = mxu(k, jnp.where(lanes == h, q, jnp.zeros_like(q)), 1, 1)
        p = jnp.exp(s - jnp.max(s, axis=0, keepdims=True))
        low = (p * (1.0 / jnp.sum(p, axis=0, keepdims=True))).astype(BF16)
        p_ref[0, h] = low
        total = total + jnp.where(rows == h, mxu(v, low, 0, 0), 0.0)
    o_ref[0] = total.T.astype(BF16)


def other_specs(share, shape):
    return [pl.BlockSpec(shape, lambda x, _, d=d: (x ^ (d >> 1), 0, 0)) for d in range(1, share)]


def attend_forward(roles, after, own, others):
    blocks, count, cols = own.shape
    share = 1 + len(others)
    part = cols // 3
    heads = part // HD
    return call(
        functools.partial(attend_forward_body, share, heads),
        roles,
        after,
        grid=(blocks,),
        in_specs=[pl.BlockSpec((1, count, cols), lambda x, _: (x, 0, 0))] + other_specs(share, (1, count, cols)),
        out_specs=[
            pl.BlockSpec((1, heads, share * count, count), lambda x, _: (x, 0, 0, 0)),
            pl.BlockSpec((1, count, part), lambda x, _: (x, 0, 0)),
        ],
        out_shape=[
            jax.ShapeDtypeStruct((blocks, heads, share * count, count), BF16),
            jax.ShapeDtypeStruct((blocks, count, part), BF16),
        ],
        name="attend_forward",
    )(own, *others)


def attend_backward_body(share, heads, roles, *refs):
    own, others = refs[0], refs[1:share]
    p_ref, o_ref, g_ref = refs[share : share + 3]
    outs = refs[share + 3 :]
    part = heads * HD
    count = own.shape[1]
    q = own[0, :, :part] * jnp.asarray(HD**-0.5, BF16)
    k = jnp.concatenate([r[0, :, part : 2 * part] for r in (own, *others)], axis=0)
    v = jnp.concatenate([r[0, :, 2 * part :] for r in (own, *others)], axis=0)
    g = g_ref[0]
    rows = lax.broadcasted_iota(jnp.int32, (part, count), 0) // HD
    lanes = lax.broadcasted_iota(jnp.int32, (count, part), 1) // HD
    prod = (g.astype(F32) * o_ref[0].astype(F32)).T
    dq = jnp.zeros((part, count), F32)
    dk = jnp.zeros((share * count, part), F32)
    dv = jnp.zeros((share * count, part), F32)
    for h in range(heads):
        q_h = jnp.where(lanes == h, q, jnp.zeros_like(q))
        g_h = jnp.where(lanes == h, g, jnp.zeros_like(g))
        p = p_ref[0, h]
        delta = jnp.sum(prod[h * HD : (h + 1) * HD], axis=0, keepdims=True)
        ds = (p.astype(F32) * (mxu(v, g_h, 1, 1) - delta)).astype(BF16)
        dq = dq + jnp.where(rows == h, mxu(k, ds, 0, 0), 0.0)
        dk = dk + mxu(ds, q_h, 1, 0)
        dv = dv + mxu(p, g_h, 1, 0)
    outs[0][0, :, :part] = (dq.T * (HD**-0.5)).astype(BF16)
    outs[0][0, :, part : 2 * part] = dk[:count].astype(BF16)
    outs[0][0, :, 2 * part :] = dv[:count].astype(BF16)
    for d in range(1, share):
        outs[d][0, :, :part] = dk[d * count : (d + 1) * count].astype(BF16)
        outs[d][0, :, part:] = dv[d * count : (d + 1) * count].astype(BF16)


def attend_backward(roles, after, own, others, probs, attended, grad):
    blocks, count, cols = own.shape
    share = 1 + len(others)
    part = cols // 3
    heads = part // HD
    spec = pl.BlockSpec((1, count, cols), lambda x, _: (x, 0, 0))
    o_spec = pl.BlockSpec((1, count, part), lambda x, _: (x, 0, 0))
    p_spec = pl.BlockSpec((1, heads, share * count, count), lambda x, _: (x, 0, 0, 0))
    return call(
        functools.partial(attend_backward_body, share, heads),
        roles,
        after,
        grid=(blocks,),
        in_specs=[spec] + other_specs(share, (1, count, cols)) + [p_spec, o_spec, o_spec],
        out_specs=[spec] + other_specs(share, (1, count, 2 * part)),
        out_shape=[jax.ShapeDtypeStruct((blocks, count, cols), BF16)]
        + [jax.ShapeDtypeStruct((blocks, count, 2 * part), BF16)] * (share - 1),
        name="attend_backward",
    )(own, *others, probs, attended, grad)


def up_tiles(left, w, k, parts, roles):
    rows = left.shape[1] // parts

    def term(x, h, at):
        return mxu(left[:, pl.ds(at * rows, rows)], w[x][h], 1, 0)

    if parts != 2:
        return [sum(term(x, h, h) for h in range(parts)) for x in range(2)]
    role = roles[k]
    one, two = term(0, 1, 1 - role), term(1, 0, role)
    return [
        term(0, 0, 0) + jnp.where(role == 0, one, two),
        term(1, 1, 1) + jnp.where(role == 0, two, one),
    ]


def up_body(ks, parts, step, roles, *refs):
    left = refs[0]
    for i, k in enumerate(ks):
        for x, tile in enumerate(up_tiles(left, refs[1 + 2 * i : 3 + 2 * i], k, parts, roles)):
            step(i, x, tile, refs[1 + 2 * len(ks) :])


def up(roles, after, name, left, weights, ks, width, col, step, outs, tile):
    parts, rows, _ = weights[0][0].shape
    per = width // tile
    count = left.shape[0]
    return call(
        functools.partial(up_body, ks, parts, step),
        roles,
        after,
        grid=(per,),
        in_specs=[whole((count, parts * rows))]
        + [pl.BlockSpec((parts, rows, tile), lambda n, _: (0, 0, col * per + n))] * (2 * len(ks)),
        out_specs=[pl.BlockSpec((2, o[0], tile), lambda n, _: (0, 0, n)) for o in outs],
        out_shape=[jax.ShapeDtypeStruct((2, o[0], width), o[1]) for o in outs],
        name=name,
    )(left, *[a for w in weights for a in w])


def up_grad_body(k, parts, step, n_extra, n_out, n_more, roles, left, left_t, *refs):
    w, extras, more = refs[:2], refs[2 : 2 + n_extra], refs[2 + n_extra : 2 + n_extra + n_more]
    outs = refs[2 + n_extra + n_more : 2 + n_extra + n_more + n_out]
    ends, kept = refs[2 + n_extra + n_more + n_out : -1], refs[-1]
    for x, tile in enumerate(up_tiles(left, w, k, parts, roles)):
        kept[x] = step(x, tile, extras, outs)
    rows = left_t.shape[0] // parts
    role = roles[k]
    for a in range(2):
        for b in range(parts):
            total = mxu(left_t[pl.ds((b + role * (a - b)) * rows, rows), :], kept[a + role * (b - a)], 1, 0)
            if n_more:
                ends[a][b] = (total + more[0][a, b].astype(F32)).astype(BF16)
            else:
                ends[0][a, b] = total.astype(BF16)


def up_grad(roles, after, name, left, left_t, weights, k, col, step, extras, outs, more=()):
    parts, rows, _ = weights[0].shape
    tile = 256
    width = extras[0].shape[2]
    per = width // tile
    count = left.shape[0]
    thin = lambda r: pl.BlockSpec((2, r, tile), lambda n, _: (0, 0, n))
    pair = pl.BlockSpec((2, parts, rows, tile), lambda n, _: (0, 0, 0, n))
    single = pl.BlockSpec((parts, rows, tile), lambda n, _: (0, 0, n))
    ends = [(single, (parts, rows, width))] * 2 if more else [(pair, (2, parts, rows, width))]
    return call(
        functools.partial(up_grad_body, k, parts, step, len(extras), len(outs), len(more)),
        roles,
        after,
        grid=(per,),
        in_specs=[whole(left.shape), whole(left_t.shape)]
        + [pl.BlockSpec((parts, rows, tile), lambda n, _: (0, 0, col * per + n))] * 2
        + [thin(e.shape[1]) for e in extras]
        + [pair] * len(more),
        out_specs=[thin(o[0]) for o in outs] + [e[0] for e in ends],
        out_shape=[jax.ShapeDtypeStruct((2, o[0], width), o[1]) for o in outs]
        + [jax.ShapeDtypeStruct(e[1], BF16) for e in ends],
        scratch_shapes=[pltpu.VMEM((2, count, tile), BF16)],
        name=name,
    )(left, left_t, *weights, *extras, *more)


def plain_step(i, x, total, refs):
    refs[i][x] = total.astype(BF16)


def gelu_step(x, total, extras, outs):
    act, slope = outs
    v = total + extras[0][x]
    half = 0.5 * (1.0 + lax.erf(v * (0.5**0.5)))
    low = (v * half).astype(BF16)
    act[x] = low
    slope[x] = (half + v * jnp.exp(-0.5 * v * v) * 0.3989422804014327).astype(BF16)
    return low


def slope_step(x, total, extras, outs):
    grad, sums = outs
    low = (total * extras[0][x].astype(F32)).astype(BF16)
    grad[x] = low
    sums[x] = jnp.sum(low.astype(F32), axis=0, keepdims=True)
    return low


def down_body(parts, per, finish, n_extra, n_out, n_in, body, roles, *refs):
    extras = refs[6 : 6 + n_extra]
    outs = refs[6 + n_extra + n_in : 6 + n_extra + n_in + n_out]
    acc = refs[-1]
    n = pl.program_id(0)

    @pl.when(n < per)
    def _():
        total = [0] * parts
        for k in range(2):
            left, w = refs[k], refs[2 + 2 * k : 4 + 2 * k]

            def term(x, h, at):
                return mxu(left[at], w[x][h], 1, 1)

            if parts == 2:
                role = roles[k]
                one, two = term(0, 1, role), term(1, 0, 1 - role)
                total[0] = total[0] + term(0, 0, 0) + jnp.where(role == 0, two, one)
                total[1] = total[1] + term(1, 1, 1) + jnp.where(role == 0, one, two)
            else:
                for h in range(parts):
                    total[h] = total[h] + term(0, h, 0) + term(1, h, 1)
        for h in range(parts):
            acc[h * per + n] = total[h]

    @pl.when(n == per - 1)
    def _():
        finish(acc, [*extras, *outs])

    if body is not None:

        @pl.when(n >= per)
        def _():
            body(roles, outs, refs[6 + n_extra : 6 + n_extra + n_in], refs[6 + n_extra + n_in + n_out : -1])


def down(roles, after, name, lefts, weights, width, col, finish, extras, outs, then=(0, None, [], [])):
    parts, rows, _ = weights[0][0].shape
    tile = min(256, rows)
    per = rows // tile
    count = lefts[0].shape[1]
    steps, body, ins, more = then

    def late(block, index):
        return pl.BlockSpec(block, lambda n, _: index(jnp.maximum(n - per, 0)))

    return call(
        functools.partial(down_body, parts, per, finish, len(extras), len(outs), len(ins), body),
        roles,
        after,
        grid=(per + steps,),
        in_specs=[whole((2, count, width))] * 2
        + [pl.BlockSpec((parts, tile, width), lambda n, _: (0, jnp.minimum(n, per - 1), col))] * 4
        + [whole(e.shape) for e in extras]
        + [late(*i[1:]) for i in ins],
        out_specs=[whole(o[0]) for o in outs] + [late(*m[2:]) for m in more],
        out_shape=[jax.ShapeDtypeStruct(*o) for o in outs] + [jax.ShapeDtypeStruct(*m[:2]) for m in more],
        scratch_shapes=[pltpu.VMEM((parts * rows // tile, count, tile), F32)],
        name=name,
    )(*lefts, *weights[0], *weights[1], *extras, *[i[0] for i in ins])


def then_up(place, weights, width, col, tile):
    parts, rows, _ = weights[0][0].shape
    per = width // tile

    def body(roles, outs, ins, ends):
        for k in range(2):
            for x, total in enumerate(up_tiles(outs[place], ins[2 * k : 2 * k + 2], k, parts, roles)):
                ends[k][x] = total.astype(BF16)

    def of(count):
        return (
            per,
            body,
            [(a, (parts, rows, tile), lambda m: (0, 0, col * per + m)) for w in weights for a in w],
            [((2, count, width), BF16, (2, count, tile), lambda m: (0, 0, m))] * 2,
        )

    return of


def then_grad(place, right, parts):
    _, count, cols = right.shape

    def body(roles, outs, ins, ends):
        b = pl.program_id(0) - pl.num_programs(0) + parts
        rows = outs[place].shape[0] // parts
        role = roles[1]
        for a in range(2):
            left = outs[place][pl.ds((b + role * (a - b)) * rows, rows), :]
            ends[0][a] = mxu(left, ins[0][a + role * (b - a)], 1, 0).astype(BF16)

    def of(depth):
        rows = depth // parts
        return (
            parts,
            body,
            [(right, right.shape, lambda m: (0, 0, 0))],
            [((2, parts, rows, cols), BF16, (2, None, rows, cols), lambda m: (0, m, 0, 0))],
        )

    return of


def row_mean(tiles):
    total = sum(jnp.sum(t, axis=-1, keepdims=True) for t in tiles)
    return total / sum(t.shape[-1] for t in tiles)


def norm_finish(has_residual, acc, refs):
    refs = list(refs)
    residual = refs.pop(0) if has_residual else None
    rows, total_ref, low_ref, low_t_ref = refs
    tiles, count, width = acc.shape
    for r in range(0, count, CHUNK):
        rr = pl.ds(r, CHUNK)
        total = []
        for i in range(tiles):
            cc = slice(i * width, (i + 1) * width)
            v = acc[i, rr, :] + rows[0:1, cc]
            if residual is not None:
                v = v + residual[rr, cc]
            total_ref[rr, cc] = v
            total.append(v)
        mean = row_mean(total)
        center = [t - mean for t in total]
        scale = lax.rsqrt(row_mean([c * c for c in center]) + EPSILON)
        for i in range(tiles):
            cc = slice(i * width, (i + 1) * width)
            v = center[i] * scale * rows[1:2, cc] + rows[2:3, cc]
            low_ref[rr, cc] = v.astype(BF16)
            low_t_ref[cc, rr] = v.T.astype(BF16)


def norm_back_finish(keep, acc, refs):
    total_ref, up_ref, rows, *outs = refs
    full_ref = outs.pop(0) if keep else None
    low_ref, low_t_ref, sums_ref = outs
    tiles, count, width = acc.shape
    zero = jnp.zeros((1, width), F32)
    sums = [[zero] * tiles for _ in range(4)]
    for r in range(0, count, CHUNK):
        rr = pl.ds(r, CHUNK)
        cuts = [slice(i * width, (i + 1) * width) for i in range(tiles)]
        total = [total_ref[rr, cc] for cc in cuts]
        mean = row_mean(total)
        center = [t - mean for t in total]
        scale = lax.rsqrt(row_mean([c * c for c in center]) + EPSILON)
        unit = [c * scale for c in center]
        grad = [acc[i, rr, :] for i in range(tiles)]
        z = [g * rows[0:1, cc] for g, cc in zip(grad, cuts)]
        z_mean = row_mean(z)
        zu_mean = row_mean([a * b for a, b in zip(z, unit)])
        for i, cc in enumerate(cuts):
            up_now = up_ref[rr, cc].astype(F32)
            v = up_now + scale * (z[i] - z_mean - unit[i] * zu_mean)
            if keep:
                full_ref[rr, cc] = v
            low_ref[rr, cc] = v.astype(BF16)
            low_t_ref[cc, rr] = v.T.astype(BF16)
            for j, s in enumerate((v, grad[i] * unit[i], grad[i], up_now)):
                sums[j][i] = sums[j][i] + jnp.sum(s, axis=0, keepdims=True)
    for j in range(4):
        for i in range(tiles):
            sums_ref[j : j + 1, i * width : (i + 1) * width] = sums[j][i]


def out_finish(acc, refs):
    total_ref, rows, low_ref = refs
    tiles, count, width = acc.shape
    for i in range(tiles):
        cc = slice(i * width, (i + 1) * width)
        v = (acc[i] + total_ref[:, cc] + rows[0:1, cc]) * rows[1:2, cc]
        low_ref[:, cc] = v.astype(BF16)


def arrived_body(roles, cot, permute, live, low_ref, low_t_ref):
    low = mxu(cot[...], permute[...], 1, 0) * live[...]
    low_ref[...] = low.astype(BF16)
    low_t_ref[...] = low.T.astype(BF16)


def arrived(roles, after, cot, permute, live):
    count, width = cot.shape
    tile = min(256, width)
    return call(
        arrived_body,
        roles,
        after,
        grid=(width // tile,),
        in_specs=[whole(cot.shape), pl.BlockSpec((width, tile), lambda n, _: (0, n)), whole((1, 1))],
        out_specs=[pl.BlockSpec((count, tile), lambda n, _: (0, n)), pl.BlockSpec((tile, count), lambda n, _: (n, 0))],
        out_shape=[jax.ShapeDtypeStruct((count, width), BF16), jax.ShapeDtypeStruct((width, count), BF16)],
        name="arrived",
    )(cot, permute, live.reshape(1, 1))


def weight_grad_body(n_parts, n_more, own, roles, *refs):
    ends = refs[4 * n_parts + n_more :]
    for a in range(2):
        at = 0
        more = [m[a].astype(F32) for m in refs[4 * n_parts : 4 * n_parts + n_more]]
        for p in range(n_parts):
            left, right = refs[4 * p + 2 * a : 4 * p + 2 * a + 2]
            total = mxu(left[...], right[...], 1, 0)
            cc = slice(at, at + total.shape[1])
            at = cc.stop
            if own:
                start = 0
                for m in more:
                    if start <= cc.start and cc.stop <= start + m.shape[1]:
                        total = total + m[:, cc.start - start : cc.stop - start]
                    start += m.shape[1]
                ends[a][:, cc] = total.astype(BF16)
            else:
                ends[0][a, :, cc] = total.astype(BF16)


def weight_grad(roles, after, lefts, rights, parts, k, more=()):
    depth, count = lefts[0].shape
    rows = depth // parts
    tile = min(256, rows)
    per = rows // tile
    cols = sum(r.shape[2] for r in rights)
    own = k == 0
    specs, args = [], []
    for left, right in zip(lefts, rights):
        for a in range(2):
            specs += [
                pl.BlockSpec((tile, count), lambda b, n, p, a=a: ((b + p[k] * (a - b)) * per + n, 0)),
                pl.BlockSpec((None, count, right.shape[2]), lambda b, n, p, a=a: (a + p[k] * (b - a), 0, 0)),
            ]
            args += [left, right]
    pair = lambda width: pl.BlockSpec((2, None, tile, width), lambda b, n, _: (0, b, n, 0))
    if own:
        out_specs = [pl.BlockSpec((None, tile, cols), lambda b, n, _: (b, n, 0))] * 2
        out_shape = [jax.ShapeDtypeStruct((parts, rows, cols), BF16)] * 2
    else:
        out_specs = [pair(cols)]
        out_shape = [jax.ShapeDtypeStruct((2, parts, rows, cols), BF16)]
    return call(
        functools.partial(weight_grad_body, len(lefts), len(more), own),
        roles,
        after,
        grid=(parts, per),
        in_specs=specs + [pair(m.shape[3]) for m in more],
        out_specs=out_specs,
        out_shape=out_shape,
        name="weight_grad",
    )(*args, *more)


def pick(array, index, axis=0):
    return lax.dynamic_index_in_dim(array, index, axis, keepdims=False)


def add(*terms):
    return sum(t.astype(F32) for t in terms).astype(BF16)


class Line:
    def __init__(self, roles):
        self.roles, self.marks = roles, []

    def gate(self, *arrays):
        leaves, form = jax.tree.flatten(arrays)
        places = [i for i, leaf in enumerate(leaves) if isinstance(leaf, jax.Array)]
        held, self.marks = lax.optimization_barrier(([leaves[i] for i in places], self.marks))
        for i, array in zip(places, held):
            leaves[i] = array
        arrays = jax.tree.unflatten(form, leaves)
        return arrays[0] if len(arrays) == 1 else arrays

    def plain(self, step, *args):
        out = step(*self.gate(args, ())[0])
        self.marks = self.marks + jax.tree.leaves(out)
        return out

    def __call__(self, step, *args):
        args = self.gate(args, ())[0]
        out, mark = step(self.roles, self.marks, *args)
        self.marks = [mark]
        return out


def on_device(
    sizes,
    tokens,
    skip_tokens,
    merger_weight,
    merger_bias,
    first_gain,
    first_shift,
    attend_weight,
    output_weight,
    output_bias,
    second_gain,
    second_shift,
    expand_weight,
    widen_bias,
    shrink_weight,
    shrink_bias,
    live_slots,
    cotangent,
):
    fs, cs, ts = sizes
    assert ts == 4
    f_rank, c_rank, t_rank = (lax.axis_index(a) for a in ALL)
    group = cs * ts
    devices = fs * group
    batches, local_seqs, local_len, part_width = tokens.shape
    slots = batches * local_seqs
    share = group // slots
    assert share in (1, 2, 4)
    fine = cotangent.shape[2] // share
    width = cotangent.shape[3]
    count = group * fine
    hidden = expand_weight.shape[1]
    rows = width // (fs * cs)
    role = t_rank % 2 if fs == 2 else 0 * t_rank
    line = Line(jnp.stack([role, (1 - role) if fs == 2 else role]).astype(jnp.int32))

    def to_group(array):
        return lax.all_to_all(array, ("ctx", "tp"), 0, 0, tiled=True)

    def over_tp(array, flip):
        return lax.ppermute(array, "tp", [(i, i ^ flip) for i in range(ts)])

    ring = list(range(0, cs, 2)) + list(range(cs - 1 - cs % 2, 0, -2))

    def over_ctx(array, d):
        return lax.ppermute(array, "ctx", [(ring[i], ring[(i + d) % cs]) for i in range(cs)])

    def ctx_behind(d):
        return jnp.asarray([ring[(ring.index(i) - d) % cs] for i in range(cs)], jnp.int32)[c_rank]

    def over_fsdp(array, d):
        return lax.ppermute(array, "fsdp", [(i, (i + d) % fs) for i in range(fs)])

    def first_pairs(i):
        f, c, t = i // (cs * ts), i // ts % cs, i % ts
        f, t = (f, t ^ 2) if t % 2 else (1 - f, t)
        return (f * cs + c) * ts + t

    def second_pairs(i):
        f, c, t = i // (cs * ts), i // ts % cs, i % ts
        f, t = (1 - f, t) if t % 2 else (f, t ^ 2)
        return (f * cs + c) * ts + t

    def over(array, target):
        return lax.ppermute(array, ALL, [(i, target(i)) for i in range(devices)])

    def gather_ctx(piece):
        return [piece] + [over_ctx(piece, d) for d in range(1, cs)]

    def ring_start(piece):
        return [piece, over_ctx(piece, 1)]

    def ring_step(moved):
        *kept, last = moved
        last = line.gate(last)
        return [*kept, last, over_ctx(last, 1)] if len(moved) < cs else [*kept, last]

    def gather_one(moved):
        own = line.plain(lambda *m: jnp.concatenate(m, axis=0), *moved)
        return own, [over(own, first_pairs)] if fs == 2 else [over_fsdp(own, h) for h in range(1, fs)]

    def gather_two(own, moved):
        first = line.plain(lambda a, m: jnp.stack([a, *m]), own, moved)
        return first, over(first, second_pairs) if fs == 2 else over_tp(first, 2)

    def gather_near(first, second):
        first = line.gate(first)
        return first, second, over_tp(first, 1)

    def gather_three(first, second, other):
        first, second, other = line.gate(first, second, other)
        return [[first, second], [other, over_tp(second, 1)]]

    def reduce_one(sums):
        keep, send = sums
        return keep, over(send, second_pairs) if fs == 2 else over_tp(send, 2)

    def reduce_two(keep, moved):
        sums = line.plain(lambda a, m: [add(a[h], m[h]) for h in range(fs)], keep, moved)
        if fs == 2:
            return sums[0], [over(sums[1], first_pairs)]
        return sums[0], [over_fsdp(sums[h], -h) for h in range(1, fs)]

    def reduce_three(*sums):
        def pieces(*sums):
            total = jnp.concatenate([add(own, *moved) for own, moved in sums], axis=1).reshape(cs, rows, -1)
            return [total[d] for d in range(cs)]

        parts = line.plain(pieces, *sums)
        return parts, over_ctx(parts[-1], -1)

    def reduce_step(parts, moving):
        *parts, last = line.plain(lambda p, m: [*p[:-2], add(p[-2], m)], parts, moving)
        return [*parts, last], over_ctx(last, -1)

    def reduce_last(parts, moving):
        while len(parts) > 2:
            parts, moving = reduce_step(parts, moving)
        return line.plain(lambda p, m: p.astype(F32) + m.astype(F32), parts[0], moving)

    spread = lambda blocks: [blocks[0][0], blocks[1][0], blocks[0][1], blocks[1][1]]
    owner = jnp.stack(
        [(f_rank - h) % fs * cs + ctx_behind(d) for h in range(fs) for d in range(cs)]
    )
    features = lax.broadcasted_iota(jnp.int32, (width, width), 0)
    places = (owner[:, None] * rows + jnp.arange(rows)[None, :]).reshape(1, width)
    permute = (features == places).astype(BF16)

    def relative(array, axis=0):
        return [
            jnp.stack([pick(array, t_rank ^ (2 * x + k), axis) for x in range(2)]) for k in range(2)
        ]

    def absolute(blocks):
        blocks = jnp.stack(spread(blocks))
        return jnp.stack([pick(blocks, t_rank ^ t) for t in range(ts)])

    flat = lambda w: w.reshape(w.shape[0], -1)
    side = merger_weight.shape[1] * merger_weight.shape[2]
    heads_width = output_weight.shape[1]

    def pack_att(m, o, a):
        return jnp.concatenate([flat(m), o, flat(a)], axis=1)

    def split_rows(one, two):
        array = jnp.concatenate([one, two], axis=-1)
        array = array.reshape(slots, ts, share, fine, -1).transpose(0, 2, 1, 3, 4)
        return array.reshape(group * ts * fine, -1)

    small = merger_bias.shape[0]
    att = gather_ctx(line.plain(pack_att, merger_weight, output_weight, attend_weight))
    packed = line.plain(
        lambda *v: jnp.broadcast_to(jnp.concatenate(v), (devices, sum(x.shape[0] for x in v))),
        merger_bias, first_gain, first_shift, output_bias, second_gain, second_shift, shrink_bias, widen_bias,
    )
    packed = lax.all_to_all(packed, ALL, 0, 0, tiled=True)
    both = line.plain(split_rows, tokens, skip_tokens)
    ffn = line.plain(lambda a, b: jnp.concatenate([a, b], axis=1), expand_weight, shrink_weight)
    packed = line.gate(packed)
    cot = to_group(line.gate(cotangent).reshape(group * fine, width))
    att = gather_one(att)
    ffn = ring_start(line.gate(ffn))
    ffn = ring_step(ffn)
    att = gather_near(*gather_two(*att))
    for _ in range(3, cs):
        ffn = ring_step(ffn)
    cot = line.gate(cot)
    both = to_group(line.gate(both))
    ffn = gather_one(ring_step(ffn))

    live = pick(live_slots.reshape(slots), (c_rank * ts + t_rank) // share).astype(F32)
    branch_low, branch_low_t = line(arrived, cot.reshape(count, width), permute, live)

    def vectors_of(packed):
        vectors = packed[:, : 7 * small].reshape(fs * cs, ts, 7, small).transpose(0, 2, 1, 3)
        vectors = vectors.reshape(fs * cs, 7, rows)
        vectors = jnp.stack([pick(vectors, owner[i]) for i in range(fs * cs)], axis=1).reshape(7, width)
        return vectors, relative(packed[:, 7 * small :].reshape(ts, 1, hidden))

    def blocks_of(both):
        both = relative(both.reshape(cs, ts, ts * fine, side), 1)
        return [b.reshape(2, count, side) for b in both]

    vectors, widen = line.plain(vectors_of, packed)
    att = gather_three(*att)
    both = line.plain(blocks_of, both)
    act = (count, width)
    turned = (width, count)
    flows = [(count, BF16)] * 2

    joined, normed, normed_t, *project = line(
        lambda *o: down(
            *o[:2], "joined", o[2], o[3], side, 0, functools.partial(norm_finish, False), [o[4][0:3]],
            [(act, F32), (act, BF16), (turned, BF16)],
            then_up(1, o[3], 3 * heads_width, 1, heads_width)(count),
        ),
        both, att, vectors,
    )
    ffn = gather_two(*ffn)
    others = [[over_tp(project[k ^ (d & 1)], d) for d in range(1, share)] for k in range(2)]
    inner = [line(attend_forward, project[0], others[0])]
    ffn = gather_near(*ffn)
    inner.append(line(attend_forward, project[1], others[1]))
    probs, attended = zip(*inner)

    ffn = gather_three(*ffn)
    second, normed_two, normed_two_t = line(
        lambda *o: down(
            *o[:2], "second", o[2], o[3], heads_width, side // heads_width, functools.partial(norm_finish, True),
            [o[4], o[5][3:6]], [(act, F32), (act, BF16), (turned, BF16)],
        ),
        attended, att, joined, vectors,
    )

    def grads(k):
        return lambda roles, after, lefts, rights, more=(): weight_grad(roles, after, lefts, rights, fs, k, more)

    def other_grads(lefts, rights):
        return over_tp(line(grads(1), lefts, rights)[0], 1)

    def hidden_step(k):
        return lambda *o: up_grad(*o[:2], "hidden", *o[2:5], k, 0, gelu_step, [o[5]], flows, *o[6:])

    def hidden_back(k):
        return lambda *o: up_grad(
            *o[:2], "hidden_back", *o[2:5], k, 1, slope_step, [o[5]], [(count, BF16), (1, F32)], *o[6:]
        )

    activated, slope, grad_expanded, wide = ([None, None] for _ in range(4))
    activated[1], slope[1], other = line(hidden_step(1), normed_two, branch_low_t, ffn[1], widen[1])
    other = over_tp(other, 1)
    grad_expanded[1], wide[1], other_two = line(hidden_back(1), branch_low, normed_two_t, ffn[1], slope[1])
    other_two = over_tp(other_two, 1)
    activated[0], slope[0], *sums = line(hidden_step(0), normed_two, branch_low_t, ffn[0], widen[0], [other])
    shrink_sums = reduce_one(sums)
    grad_expanded[0], wide[0], *sums = line(hidden_back(0), branch_low, normed_two_t, ffn[0], slope[0], [other_two])
    expand_sums = reduce_one(sums)
    grad_second, attn_low, attn_low_t, sums_two, *grad_attended = line(
        lambda *o: down(
            *o[:2], "second_back", o[2], o[3], hidden, 0, functools.partial(norm_back_finish, True),
            [o[4], o[5], o[6][4:5]], [(act, F32), (act, BF16), (turned, BF16), ((4, width), F32)],
            then_up(1, o[7], heads_width, side // heads_width, heads_width // 2)(count),
        ),
        grad_expanded, ffn, second, branch_low, vectors, att,
    )
    shrink_sums = reduce_two(*shrink_sums)
    inner = [None, None]
    inner[1] = line(attend_backward, project[1], others[1], probs[1], attended[1], grad_attended[1])

    def layer_end(roles, after, a, w, t, v):
        ends = jnp.stack([v[6], jnp.full((width,), live)])
        return down(roles, after, "layer_out", a, w, hidden, 1, out_finish, [t, ends], [(act, BF16)])

    (layer_out,) = line(layer_end, activated, ffn, second, vectors)
    layer_out = line.plain(lambda a, p: mxu(a, p, 1, 1).astype(BF16), layer_out, permute)
    layer_out = to_group(layer_out.reshape(group * fine, width))
    expand_sums = reduce_two(*expand_sums)
    inner[0] = line(attend_backward, project[0], others[0], probs[0], attended[0], grad_attended[0])
    ffn_sums = reduce_three(shrink_sums, expand_sums)

    def close(k):
        def total(own, *moves):
            third = own.shape[2] // 3
            return jnp.concatenate([own[:, :, :third], add(own[:, :, third:], *moves)], axis=-1)

        moves = [over_tp(inner[k ^ (d & 1)][d], d) for d in range(1, share)]
        return line.plain(total, inner[k][0], *moves)

    grad_project = [None, None]
    grad_project[1] = close(1)
    attend_other = other_grads([attn_low_t, normed_t], [attended[1], grad_project[1]])
    grad_project[0] = close(0)
    joined_low, joined_low_t, sums_one, merger_other = line(
        lambda *o: down(
            *o[:2], "first_back", o[2], o[3], 3 * heads_width, 1, functools.partial(norm_back_finish, False),
            [o[4], o[5], o[6][1:2]], [(act, BF16), (turned, BF16), ((4, width), F32)],
            then_grad(1, o[7], fs)(width),
        ),
        grad_project, att, joined, grad_second, vectors, both[1],
    )
    merger_other = over_tp(merger_other, 1)
    layer_out = line.gate(layer_out)
    ffn_sums = reduce_step(*ffn_sums)
    out = line(
        lambda *o: up(*o[:2], "inputs_back", *o[2:], (0, 1), side, 0, plain_step, flows, 256),
        joined_low, att,
    )
    def turn_back(out):
        out = absolute(out).reshape(ts, cs, ts * fine, side)
        return out.transpose(1, 0, 2, 3).reshape(group * ts * fine, side)

    out = to_group(line.plain(turn_back, out))
    ffn_sums = reduce_step(*ffn_sums)
    att_sums = reduce_one(
        line(
            grads(0), [joined_low_t, attn_low_t, normed_t], [both[0], attended[0], grad_project[0]],
            [merger_other, attend_other],
        )
    )
    grad_ffn = reduce_last(*ffn_sums)

    def vector_sums(one, two, wide):
        sums = jnp.concatenate([one[0:3], two]).reshape(7, fs * cs, rows)
        place = jnp.asarray([ring.index(i) for i in range(cs)], jnp.int32)[c_rank]
        places = [(f_rank - f) % fs * cs + (place - ring.index(c)) % cs for f in range(fs) for c in range(cs)]
        sums = jnp.stack([pick(sums, p, 1) for p in places])
        sums = sums.reshape(fs * cs, 7, ts, small).transpose(0, 2, 1, 3).reshape(devices, 7 * small)
        return jnp.concatenate([sums, absolute(wide).reshape(devices, -1)], axis=1)

    vec = line.plain(vector_sums, sums_one, sums_two, wide).reshape(fs, cs, 2, 2, -1)
    moved = over_tp(pick(vec, 1 - t_rank % 2, 3), 1)
    vec = line.plain(lambda v, m: pick(v, t_rank % 2, 3) + m, vec, moved)
    moved = over_tp(pick(vec, 1 - t_rank // 2, 2), 2)
    out = line.gate(out)
    att_sums = reduce_two(*att_sums)
    vec = line.plain(lambda v, m: pick(v, t_rank // 2, 2) + m, vec, moved)
    moved = [over_fsdp(pick(vec, (f_rank - h) % fs), -h) for h in range(1, fs)]
    att_sums = reduce_three(att_sums)
    vec = line.plain(lambda v, m: sum(m, pick(v, f_rank)), vec, moved)
    moved = [over_ctx(pick(vec, ctx_behind(d)), -d) for d in range(1, cs)]
    att_sums = reduce_step(*att_sums)
    vec = line.plain(lambda v, m: sum(m, pick(v, c_rank)), vec, moved)
    grad_att = reduce_last(*att_sums)

    def unpack(out, layer_out):
        out = out.reshape(slots, share, ts, fine, side).transpose(0, 2, 1, 3, 4)
        out = out.reshape(batches, local_seqs, local_len, side).astype(F32)
        layer_out = layer_out.reshape(batches, local_seqs, share * fine, width)
        return out[..., :part_width], out[..., part_width:], layer_out

    grad_tokens, grad_skip, layer_out = line.plain(unpack, out, layer_out)
    cut = side + heads_width
    vec_out = [vec[i * small : (i + 1) * small] for i in range(7)] + [vec[7 * small :]]
    return (
        layer_out,
        grad_tokens,
        grad_skip,
        grad_att[:, :side].reshape(merger_weight.shape),
        vec_out[0],
        vec_out[1],
        vec_out[2],
        grad_att[:, cut:].reshape(attend_weight.shape),
        grad_att[:, side:cut],
        vec_out[3],
        vec_out[4],
        vec_out[5],
        grad_ffn[:, hidden:],
        vec_out[7],
        grad_ffn[:, :hidden],
        vec_out[6],
    )


def solution(mesh):
    sizes = tuple(mesh.shape[a] for a in ALL)
    act = P(None, "fsdp", "ctx", "tp")
    vec = P(ALL)
    flat = P(None, "fsdp", ("ctx", "tp"), None)
    w_three = P(("fsdp", "ctx"), None, "tp")
    w_two = P(("fsdp", "ctx"), "tp")
    return jax.shard_map(
        functools.partial(on_device, sizes),
        mesh=mesh,
        in_specs=(
            act, act, w_three, vec, vec, vec, w_three, w_two, vec, vec, vec, w_two, vec, w_two, vec,
            P(None, "fsdp"), flat,
        ),
        out_specs=(
            flat, act, act, w_three, vec, vec, vec, w_three, w_two, vec, vec, vec, w_two, vec, w_two, vec,
        ),
        check_vma=False,
    )
```

```python
import functools

import jax
import jax.numpy as jnp
from jax import lax
from jax.experimental import pallas as pl
from jax.experimental.pallas import tpu as pltpu
from jax.sharding import PartitionSpec as P

HD = 64
EPSILON = 1e-05
F32 = jnp.float32
BF16 = jnp.bfloat16
ALL = ("fsdp", "ctx", "tp")
PARAMS = pltpu.CompilerParams(vmem_limit_bytes=56 * 1024 * 1024)
CHUNK = 128


def mxu(a, b, a_dim, b_dim):
    return lax.dot_general(a, b, (((a_dim,), (b_dim,)), ((), ())), preferred_element_type=F32)


def whole(shape):
    return pl.BlockSpec(shape, lambda *_: (0,) * len(shape))


def call(body, roles, after, *, in_specs, out_specs, out_shape, grid, name, scratch_shapes=()):
    n_in, n_after, n_out = len(in_specs), len(after), len(out_specs)

    def run(roles_ref, *refs):
        outs = refs[n_in + n_after :]
        outs[n_out][...] = jnp.zeros((8, 128), F32)
        body(roles_ref, *refs[:n_in], *outs[:n_out], *outs[n_out + 1 :])

    def apply(*args):
        outs = pl.pallas_call(
            run,
            grid_spec=pltpu.PrefetchScalarGridSpec(
                num_scalar_prefetch=1,
                grid=grid,
                in_specs=[*in_specs, *[pl.BlockSpec(memory_space=pl.ANY)] * n_after],
                out_specs=[*out_specs, whole((8, 128))],
                scratch_shapes=scratch_shapes,
            ),
            out_shape=[*out_shape, jax.ShapeDtypeStruct((8, 128), F32)],
            compiler_params=PARAMS,
            cost_estimate=pl.CostEstimate(flops=1, bytes_accessed=1, transcendentals=0),
            name=name,
        )(roles, *args, *after)
        return outs[:-1], outs[-1]

    return apply


def attend_forward_body(share, heads, roles, *refs):
    own, others = refs[0], refs[1:share]
    p_ref, o_ref = refs[share:]
    part = heads * HD
    rows = lax.broadcasted_iota(jnp.int32, (part, own.shape[1]), 0) // HD
    lanes = lax.broadcasted_iota(jnp.int32, (own.shape[1], part), 1) // HD
    q = own[0, :, :part] * jnp.asarray(HD**-0.5, BF16)
    k = jnp.concatenate([r[0, :, part : 2 * part] for r in (own, *others)], axis=0)
    v = jnp.concatenate([r[0, :, 2 * part :] for r in (own, *others)], axis=0)
    total = jnp.zeros((part, q.shape[0]), F32)
    for h in range(heads):
        s = mxu(k, jnp.where(lanes == h, q, jnp.zeros_like(q)), 1, 1)
        p = jnp.exp(s - jnp.max(s, axis=0, keepdims=True))
        low = (p * (1.0 / jnp.sum(p, axis=0, keepdims=True))).astype(BF16)
        p_ref[0, h] = low
        total = total + jnp.where(rows == h, mxu(v, low, 0, 0), 0.0)
    o_ref[0] = total.T.astype(BF16)


def other_specs(share, shape):
    return [pl.BlockSpec(shape, lambda x, _, d=d: (x ^ (d >> 1), 0, 0)) for d in range(1, share)]


def attend_forward(roles, after, own, others):
    blocks, count, cols = own.shape
    share = 1 + len(others)
    part = cols // 3
    heads = part // HD
    return call(
        functools.partial(attend_forward_body, share, heads),
        roles,
        after,
        grid=(blocks,),
        in_specs=[pl.BlockSpec((1, count, cols), lambda x, _: (x, 0, 0))] + other_specs(share, (1, count, cols)),
        out_specs=[
            pl.BlockSpec((1, heads, share * count, count), lambda x, _: (x, 0, 0, 0)),
            pl.BlockSpec((1, count, part), lambda x, _: (x, 0, 0)),
        ],
        out_shape=[
            jax.ShapeDtypeStruct((blocks, heads, share * count, count), BF16),
            jax.ShapeDtypeStruct((blocks, count, part), BF16),
        ],
        name="attend_forward",
    )(own, *others)


def attend_backward_body(share, heads, roles, *refs):
    own, others = refs[0], refs[1:share]
    p_ref, o_ref, g_ref = refs[share : share + 3]
    outs = refs[share + 3 :]
    part = heads * HD
    count = own.shape[1]
    q = own[0, :, :part] * jnp.asarray(HD**-0.5, BF16)
    k = jnp.concatenate([r[0, :, part : 2 * part] for r in (own, *others)], axis=0)
    v = jnp.concatenate([r[0, :, 2 * part :] for r in (own, *others)], axis=0)
    g = g_ref[0]
    rows = lax.broadcasted_iota(jnp.int32, (part, count), 0) // HD
    lanes = lax.broadcasted_iota(jnp.int32, (count, part), 1) // HD
    prod = (g.astype(F32) * o_ref[0].astype(F32)).T
    dq = jnp.zeros((part, count), F32)
    dk = jnp.zeros((share * count, part), F32)
    dv = jnp.zeros((share * count, part), F32)
    for h in range(heads):
        q_h = jnp.where(lanes == h, q, jnp.zeros_like(q))
        g_h = jnp.where(lanes == h, g, jnp.zeros_like(g))
        p = p_ref[0, h]
        delta = jnp.sum(prod[h * HD : (h + 1) * HD], axis=0, keepdims=True)
        ds = (p.astype(F32) * (mxu(v, g_h, 1, 1) - delta)).astype(BF16)
        dq = dq + jnp.where(rows == h, mxu(k, ds, 0, 0), 0.0)
        dk = dk + mxu(ds, q_h, 1, 0)
        dv = dv + mxu(p, g_h, 1, 0)
    outs[0][0, :, :part] = (dq.T * (HD**-0.5)).astype(BF16)
    outs[0][0, :, part : 2 * part] = dk[:count].astype(BF16)
    outs[0][0, :, 2 * part :] = dv[:count].astype(BF16)
    for d in range(1, share):
        outs[d][0, :, :part] = dk[d * count : (d + 1) * count].astype(BF16)
        outs[d][0, :, part:] = dv[d * count : (d + 1) * count].astype(BF16)


def attend_backward(roles, after, own, others, probs, attended, grad):
    blocks, count, cols = own.shape
    share = 1 + len(others)
    part = cols // 3
    heads = part // HD
    spec = pl.BlockSpec((1, count, cols), lambda x, _: (x, 0, 0))
    o_spec = pl.BlockSpec((1, count, part), lambda x, _: (x, 0, 0))
    p_spec = pl.BlockSpec((1, heads, share * count, count), lambda x, _: (x, 0, 0, 0))
    return call(
        functools.partial(attend_backward_body, share, heads),
        roles,
        after,
        grid=(blocks,),
        in_specs=[spec] + other_specs(share, (1, count, cols)) + [p_spec, o_spec, o_spec],
        out_specs=[spec] + other_specs(share, (1, count, 2 * part)),
        out_shape=[jax.ShapeDtypeStruct((blocks, count, cols), BF16)]
        + [jax.ShapeDtypeStruct((blocks, count, 2 * part), BF16)] * (share - 1),
        name="attend_backward",
    )(own, *others, probs, attended, grad)


def up_tiles(left, w, k, parts, roles):
    rows = left.shape[1] // parts

    def term(x, h, at):
        return mxu(left[:, pl.ds(at * rows, rows)], w[x][h], 1, 0)

    if parts != 2:
        return [sum(term(x, h, h) for h in range(parts)) for x in range(2)]
    role = roles[k]
    one, two = term(0, 1, 1 - role), term(1, 0, role)
    return [
        term(0, 0, 0) + jnp.where(role == 0, one, two),
        term(1, 1, 1) + jnp.where(role == 0, two, one),
    ]


def up_body(ks, parts, step, roles, *refs):
    left = refs[0]
    for i, k in enumerate(ks):
        for x, tile in enumerate(up_tiles(left, refs[1 + 2 * i : 3 + 2 * i], k, parts, roles)):
            step(i, x, tile, refs[1 + 2 * len(ks) :])


def up(roles, after, name, left, weights, ks, width, col, step, outs, tile):
    parts, rows, _ = weights[0][0].shape
    per = width // tile
    count = left.shape[0]
    return call(
        functools.partial(up_body, ks, parts, step),
        roles,
        after,
        grid=(per,),
        in_specs=[whole((count, parts * rows))]
        + [pl.BlockSpec((parts, rows, tile), lambda n, _: (0, 0, col * per + n))] * (2 * len(ks)),
        out_specs=[pl.BlockSpec((2, o[0], tile), lambda n, _: (0, 0, n)) for o in outs],
        out_shape=[jax.ShapeDtypeStruct((2, o[0], width), o[1]) for o in outs],
        name=name,
    )(left, *[a for w in weights for a in w])


def up_grad_body(k, parts, step, n_extra, n_out, n_more, roles, left, left_t, *refs):
    w, extras, more = refs[:2], refs[2 : 2 + n_extra], refs[2 + n_extra : 2 + n_extra + n_more]
    outs = refs[2 + n_extra + n_more : 2 + n_extra + n_more + n_out]
    ends, kept = refs[2 + n_extra + n_more + n_out : -1], refs[-1]
    for x, tile in enumerate(up_tiles(left, w, k, parts, roles)):
        kept[x] = step(x, tile, extras, outs)
    rows = left_t.shape[0] // parts
    role = roles[k]
    for a in range(2):
        for b in range(parts):
            total = mxu(left_t[pl.ds((b + role * (a - b)) * rows, rows), :], kept[a + role * (b - a)], 1, 0)
            if n_more:
                ends[a][b] = (total + more[0][a, b].astype(F32)).astype(BF16)
            else:
                ends[0][a, b] = total.astype(BF16)


def up_grad(roles, after, name, left, left_t, weights, k, col, step, extras, outs, more=()):
    parts, rows, _ = weights[0].shape
    tile = 256
    width = extras[0].shape[2]
    per = width // tile
    count = left.shape[0]
    thin = lambda r: pl.BlockSpec((2, r, tile), lambda n, _: (0, 0, n))
    pair = pl.BlockSpec((2, parts, rows, tile), lambda n, _: (0, 0, 0, n))
    single = pl.BlockSpec((parts, rows, tile), lambda n, _: (0, 0, n))
    ends = [(single, (parts, rows, width))] * 2 if more else [(pair, (2, parts, rows, width))]
    return call(
        functools.partial(up_grad_body, k, parts, step, len(extras), len(outs), len(more)),
        roles,
        after,
        grid=(per,),
        in_specs=[whole(left.shape), whole(left_t.shape)]
        + [pl.BlockSpec((parts, rows, tile), lambda n, _: (0, 0, col * per + n))] * 2
        + [thin(e.shape[1]) for e in extras]
        + [pair] * len(more),
        out_specs=[thin(o[0]) for o in outs] + [e[0] for e in ends],
        out_shape=[jax.ShapeDtypeStruct((2, o[0], width), o[1]) for o in outs]
        + [jax.ShapeDtypeStruct(e[1], BF16) for e in ends],
        scratch_shapes=[pltpu.VMEM((2, count, tile), BF16)],
        name=name,
    )(left, left_t, *weights, *extras, *more)


def plain_step(i, x, total, refs):
    refs[i][x] = total.astype(BF16)


def gelu_step(x, total, extras, outs):
    act, slope = outs
    v = total + extras[0][x]
    half = 0.5 * (1.0 + lax.erf(v * (0.5**0.5)))
    low = (v * half).astype(BF16)
    act[x] = low
    slope[x] = (half + v * jnp.exp(-0.5 * v * v) * 0.3989422804014327).astype(BF16)
    return low


def slope_step(x, total, extras, outs):
    grad, sums = outs
    low = (total * extras[0][x].astype(F32)).astype(BF16)
    grad[x] = low
    sums[x] = jnp.sum(low.astype(F32), axis=0, keepdims=True)
    return low


def down_body(parts, per, finish, n_extra, n_out, n_in, body, roles, *refs):
    extras = refs[6 : 6 + n_extra]
    outs = refs[6 + n_extra + n_in : 6 + n_extra + n_in + n_out]
    acc = refs[-1]
    n = pl.program_id(0)

    @pl.when(n < per)
    def _():
        total = [0] * parts
        for k in range(2):
            left, w = refs[k], refs[2 + 2 * k : 4 + 2 * k]

            def term(x, h, at):
                return mxu(left[at], w[x][h], 1, 1)

            if parts == 2:
                role = roles[k]
                one, two = term(0, 1, role), term(1, 0, 1 - role)
                total[0] = total[0] + term(0, 0, 0) + jnp.where(role == 0, two, one)
                total[1] = total[1] + term(1, 1, 1) + jnp.where(role == 0, one, two)
            else:
                for h in range(parts):
                    total[h] = total[h] + term(0, h, 0) + term(1, h, 1)
        for h in range(parts):
            acc[h * per + n] = total[h]

    @pl.when(n == per - 1)
    def _():
        finish(acc, [*extras, *outs])

    if body is not None:

        @pl.when(n >= per)
        def _():
            body(roles, outs, refs[6 + n_extra : 6 + n_extra + n_in], refs[6 + n_extra + n_in + n_out : -1])


def down(roles, after, name, lefts, weights, width, col, finish, extras, outs, then=(0, None, [], [])):
    parts, rows, _ = weights[0][0].shape
    tile = min(256, rows)
    per = rows // tile
    count = lefts[0].shape[1]
    steps, body, ins, more = then

    def late(block, index):
        return pl.BlockSpec(block, lambda n, _: index(jnp.maximum(n - per, 0)))

    return call(
        functools.partial(down_body, parts, per, finish, len(extras), len(outs), len(ins), body),
        roles,
        after,
        grid=(per + steps,),
        in_specs=[whole((2, count, width))] * 2
        + [pl.BlockSpec((parts, tile, width), lambda n, _: (0, jnp.minimum(n, per - 1), col))] * 4
        + [whole(e.shape) for e in extras]
        + [late(*i[1:]) for i in ins],
        out_specs=[whole(o[0]) for o in outs] + [late(*m[2:]) for m in more],
        out_shape=[jax.ShapeDtypeStruct(*o) for o in outs] + [jax.ShapeDtypeStruct(*m[:2]) for m in more],
        scratch_shapes=[pltpu.VMEM((parts * rows // tile, count, tile), F32)],
        name=name,
    )(*lefts, *weights[0], *weights[1], *extras, *[i[0] for i in ins])


def then_up(place, weights, width, col, tile):
    parts, rows, _ = weights[0][0].shape
    per = width // tile

    def body(roles, outs, ins, ends):
        for k in range(2):
            for x, total in enumerate(up_tiles(outs[place], ins[2 * k : 2 * k + 2], k, parts, roles)):
                ends[k][x] = total.astype(BF16)

    def of(count):
        return (
            per,
            body,
            [(a, (parts, rows, tile), lambda m: (0, 0, col * per + m)) for w in weights for a in w],
            [((2, count, width), BF16, (2, count, tile), lambda m: (0, 0, m))] * 2,
        )

    return of


def then_grad(place, right, parts):
    _, count, cols = right.shape

    def body(roles, outs, ins, ends):
        b = pl.program_id(0) - pl.num_programs(0) + parts
        rows = outs[place].shape[0] // parts
        role = roles[1]
        for a in range(2):
            left = outs[place][pl.ds((b + role * (a - b)) * rows, rows), :]
            ends[0][a] = mxu(left, ins[0][a + role * (b - a)], 1, 0).astype(BF16)

    def of(depth):
        rows = depth // parts
        return (
            parts,
            body,
            [(right, right.shape, lambda m: (0, 0, 0))],
            [((2, parts, rows, cols), BF16, (2, None, rows, cols), lambda m: (0, m, 0, 0))],
        )

    return of


def row_mean(tiles):
    total = sum(jnp.sum(t, axis=-1, keepdims=True) for t in tiles)
    return total / sum(t.shape[-1] for t in tiles)


def norm_finish(has_residual, acc, refs):
    refs = list(refs)
    residual = refs.pop(0) if has_residual else None
    rows, total_ref, low_ref, low_t_ref = refs
    tiles, count, width = acc.shape
    for r in range(0, count, CHUNK):
        rr = pl.ds(r, CHUNK)
        total = []
        for i in range(tiles):
            cc = slice(i * width, (i + 1) * width)
            v = acc[i, rr, :] + rows[0:1, cc]
            if residual is not None:
                v = v + residual[rr, cc]
            total_ref[rr, cc] = v
            total.append(v)
        mean = row_mean(total)
        center = [t - mean for t in total]
        scale = lax.rsqrt(row_mean([c * c for c in center]) + EPSILON)
        for i in range(tiles):
            cc = slice(i * width, (i + 1) * width)
            v = center[i] * scale * rows[1:2, cc] + rows[2:3, cc]
            low_ref[rr, cc] = v.astype(BF16)
            low_t_ref[cc, rr] = v.T.astype(BF16)


def norm_back_finish(keep, acc, refs):
    total_ref, up_ref, rows, *outs = refs
    full_ref = outs.pop(0) if keep else None
    low_ref, low_t_ref, sums_ref = outs
    tiles, count, width = acc.shape
    zero = jnp.zeros((1, width), F32)
    sums = [[zero] * tiles for _ in range(4)]
    for r in range(0, count, CHUNK):
        rr = pl.ds(r, CHUNK)
        cuts = [slice(i * width, (i + 1) * width) for i in range(tiles)]
        total = [total_ref[rr, cc] for cc in cuts]
        mean = row_mean(total)
        center = [t - mean for t in total]
        scale = lax.rsqrt(row_mean([c * c for c in center]) + EPSILON)
        unit = [c * scale for c in center]
        grad = [acc[i, rr, :] for i in range(tiles)]
        z = [g * rows[0:1, cc] for g, cc in zip(grad, cuts)]
        z_mean = row_mean(z)
        zu_mean = row_mean([a * b for a, b in zip(z, unit)])
        for i, cc in enumerate(cuts):
            up_now = up_ref[rr, cc].astype(F32)
            v = up_now + scale * (z[i] - z_mean - unit[i] * zu_mean)
            if keep:
                full_ref[rr, cc] = v
            low_ref[rr, cc] = v.astype(BF16)
            low_t_ref[cc, rr] = v.T.astype(BF16)
            for j, s in enumerate((v, grad[i] * unit[i], grad[i], up_now)):
                sums[j][i] = sums[j][i] + jnp.sum(s, axis=0, keepdims=True)
    for j in range(4):
        for i in range(tiles):
            sums_ref[j : j + 1, i * width : (i + 1) * width] = sums[j][i]


def out_finish(acc, refs):
    total_ref, rows, low_ref = refs
    tiles, count, width = acc.shape
    for i in range(tiles):
        cc = slice(i * width, (i + 1) * width)
        v = (acc[i] + total_ref[:, cc] + rows[0:1, cc]) * rows[1:2, cc]
        low_ref[:, cc] = v.astype(BF16)


def arrived_body(roles, cot, permute, live, low_ref, low_t_ref):
    low = mxu(cot[...], permute[...], 1, 0) * live[...]
    low_ref[...] = low.astype(BF16)
    low_t_ref[...] = low.T.astype(BF16)


def arrived(roles, after, cot, permute, live):
    count, width = cot.shape
    tile = min(256, width)
    return call(
        arrived_body,
        roles,
        after,
        grid=(width // tile,),
        in_specs=[whole(cot.shape), pl.BlockSpec((width, tile), lambda n, _: (0, n)), whole((1, 1))],
        out_specs=[pl.BlockSpec((count, tile), lambda n, _: (0, n)), pl.BlockSpec((tile, count), lambda n, _: (n, 0))],
        out_shape=[jax.ShapeDtypeStruct((count, width), BF16), jax.ShapeDtypeStruct((width, count), BF16)],
        name="arrived",
    )(cot, permute, live.reshape(1, 1))


def weight_grad_body(n_parts, n_more, own, roles, *refs):
    ends = refs[4 * n_parts + n_more :]
    for a in range(2):
        at = 0
        more = [m[a].astype(F32) for m in refs[4 * n_parts : 4 * n_parts + n_more]]
        for p in range(n_parts):
            left, right = refs[4 * p + 2 * a : 4 * p + 2 * a + 2]
            total = mxu(left[...], right[...], 1, 0)
            cc = slice(at, at + total.shape[1])
            at = cc.stop
            if own:
                start = 0
                for m in more:
                    if start <= cc.start and cc.stop <= start + m.shape[1]:
                        total = total + m[:, cc.start - start : cc.stop - start]
                    start += m.shape[1]
                ends[a][:, cc] = total.astype(BF16)
            else:
                ends[0][a, :, cc] = total.astype(BF16)


def weight_grad(roles, after, lefts, rights, parts, k, more=()):
    depth, count = lefts[0].shape
    rows = depth // parts
    tile = min(256, rows)
    per = rows // tile
    cols = sum(r.shape[2] for r in rights)
    own = k == 0
    specs, args = [], []
    for left, right in zip(lefts, rights):
        for a in range(2):
            specs += [
                pl.BlockSpec((tile, count), lambda b, n, p, a=a: ((b + p[k] * (a - b)) * per + n, 0)),
                pl.BlockSpec((None, count, right.shape[2]), lambda b, n, p, a=a: (a + p[k] * (b - a), 0, 0)),
            ]
            args += [left, right]
    pair = lambda width: pl.BlockSpec((2, None, tile, width), lambda b, n, _: (0, b, n, 0))
    if own:
        out_specs = [pl.BlockSpec((None, tile, cols), lambda b, n, _: (b, n, 0))] * 2
        out_shape = [jax.ShapeDtypeStruct((parts, rows, cols), BF16)] * 2
    else:
        out_specs = [pair(cols)]
        out_shape = [jax.ShapeDtypeStruct((2, parts, rows, cols), BF16)]
    return call(
        functools.partial(weight_grad_body, len(lefts), len(more), own),
        roles,
        after,
        grid=(parts, per),
        in_specs=specs + [pair(m.shape[3]) for m in more],
        out_specs=out_specs,
        out_shape=out_shape,
        name="weight_grad",
    )(*args, *more)


def pick(array, index, axis=0):
    return lax.dynamic_index_in_dim(array, index, axis, keepdims=False)


def add(*terms):
    return sum(t.astype(F32) for t in terms).astype(BF16)


class Line:
    def __init__(self, roles):
        self.roles, self.marks = roles, []

    def gate(self, *arrays):
        leaves, form = jax.tree.flatten(arrays)
        places = [i for i, leaf in enumerate(leaves) if isinstance(leaf, jax.Array)]
        held, self.marks = lax.optimization_barrier(([leaves[i] for i in places], self.marks))
        for i, array in zip(places, held):
            leaves[i] = array
        arrays = jax.tree.unflatten(form, leaves)
        return arrays[0] if len(arrays) == 1 else arrays

    def plain(self, step, *args):
        out = step(*self.gate(args, ())[0])
        self.marks = self.marks + jax.tree.leaves(out)
        return out

    def __call__(self, step, *args):
        args = self.gate(args, ())[0]
        out, mark = step(self.roles, self.marks, *args)
        self.marks = [mark]
        return out


def on_device(
    sizes,
    tokens,
    skip_tokens,
    merger_weight,
    merger_bias,
    first_gain,
    first_shift,
    attend_weight,
    output_weight,
    output_bias,
    second_gain,
    second_shift,
    expand_weight,
    widen_bias,
    shrink_weight,
    shrink_bias,
    live_slots,
    cotangent,
):
    fs, cs, ts = sizes
    assert ts == 4
    f_rank, c_rank, t_rank = (lax.axis_index(a) for a in ALL)
    group = cs * ts
    devices = fs * group
    batches, local_seqs, local_len, part_width = tokens.shape
    slots = batches * local_seqs
    share = group // slots
    assert share in (1, 2, 4)
    fine = cotangent.shape[2] // share
    width = cotangent.shape[3]
    count = group * fine
    hidden = expand_weight.shape[1]
    rows = width // (fs * cs)
    role = t_rank % 2 if fs == 2 else 0 * t_rank
    line = Line(jnp.stack([role, (1 - role) if fs == 2 else role]).astype(jnp.int32))

    def to_group(array):
        return lax.all_to_all(array, ("ctx", "tp"), 0, 0, tiled=True)

    def over_tp(array, flip):
        return lax.ppermute(array, "tp", [(i, i ^ flip) for i in range(ts)])

    ring = list(range(0, cs, 2)) + list(range(cs - 1 - cs % 2, 0, -2))

    def over_ctx(array, d):
        return lax.ppermute(array, "ctx", [(ring[i], ring[(i + d) % cs]) for i in range(cs)])

    def ctx_behind(d):
        return jnp.asarray([ring[(ring.index(i) - d) % cs] for i in range(cs)], jnp.int32)[c_rank]

    def over_fsdp(array, d):
        return lax.ppermute(array, "fsdp", [(i, (i + d) % fs) for i in range(fs)])

    def first_pairs(i):
        f, c, t = i // (cs * ts), i // ts % cs, i % ts
        f, t = (f, t ^ 2) if t % 2 else (1 - f, t)
        return (f * cs + c) * ts + t

    def second_pairs(i):
        f, c, t = i // (cs * ts), i // ts % cs, i % ts
        f, t = (1 - f, t) if t % 2 else (f, t ^ 2)
        return (f * cs + c) * ts + t

    def over(array, target):
        return lax.ppermute(array, ALL, [(i, target(i)) for i in range(devices)])

    def gather_ctx(piece):
        return [piece] + [over_ctx(piece, d) for d in range(1, cs)]

    def ring_start(piece):
        return [piece, over_ctx(piece, 1)]

    def ring_step(moved):
        *kept, last = moved
        last = line.gate(last)
        return [*kept, last, over_ctx(last, 1)] if len(moved) < cs else [*kept, last]

    def gather_one(moved):
        own = line.plain(lambda *m: jnp.concatenate(m, axis=0), *moved)
        return own, [over(own, first_pairs)] if fs == 2 else [over_fsdp(own, h) for h in range(1, fs)]

    def gather_two(own, moved):
        first = line.plain(lambda a, m: jnp.stack([a, *m]), own, moved)
        return first, over(first, second_pairs) if fs == 2 else over_tp(first, 2)

    def gather_near(first, second):
        first = line.gate(first)
        return first, second, over_tp(first, 1)

    def gather_three(first, second, other):
        first, second, other = line.gate(first, second, other)
        return [[first, second], [other, over_tp(second, 1)]]

    def reduce_one(sums):
        keep, send = sums
        return keep, over(send, second_pairs) if fs == 2 else over_tp(send, 2)

    def reduce_two(keep, moved):
        sums = line.plain(lambda a, m: [add(a[h], m[h]) for h in range(fs)], keep, moved)
        if fs == 2:
            return sums[0], [over(sums[1], first_pairs)]
        return sums[0], [over_fsdp(sums[h], -h) for h in range(1, fs)]

    def reduce_three(*sums):
        def pieces(*sums):
            total = jnp.concatenate([add(own, *moved) for own, moved in sums], axis=1).reshape(cs, rows, -1)
            return [total[d] for d in range(cs)]

        parts = line.plain(pieces, *sums)
        return parts, over_ctx(parts[-1], -1)

    def reduce_step(parts, moving):
        *parts, last = line.plain(lambda p, m: [*p[:-2], add(p[-2], m)], parts, moving)
        return [*parts, last], over_ctx(last, -1)

    def reduce_last(parts, moving):
        while len(parts) > 2:
            parts, moving = reduce_step(parts, moving)
        return line.plain(lambda p, m: p.astype(F32) + m.astype(F32), parts[0], moving)

    spread = lambda blocks: [blocks[0][0], blocks[1][0], blocks[0][1], blocks[1][1]]
    owner = jnp.stack(
        [(f_rank - h) % fs * cs + ctx_behind(d) for h in range(fs) for d in range(cs)]
    )
    features = lax.broadcasted_iota(jnp.int32, (width, width), 0)
    places = (owner[:, None] * rows + jnp.arange(rows)[None, :]).reshape(1, width)
    permute = (features == places).astype(BF16)

    def relative(array, axis=0):
        return [
            jnp.stack([pick(array, t_rank ^ (2 * x + k), axis) for x in range(2)]) for k in range(2)
        ]

    def absolute(blocks):
        blocks = jnp.stack(spread(blocks))
        return jnp.stack([pick(blocks, t_rank ^ t) for t in range(ts)])

    flat = lambda w: w.reshape(w.shape[0], -1)
    side = merger_weight.shape[1] * merger_weight.shape[2]
    heads_width = output_weight.shape[1]

    def pack_att(m, o, a):
        return jnp.concatenate([flat(m), o, flat(a)], axis=1)

    def split_rows(one, two):
        array = jnp.concatenate([one, two], axis=-1)
        array = array.reshape(slots, ts, share, fine, -1).transpose(0, 2, 1, 3, 4)
        return array.reshape(group * ts * fine, -1)

    small = merger_bias.shape[0]
    att = gather_ctx(line.plain(pack_att, merger_weight, output_weight, attend_weight))
    packed = line.plain(
        lambda *v: jnp.broadcast_to(jnp.concatenate(v), (devices, sum(x.shape[0] for x in v))),
        merger_bias, first_gain, first_shift, output_bias, second_gain, second_shift, shrink_bias, widen_bias,
    )
    packed = lax.all_to_all(packed, ALL, 0, 0, tiled=True)
    both = line.plain(split_rows, tokens, skip_tokens)
    ffn = line.plain(lambda a, b: jnp.concatenate([a, b], axis=1), expand_weight, shrink_weight)
    packed = line.gate(packed)
    cot = to_group(line.gate(cotangent).reshape(group * fine, width))
    att = gather_one(att)
    ffn = ring_start(line.gate(ffn))
    ffn = ring_step(ffn)
    att = gather_near(*gather_two(*att))
    for _ in range(3, cs):
        ffn = ring_step(ffn)
    cot = line.gate(cot)
    both = to_group(line.gate(both))
    ffn = gather_one(ring_step(ffn))

    live = pick(live_slots.reshape(slots), (c_rank * ts + t_rank) // share).astype(F32)
    branch_low, branch_low_t = line(arrived, cot.reshape(count, width), permute, live)

    def vectors_of(packed):
        vectors = packed[:, : 7 * small].reshape(fs * cs, ts, 7, small).transpose(0, 2, 1, 3)
        vectors = vectors.reshape(fs * cs, 7, rows)
        vectors = jnp.stack([pick(vectors, owner[i]) for i in range(fs * cs)], axis=1).reshape(7, width)
        return vectors, relative(packed[:, 7 * small :].reshape(ts, 1, hidden))

    def blocks_of(both):
        both = relative(both.reshape(cs, ts, ts * fine, side), 1)
        return [b.reshape(2, count, side) for b in both]

    vectors, widen = line.plain(vectors_of, packed)
    att = gather_three(*att)
    both = line.plain(blocks_of, both)
    act = (count, width)
    turned = (width, count)
    flows = [(count, BF16)] * 2

    joined, normed, normed_t, *project = line(
        lambda *o: down(
            *o[:2], "joined", o[2], o[3], side, 0, functools.partial(norm_finish, False), [o[4][0:3]],
            [(act, F32), (act, BF16), (turned, BF16)],
            then_up(1, o[3], 3 * heads_width, 1, heads_width)(count),
        ),
        both, att, vectors,
    )
    ffn = gather_two(*ffn)
    others = [[over_tp(project[k ^ (d & 1)], d) for d in range(1, share)] for k in range(2)]
    others = line.gate(others)
    inner = [line(attend_forward, project[0], others[0])]
    ffn = gather_near(*ffn)
    inner.append(line(attend_forward, project[1], others[1]))
    probs, attended = zip(*inner)

    ffn = gather_three(*ffn)
    second, normed_two, normed_two_t = line(
        lambda *o: down(
            *o[:2], "second", o[2], o[3], heads_width, side // heads_width, functools.partial(norm_finish, True),
            [o[4], o[5][3:6]], [(act, F32), (act, BF16), (turned, BF16)],
        ),
        attended, att, joined, vectors,
    )

    def grads(k):
        return lambda roles, after, lefts, rights, more=(): weight_grad(roles, after, lefts, rights, fs, k, more)

    def other_grads(lefts, rights):
        return over_tp(line(grads(1), lefts, rights)[0], 1)

    def hidden_step(k):
        return lambda *o: up_grad(*o[:2], "hidden", *o[2:5], k, 0, gelu_step, [o[5]], flows, *o[6:])

    def hidden_back(k):
        return lambda *o: up_grad(
            *o[:2], "hidden_back", *o[2:5], k, 1, slope_step, [o[5]], [(count, BF16), (1, F32)], *o[6:]
        )

    activated, slope, grad_expanded, wide = ([None, None] for _ in range(4))
    activated[1], slope[1], other = line(hidden_step(1), normed_two, branch_low_t, ffn[1], widen[1])
    other = over_tp(other, 1)
    grad_expanded[1], wide[1], other_two = line(hidden_back(1), branch_low, normed_two_t, ffn[1], slope[1])
    other_two = over_tp(other_two, 1)
    activated[0], slope[0], *sums = line(hidden_step(0), normed_two, branch_low_t, ffn[0], widen[0], [other])
    shrink_sums = reduce_one(sums)
    grad_expanded[0], wide[0], *sums = line(hidden_back(0), branch_low, normed_two_t, ffn[0], slope[0], [other_two])
    expand_sums = reduce_one(sums)
    grad_second, attn_low, attn_low_t, sums_two, *grad_attended = line(
        lambda *o: down(
            *o[:2], "second_back", o[2], o[3], hidden, 0, functools.partial(norm_back_finish, True),
            [o[4], o[5], o[6][4:5]], [(act, F32), (act, BF16), (turned, BF16), ((4, width), F32)],
            then_up(1, o[7], heads_width, side // heads_width, heads_width // 2)(count),
        ),
        grad_expanded, ffn, second, branch_low, vectors, att,
    )
    shrink_sums = reduce_two(*shrink_sums)
    inner = [None, None]
    inner[1] = line(attend_backward, project[1], others[1], probs[1], attended[1], grad_attended[1])

    def layer_end(roles, after, a, w, t, v):
        ends = jnp.stack([v[6], jnp.full((width,), live)])
        return down(roles, after, "layer_out", a, w, hidden, 1, out_finish, [t, ends], [(act, BF16)])

    (layer_out,) = line(layer_end, activated, ffn, second, vectors)
    layer_out = line.plain(lambda a, p: mxu(a, p, 1, 1).astype(BF16), layer_out, permute)
    layer_out = to_group(layer_out.reshape(group * fine, width))
    expand_sums = reduce_two(*expand_sums)
    inner[0] = line(attend_backward, project[0], others[0], probs[0], attended[0], grad_attended[0])
    ffn_sums = reduce_three(shrink_sums, expand_sums)

    def close(k):
        def total(own, *moves):
            third = own.shape[2] // 3
            return jnp.concatenate([own[:, :, :third], add(own[:, :, third:], *moves)], axis=-1)

        moves = [over_tp(inner[k ^ (d & 1)][d], d) for d in range(1, share)]
        return line.plain(total, inner[k][0], *moves)

    grad_project = [None, None]
    grad_project[1] = close(1)
    attend_other = other_grads([attn_low_t, normed_t], [attended[1], grad_project[1]])
    grad_project[0] = close(0)
    joined_low, joined_low_t, sums_one, merger_other = line(
        lambda *o: down(
            *o[:2], "first_back", o[2], o[3], 3 * heads_width, 1, functools.partial(norm_back_finish, False),
            [o[4], o[5], o[6][1:2]], [(act, BF16), (turned, BF16), ((4, width), F32)],
            then_grad(1, o[7], fs)(width),
        ),
        grad_project, att, joined, grad_second, vectors, both[1],
    )
    merger_other = over_tp(merger_other, 1)
    out = line(
        lambda *o: up(*o[:2], "inputs_back", *o[2:], (0, 1), side, 0, plain_step, flows, 256),
        joined_low, att,
    )
    att_sums = reduce_one(
        line(
            grads(0), [joined_low_t, attn_low_t, normed_t], [both[0], attended[0], grad_project[0]],
            [merger_other, attend_other],
        )
    )
    layer_out = line.gate(layer_out)
    def turn_back(out):
        out = absolute(out).reshape(ts, cs, ts * fine, side)
        return out.transpose(1, 0, 2, 3).reshape(group * ts * fine, side)

    out = to_group(line.plain(turn_back, out))
    ffn_sums = reduce_step(*ffn_sums)
    def vector_sums(one, two, wide):
        sums = jnp.concatenate([one[0:3], two]).reshape(7, fs * cs, rows)
        place = jnp.asarray([ring.index(i) for i in range(cs)], jnp.int32)[c_rank]
        places = [(f_rank - f) % fs * cs + (place - ring.index(c)) % cs for f in range(fs) for c in range(cs)]
        sums = jnp.stack([pick(sums, p, 1) for p in places])
        sums = sums.reshape(fs * cs, 7, ts, small).transpose(0, 2, 1, 3).reshape(devices, 7 * small)
        return jnp.concatenate([sums, absolute(wide).reshape(devices, -1)], axis=1)

    vec = line.plain(vector_sums, sums_one, sums_two, wide).reshape(fs, cs, 2, 2, -1)
    moved = over_tp(pick(vec, 1 - t_rank % 2, 3), 1)
    ffn_sums = reduce_step(*ffn_sums)
    vec = line.plain(lambda v, m: pick(v, t_rank % 2, 3) + m, vec, moved)
    moved = over_tp(pick(vec, 1 - t_rank // 2, 2), 2)
    out = line.gate(out)
    att_sums = reduce_two(*att_sums)
    vec = line.plain(lambda v, m: pick(v, t_rank // 2, 2) + m, vec, moved)
    moved = [over_fsdp(pick(vec, (f_rank - h) % fs), -h) for h in range(1, fs)]
    grad_ffn = reduce_last(*ffn_sums)

    def unpack(out, layer_out):
        out = out.reshape(slots, share, ts, fine, side).transpose(0, 2, 1, 3, 4)
        out = out.reshape(batches, local_seqs, local_len, side).astype(F32)
        layer_out = layer_out.reshape(batches, local_seqs, share * fine, width)
        return out[..., :part_width], out[..., part_width:], layer_out

    grad_tokens, grad_skip, layer_out = line.plain(unpack, out, layer_out)
    att_sums = reduce_three(att_sums)
    vec = line.plain(lambda v, m: sum(m, pick(v, f_rank)), vec, moved)
    moved = [over_ctx(pick(vec, ctx_behind(d)), -d) for d in range(1, cs)]
    att_sums = reduce_step(*att_sums)
    vec = line.plain(lambda v, m: sum(m, pick(v, c_rank)), vec, moved)
    grad_att = reduce_last(*att_sums)
    cut = side + heads_width
    vec_out = [vec[i * small : (i + 1) * small] for i in range(7)] + [vec[7 * small :]]
    return (
        layer_out,
        grad_tokens,
        grad_skip,
        grad_att[:, :side].reshape(merger_weight.shape),
        vec_out[0],
        vec_out[1],
        vec_out[2],
        grad_att[:, cut:].reshape(attend_weight.shape),
        grad_att[:, side:cut],
        vec_out[3],
        vec_out[4],
        vec_out[5],
        grad_ffn[:, hidden:],
        vec_out[7],
        grad_ffn[:, :hidden],
        vec_out[6],
    )


def solution(mesh):
    sizes = tuple(mesh.shape[a] for a in ALL)
    act = P(None, "fsdp", "ctx", "tp")
    vec = P(ALL)
    flat = P(None, "fsdp", ("ctx", "tp"), None)
    w_three = P(("fsdp", "ctx"), None, "tp")
    w_two = P(("fsdp", "ctx"), "tp")
    return jax.shard_map(
        functools.partial(on_device, sizes),
        mesh=mesh,
        in_specs=(
            act, act, w_three, vec, vec, vec, w_three, w_two, vec, vec, vec, w_two, vec, w_two, vec,
            P(None, "fsdp"), flat,
        ),
        out_specs=(
            flat, act, act, w_three, vec, vec, vec, w_three, w_two, vec, vec, vec, w_two, vec, w_two, vec,
        ),
        check_vma=False,
    )
```

```python
import functools

import jax
import jax.numpy as jnp
from jax import lax
from jax.experimental import pallas as pl
from jax.experimental.pallas import tpu as pltpu
from jax.sharding import PartitionSpec as P

HD = 64
EPSILON = 1e-05
F32 = jnp.float32
BF16 = jnp.bfloat16
ALL = ("fsdp", "ctx", "tp")
PARAMS = pltpu.CompilerParams(vmem_limit_bytes=56 * 1024 * 1024)
CHUNK = 128


def mxu(a, b, a_dim, b_dim):
    return lax.dot_general(a, b, (((a_dim,), (b_dim,)), ((), ())), preferred_element_type=F32)


def whole(shape):
    return pl.BlockSpec(shape, lambda *_: (0,) * len(shape))


def call(body, roles, after, *, in_specs, out_specs, out_shape, grid, name, scratch_shapes=()):
    n_in, n_after, n_out = len(in_specs), len(after), len(out_specs)

    def run(roles_ref, *refs):
        outs = refs[n_in + n_after :]
        outs[n_out][...] = jnp.zeros((8, 128), F32)
        body(roles_ref, *refs[:n_in], *outs[:n_out], *outs[n_out + 1 :])

    def apply(*args):
        outs = pl.pallas_call(
            run,
            grid_spec=pltpu.PrefetchScalarGridSpec(
                num_scalar_prefetch=1,
                grid=grid,
                in_specs=[*in_specs, *[pl.BlockSpec(memory_space=pl.ANY)] * n_after],
                out_specs=[*out_specs, whole((8, 128))],
                scratch_shapes=scratch_shapes,
            ),
            out_shape=[*out_shape, jax.ShapeDtypeStruct((8, 128), F32)],
            compiler_params=PARAMS,
            cost_estimate=pl.CostEstimate(flops=1, bytes_accessed=1, transcendentals=0),
            name=name,
        )(roles, *args, *after)
        return outs[:-1], outs[-1]

    return apply


def attend_forward_body(share, heads, roles, *refs):
    own, others = refs[0], refs[1:share]
    p_ref, o_ref = refs[share:]
    part = heads * HD
    rows = lax.broadcasted_iota(jnp.int32, (part, own.shape[1]), 0) // HD
    lanes = lax.broadcasted_iota(jnp.int32, (own.shape[1], part), 1) // HD
    q = own[0, :, :part] * jnp.asarray(HD**-0.5, BF16)
    k = jnp.concatenate([r[0, :, part : 2 * part] for r in (own, *others)], axis=0)
    v = jnp.concatenate([r[0, :, 2 * part :] for r in (own, *others)], axis=0)
    total = jnp.zeros((part, q.shape[0]), F32)
    for h in range(heads):
        s = mxu(k, jnp.where(lanes == h, q, jnp.zeros_like(q)), 1, 1)
        p = jnp.exp(s - jnp.max(s, axis=0, keepdims=True))
        low = (p * (1.0 / jnp.sum(p, axis=0, keepdims=True))).astype(BF16)
        p_ref[0, h] = low
        total = total + jnp.where(rows == h, mxu(v, low, 0, 0), 0.0)
    o_ref[0] = total.T.astype(BF16)


def other_specs(share, shape):
    return [pl.BlockSpec(shape, lambda x, _, d=d: (x ^ (d >> 1), 0, 0)) for d in range(1, share)]


def attend_forward(roles, after, own, others):
    blocks, count, cols = own.shape
    share = 1 + len(others)
    part = cols // 3
    heads = part // HD
    return call(
        functools.partial(attend_forward_body, share, heads),
        roles,
        after,
        grid=(blocks,),
        in_specs=[pl.BlockSpec((1, count, cols), lambda x, _: (x, 0, 0))] + other_specs(share, (1, count, cols)),
        out_specs=[
            pl.BlockSpec((1, heads, share * count, count), lambda x, _: (x, 0, 0, 0)),
            pl.BlockSpec((1, count, part), lambda x, _: (x, 0, 0)),
        ],
        out_shape=[
            jax.ShapeDtypeStruct((blocks, heads, share * count, count), BF16),
            jax.ShapeDtypeStruct((blocks, count, part), BF16),
        ],
        name="attend_forward",
    )(own, *others)


def attend_backward_body(share, heads, roles, *refs):
    own, others = refs[0], refs[1:share]
    p_ref, o_ref, g_ref = refs[share : share + 3]
    outs = refs[share + 3 :]
    part = heads * HD
    count = own.shape[1]
    q = own[0, :, :part] * jnp.asarray(HD**-0.5, BF16)
    k = jnp.concatenate([r[0, :, part : 2 * part] for r in (own, *others)], axis=0)
    v = jnp.concatenate([r[0, :, 2 * part :] for r in (own, *others)], axis=0)
    g = g_ref[0]
    rows = lax.broadcasted_iota(jnp.int32, (part, count), 0) // HD
    lanes = lax.broadcasted_iota(jnp.int32, (count, part), 1) // HD
    prod = (g.astype(F32) * o_ref[0].astype(F32)).T
    dq = jnp.zeros((part, count), F32)
    dk = jnp.zeros((share * count, part), F32)
    dv = jnp.zeros((share * count, part), F32)
    for h in range(heads):
        q_h = jnp.where(lanes == h, q, jnp.zeros_like(q))
        g_h = jnp.where(lanes == h, g, jnp.zeros_like(g))
        p = p_ref[0, h]
        delta = jnp.sum(prod[h * HD : (h + 1) * HD], axis=0, keepdims=True)
        ds = (p.astype(F32) * (mxu(v, g_h, 1, 1) - delta)).astype(BF16)
        dq = dq + jnp.where(rows == h, mxu(k, ds, 0, 0), 0.0)
        dk = dk + mxu(ds, q_h, 1, 0)
        dv = dv + mxu(p, g_h, 1, 0)
    outs[0][0, :, :part] = (dq.T * (HD**-0.5)).astype(BF16)
    outs[0][0, :, part : 2 * part] = dk[:count].astype(BF16)
    outs[0][0, :, 2 * part :] = dv[:count].astype(BF16)
    for d in range(1, share):
        outs[d][0, :, :part] = dk[d * count : (d + 1) * count].astype(BF16)
        outs[d][0, :, part:] = dv[d * count : (d + 1) * count].astype(BF16)


def attend_backward(roles, after, own, others, probs, attended, grad):
    blocks, count, cols = own.shape
    share = 1 + len(others)
    part = cols // 3
    heads = part // HD
    spec = pl.BlockSpec((1, count, cols), lambda x, _: (x, 0, 0))
    o_spec = pl.BlockSpec((1, count, part), lambda x, _: (x, 0, 0))
    p_spec = pl.BlockSpec((1, heads, share * count, count), lambda x, _: (x, 0, 0, 0))
    return call(
        functools.partial(attend_backward_body, share, heads),
        roles,
        after,
        grid=(blocks,),
        in_specs=[spec] + other_specs(share, (1, count, cols)) + [p_spec, o_spec, o_spec],
        out_specs=[spec] + other_specs(share, (1, count, 2 * part)),
        out_shape=[jax.ShapeDtypeStruct((blocks, count, cols), BF16)]
        + [jax.ShapeDtypeStruct((blocks, count, 2 * part), BF16)] * (share - 1),
        name="attend_backward",
    )(own, *others, probs, attended, grad)


def up_tiles(left, w, k, parts, roles):
    rows = left.shape[1] // parts

    def term(x, h, at):
        return mxu(left[:, pl.ds(at * rows, rows)], w[x][h], 1, 0)

    if parts != 2:
        return [sum(term(x, h, h) for h in range(parts)) for x in range(2)]
    role = roles[k]
    one, two = term(0, 1, 1 - role), term(1, 0, role)
    return [
        term(0, 0, 0) + jnp.where(role == 0, one, two),
        term(1, 1, 1) + jnp.where(role == 0, two, one),
    ]


def up_body(ks, parts, step, roles, *refs):
    left = refs[0]
    for i, k in enumerate(ks):
        for x, tile in enumerate(up_tiles(left, refs[1 + 2 * i : 3 + 2 * i], k, parts, roles)):
            step(i, x, tile, refs[1 + 2 * len(ks) :])


def up(roles, after, name, left, weights, ks, width, col, step, outs, tile):
    parts, rows, _ = weights[0][0].shape
    per = width // tile
    count = left.shape[0]
    return call(
        functools.partial(up_body, ks, parts, step),
        roles,
        after,
        grid=(per,),
        in_specs=[whole((count, parts * rows))]
        + [pl.BlockSpec((parts, rows, tile), lambda n, _: (0, 0, col * per + n))] * (2 * len(ks)),
        out_specs=[pl.BlockSpec((2, o[0], tile), lambda n, _: (0, 0, n)) for o in outs],
        out_shape=[jax.ShapeDtypeStruct((2, o[0], width), o[1]) for o in outs],
        name=name,
    )(left, *[a for w in weights for a in w])


def up_grad_body(k, parts, step, n_extra, n_out, n_more, roles, left, left_t, *refs):
    w, extras, more = refs[:2], refs[2 : 2 + n_extra], refs[2 + n_extra : 2 + n_extra + n_more]
    outs = refs[2 + n_extra + n_more : 2 + n_extra + n_more + n_out]
    ends, kept = refs[2 + n_extra + n_more + n_out : -1], refs[-1]
    for x, tile in enumerate(up_tiles(left, w, k, parts, roles)):
        kept[x] = step(x, tile, extras, outs)
    rows = left_t.shape[0] // parts
    role = roles[k]
    for a in range(2):
        for b in range(parts):
            total = mxu(left_t[pl.ds((b + role * (a - b)) * rows, rows), :], kept[a + role * (b - a)], 1, 0)
            if n_more:
                ends[a][b] = (total + more[0][a, b].astype(F32)).astype(BF16)
            else:
                ends[0][a, b] = total.astype(BF16)


def up_grad(roles, after, name, left, left_t, weights, k, col, step, extras, outs, more=()):
    parts, rows, _ = weights[0].shape
    tile = 256
    width = extras[0].shape[2]
    per = width // tile
    count = left.shape[0]
    thin = lambda r: pl.BlockSpec((2, r, tile), lambda n, _: (0, 0, n))
    pair = pl.BlockSpec((2, parts, rows, tile), lambda n, _: (0, 0, 0, n))
    single = pl.BlockSpec((parts, rows, tile), lambda n, _: (0, 0, n))
    ends = [(single, (parts, rows, width))] * 2 if more else [(pair, (2, parts, rows, width))]
    return call(
        functools.partial(up_grad_body, k, parts, step, len(extras), len(outs), len(more)),
        roles,
        after,
        grid=(per,),
        in_specs=[whole(left.shape), whole(left_t.shape)]
        + [pl.BlockSpec((parts, rows, tile), lambda n, _: (0, 0, col * per + n))] * 2
        + [thin(e.shape[1]) for e in extras]
        + [pair] * len(more),
        out_specs=[thin(o[0]) for o in outs] + [e[0] for e in ends],
        out_shape=[jax.ShapeDtypeStruct((2, o[0], width), o[1]) for o in outs]
        + [jax.ShapeDtypeStruct(e[1], BF16) for e in ends],
        scratch_shapes=[pltpu.VMEM((2, count, tile), BF16)],
        name=name,
    )(left, left_t, *weights, *extras, *more)


def plain_step(i, x, total, refs):
    refs[i][x] = total.astype(BF16)


def gelu_step(x, total, extras, outs):
    act, slope = outs
    v = total + extras[0][x]
    half = 0.5 * (1.0 + lax.erf(v * (0.5**0.5)))
    low = (v * half).astype(BF16)
    act[x] = low
    slope[x] = (half + v * jnp.exp(-0.5 * v * v) * 0.3989422804014327).astype(BF16)
    return low


def slope_step(x, total, extras, outs):
    grad, sums = outs
    low = (total * extras[0][x].astype(F32)).astype(BF16)
    grad[x] = low
    sums[x] = jnp.sum(low.astype(F32), axis=0, keepdims=True)
    return low


def down_body(parts, per, finish, n_extra, n_out, n_in, body, roles, *refs):
    extras = refs[6 : 6 + n_extra]
    outs = refs[6 + n_extra + n_in : 6 + n_extra + n_in + n_out]
    acc = refs[-1]
    n = pl.program_id(0)

    @pl.when(n < per)
    def _():
        total = [0] * parts
        for k in range(2):
            left, w = refs[k], refs[2 + 2 * k : 4 + 2 * k]

            def term(x, h, at):
                return mxu(left[at], w[x][h], 1, 1)

            if parts == 2:
                role = roles[k]
                one, two = term(0, 1, role), term(1, 0, 1 - role)
                total[0] = total[0] + term(0, 0, 0) + jnp.where(role == 0, two, one)
                total[1] = total[1] + term(1, 1, 1) + jnp.where(role == 0, one, two)
            else:
                for h in range(parts):
                    total[h] = total[h] + term(0, h, 0) + term(1, h, 1)
        for h in range(parts):
            acc[h * per + n] = total[h]

    @pl.when(n == per - 1)
    def _():
        finish(acc, [*extras, *outs])

    if body is not None:

        @pl.when(n >= per)
        def _():
            body(roles, outs, refs[6 + n_extra : 6 + n_extra + n_in], refs[6 + n_extra + n_in + n_out : -1])


def down(roles, after, name, lefts, weights, width, col, finish, extras, outs, then=(0, None, [], [])):
    parts, rows, _ = weights[0][0].shape
    tile = min(256, rows)
    per = rows // tile
    count = lefts[0].shape[1]
    steps, body, ins, more = then

    def late(block, index):
        return pl.BlockSpec(block, lambda n, _: index(jnp.maximum(n - per, 0)))

    return call(
        functools.partial(down_body, parts, per, finish, len(extras), len(outs), len(ins), body),
        roles,
        after,
        grid=(per + steps,),
        in_specs=[whole((2, count, width))] * 2
        + [pl.BlockSpec((parts, tile, width), lambda n, _: (0, jnp.minimum(n, per - 1), col))] * 4
        + [whole(e.shape) for e in extras]
        + [late(*i[1:]) for i in ins],
        out_specs=[whole(o[0]) for o in outs] + [late(*m[2:]) for m in more],
        out_shape=[jax.ShapeDtypeStruct(*o) for o in outs] + [jax.ShapeDtypeStruct(*m[:2]) for m in more],
        scratch_shapes=[pltpu.VMEM((parts * rows // tile, count, tile), F32)],
        name=name,
    )(*lefts, *weights[0], *weights[1], *extras, *[i[0] for i in ins])


def then_up(place, weights, width, col, tile):
    parts, rows, _ = weights[0][0].shape
    per = width // tile

    def body(roles, outs, ins, ends):
        for k in range(2):
            for x, total in enumerate(up_tiles(outs[place], ins[2 * k : 2 * k + 2], k, parts, roles)):
                ends[k][x] = total.astype(BF16)

    def of(count):
        return (
            per,
            body,
            [(a, (parts, rows, tile), lambda m: (0, 0, col * per + m)) for w in weights for a in w],
            [((2, count, width), BF16, (2, count, tile), lambda m: (0, 0, m))] * 2,
        )

    return of


def then_grad(place, right, parts):
    _, count, cols = right.shape

    def body(roles, outs, ins, ends):
        b = pl.program_id(0) - pl.num_programs(0) + parts
        rows = outs[place].shape[0] // parts
        role = roles[1]
        for a in range(2):
            left = outs[place][pl.ds((b + role * (a - b)) * rows, rows), :]
            ends[0][a] = mxu(left, ins[0][a + role * (b - a)], 1, 0).astype(BF16)

    def of(depth):
        rows = depth // parts
        return (
            parts,
            body,
            [(right, right.shape, lambda m: (0, 0, 0))],
            [((2, parts, rows, cols), BF16, (2, None, rows, cols), lambda m: (0, m, 0, 0))],
        )

    return of


def row_mean(tiles):
    total = sum(jnp.sum(t, axis=-1, keepdims=True) for t in tiles)
    return total / sum(t.shape[-1] for t in tiles)


def norm_finish(has_residual, acc, refs):
    refs = list(refs)
    residual = refs.pop(0) if has_residual else None
    rows, total_ref, low_ref, low_t_ref = refs
    tiles, count, width = acc.shape
    for r in range(0, count, CHUNK):
        rr = pl.ds(r, CHUNK)
        total = []
        for i in range(tiles):
            cc = slice(i * width, (i + 1) * width)
            v = acc[i, rr, :] + rows[0:1, cc]
            if residual is not None:
                v = v + residual[rr, cc]
            total_ref[rr, cc] = v
            total.append(v)
        mean = row_mean(total)
        center = [t - mean for t in total]
        scale = lax.rsqrt(row_mean([c * c for c in center]) + EPSILON)
        for i in range(tiles):
            cc = slice(i * width, (i + 1) * width)
            v = center[i] * scale * rows[1:2, cc] + rows[2:3, cc]
            low_ref[rr, cc] = v.astype(BF16)
            low_t_ref[cc, rr] = v.T.astype(BF16)


def norm_back_finish(keep, acc, refs):
    total_ref, up_ref, rows, *outs = refs
    full_ref = outs.pop(0) if keep else None
    low_ref, low_t_ref, sums_ref = outs
    tiles, count, width = acc.shape
    zero = jnp.zeros((1, width), F32)
    sums = [[zero] * tiles for _ in range(4)]
    for r in range(0, count, CHUNK):
        rr = pl.ds(r, CHUNK)
        cuts = [slice(i * width, (i + 1) * width) for i in range(tiles)]
        total = [total_ref[rr, cc] for cc in cuts]
        mean = row_mean(total)
        center = [t - mean for t in total]
        scale = lax.rsqrt(row_mean([c * c for c in center]) + EPSILON)
        unit = [c * scale for c in center]
        grad = [acc[i, rr, :] for i in range(tiles)]
        z = [g * rows[0:1, cc] for g, cc in zip(grad, cuts)]
        z_mean = row_mean(z)
        zu_mean = row_mean([a * b for a, b in zip(z, unit)])
        for i, cc in enumerate(cuts):
            up_now = up_ref[rr, cc].astype(F32)
            v = up_now + scale * (z[i] - z_mean - unit[i] * zu_mean)
            if keep:
                full_ref[rr, cc] = v
            low_ref[rr, cc] = v.astype(BF16)
            low_t_ref[cc, rr] = v.T.astype(BF16)
            for j, s in enumerate((v, grad[i] * unit[i], grad[i], up_now)):
                sums[j][i] = sums[j][i] + jnp.sum(s, axis=0, keepdims=True)
    for j in range(4):
        for i in range(tiles):
            sums_ref[j : j + 1, i * width : (i + 1) * width] = sums[j][i]


def out_finish(acc, refs):
    total_ref, rows, low_ref = refs
    tiles, count, width = acc.shape
    for i in range(tiles):
        cc = slice(i * width, (i + 1) * width)
        v = (acc[i] + total_ref[:, cc] + rows[0:1, cc]) * rows[1:2, cc]
        low_ref[:, cc] = v.astype(BF16)


def arrived_body(roles, cot, permute, live, low_ref, low_t_ref):
    low = mxu(cot[...], permute[...], 1, 0) * live[...]
    low_ref[...] = low.astype(BF16)
    low_t_ref[...] = low.T.astype(BF16)


def arrived(roles, after, cot, permute, live):
    count, width = cot.shape
    tile = min(256, width)
    return call(
        arrived_body,
        roles,
        after,
        grid=(width // tile,),
        in_specs=[whole(cot.shape), pl.BlockSpec((width, tile), lambda n, _: (0, n)), whole((1, 1))],
        out_specs=[pl.BlockSpec((count, tile), lambda n, _: (0, n)), pl.BlockSpec((tile, count), lambda n, _: (n, 0))],
        out_shape=[jax.ShapeDtypeStruct((count, width), BF16), jax.ShapeDtypeStruct((width, count), BF16)],
        name="arrived",
    )(cot, permute, live.reshape(1, 1))


def weight_grad_body(n_parts, n_more, own, roles, *refs):
    ends = refs[4 * n_parts + n_more :]
    for a in range(2):
        at = 0
        more = [m[a].astype(F32) for m in refs[4 * n_parts : 4 * n_parts + n_more]]
        for p in range(n_parts):
            left, right = refs[4 * p + 2 * a : 4 * p + 2 * a + 2]
            total = mxu(left[...], right[...], 1, 0)
            cc = slice(at, at + total.shape[1])
            at = cc.stop
            if own:
                start = 0
                for m in more:
                    if start <= cc.start and cc.stop <= start + m.shape[1]:
                        total = total + m[:, cc.start - start : cc.stop - start]
                    start += m.shape[1]
                ends[a][:, cc] = total.astype(BF16)
            else:
                ends[0][a, :, cc] = total.astype(BF16)


def weight_grad(roles, after, lefts, rights, parts, k, more=()):
    depth, count = lefts[0].shape
    rows = depth // parts
    tile = min(256, rows)
    per = rows // tile
    cols = sum(r.shape[2] for r in rights)
    own = k == 0
    specs, args = [], []
    for left, right in zip(lefts, rights):
        for a in range(2):
            specs += [
                pl.BlockSpec((tile, count), lambda b, n, p, a=a: ((b + p[k] * (a - b)) * per + n, 0)),
                pl.BlockSpec((None, count, right.shape[2]), lambda b, n, p, a=a: (a + p[k] * (b - a), 0, 0)),
            ]
            args += [left, right]
    pair = lambda width: pl.BlockSpec((2, None, tile, width), lambda b, n, _: (0, b, n, 0))
    if own:
        out_specs = [pl.BlockSpec((None, tile, cols), lambda b, n, _: (b, n, 0))] * 2
        out_shape = [jax.ShapeDtypeStruct((parts, rows, cols), BF16)] * 2
    else:
        out_specs = [pair(cols)]
        out_shape = [jax.ShapeDtypeStruct((2, parts, rows, cols), BF16)]
    return call(
        functools.partial(weight_grad_body, len(lefts), len(more), own),
        roles,
        after,
        grid=(parts, per),
        in_specs=specs + [pair(m.shape[3]) for m in more],
        out_specs=out_specs,
        out_shape=out_shape,
        name="weight_grad",
    )(*args, *more)


def pick(array, index, axis=0):
    return lax.dynamic_index_in_dim(array, index, axis, keepdims=False)


def add(*terms):
    return sum(t.astype(F32) for t in terms).astype(BF16)


class Line:
    def __init__(self, roles):
        self.roles, self.marks = roles, []

    def gate(self, *arrays):
        leaves, form = jax.tree.flatten(arrays)
        places = [i for i, leaf in enumerate(leaves) if isinstance(leaf, jax.Array)]
        held, self.marks = lax.optimization_barrier(([leaves[i] for i in places], self.marks))
        for i, array in zip(places, held):
            leaves[i] = array
        arrays = jax.tree.unflatten(form, leaves)
        return arrays[0] if len(arrays) == 1 else arrays

    def plain(self, step, *args):
        out = step(*self.gate(args, ())[0])
        self.marks = self.marks + jax.tree.leaves(out)
        return out

    def __call__(self, step, *args):
        args = self.gate(args, ())[0]
        out, mark = step(self.roles, self.marks, *args)
        self.marks = [mark]
        return out


def on_device(
    sizes,
    tokens,
    skip_tokens,
    merger_weight,
    merger_bias,
    first_gain,
    first_shift,
    attend_weight,
    output_weight,
    output_bias,
    second_gain,
    second_shift,
    expand_weight,
    widen_bias,
    shrink_weight,
    shrink_bias,
    live_slots,
    cotangent,
):
    fs, cs, ts = sizes
    assert ts == 4
    f_rank, c_rank, t_rank = (lax.axis_index(a) for a in ALL)
    group = cs * ts
    devices = fs * group
    batches, local_seqs, local_len, part_width = tokens.shape
    slots = batches * local_seqs
    share = group // slots
    assert share in (1, 2, 4)
    fine = cotangent.shape[2] // share
    width = cotangent.shape[3]
    count = group * fine
    hidden = expand_weight.shape[1]
    rows = width // (fs * cs)
    role = t_rank % 2 if fs == 2 else 0 * t_rank
    line = Line(jnp.stack([role, (1 - role) if fs == 2 else role]).astype(jnp.int32))

    def to_group(array):
        return lax.all_to_all(array, ("ctx", "tp"), 0, 0, tiled=True)

    def over_tp(array, flip):
        return lax.ppermute(array, "tp", [(i, i ^ flip) for i in range(ts)])

    ring = list(range(0, cs, 2)) + list(range(cs - 1 - cs % 2, 0, -2))

    def over_ctx(array, d):
        return lax.ppermute(array, "ctx", [(ring[i], ring[(i + d) % cs]) for i in range(cs)])

    def ctx_behind(d):
        return jnp.asarray([ring[(ring.index(i) - d) % cs] for i in range(cs)], jnp.int32)[c_rank]

    def over_fsdp(array, d):
        return lax.ppermute(array, "fsdp", [(i, (i + d) % fs) for i in range(fs)])

    def first_pairs(i):
        f, c, t = i // (cs * ts), i // ts % cs, i % ts
        f, t = (f, t ^ 2) if t % 2 else (1 - f, t)
        return (f * cs + c) * ts + t

    def second_pairs(i):
        f, c, t = i // (cs * ts), i // ts % cs, i % ts
        f, t = (1 - f, t) if t % 2 else (f, t ^ 2)
        return (f * cs + c) * ts + t

    def over(array, target):
        return lax.ppermute(array, ALL, [(i, target(i)) for i in range(devices)])

    def gather_ctx(piece):
        return [piece] + [over_ctx(piece, d) for d in range(1, cs)]

    def ring_start(piece):
        return [piece, over_ctx(piece, 1)]

    def ring_step(moved):
        *kept, last = moved
        last = line.gate(last)
        return [*kept, last, over_ctx(last, 1)] if len(moved) < cs else [*kept, last]

    def gather_one(moved):
        own = line.plain(lambda *m: jnp.concatenate(m, axis=0), *moved)
        return own, [over(own, first_pairs)] if fs == 2 else [over_fsdp(own, h) for h in range(1, fs)]

    def gather_two(own, moved):
        first = line.plain(lambda a, m: jnp.stack([a, *m]), own, moved)
        return first, second_move(first)

    def second_move(first):
        return over(first, second_pairs) if fs == 2 else over_tp(first, 2)

    def gather_near(first, second):
        first = line.gate(first)
        return first, second, over_tp(first, 1)

    def gather_three(first, second, other):
        first, second, other = line.gate(first, second, other)
        return [[first, second], [other, over_tp(second, 1)]]

    def reduce_one(sums):
        keep, send = sums
        return keep, over(send, second_pairs) if fs == 2 else over_tp(send, 2)

    def reduce_two(keep, moved):
        sums = line.plain(lambda a, m: [add(a[h], m[h]) for h in range(fs)], keep, moved)
        if fs == 2:
            return sums[0], [over(sums[1], first_pairs)]
        return sums[0], [over_fsdp(sums[h], -h) for h in range(1, fs)]

    def reduce_three(*sums):
        def pieces(*sums):
            total = jnp.concatenate([add(own, *moved) for own, moved in sums], axis=1).reshape(cs, rows, -1)
            return [total[d] for d in range(cs)]

        parts = line.plain(pieces, *sums)
        return parts, over_ctx(parts[-1], -1)

    def reduce_step(parts, moving):
        *parts, last = line.plain(lambda p, m: [*p[:-2], add(p[-2], m)], parts, moving)
        return [*parts, last], over_ctx(last, -1)

    def reduce_last(parts, moving):
        while len(parts) > 2:
            parts, moving = reduce_step(parts, moving)
        return line.plain(lambda p, m: p.astype(F32) + m.astype(F32), parts[0], moving)

    spread = lambda blocks: [blocks[0][0], blocks[1][0], blocks[0][1], blocks[1][1]]
    owner = jnp.stack(
        [(f_rank - h) % fs * cs + ctx_behind(d) for h in range(fs) for d in range(cs)]
    )
    features = lax.broadcasted_iota(jnp.int32, (width, width), 0)
    places = (owner[:, None] * rows + jnp.arange(rows)[None, :]).reshape(1, width)
    permute = (features == places).astype(BF16)

    def relative(array, axis=0):
        return [
            jnp.stack([pick(array, t_rank ^ (2 * x + k), axis) for x in range(2)]) for k in range(2)
        ]

    def absolute(blocks):
        blocks = jnp.stack(spread(blocks))
        return jnp.stack([pick(blocks, t_rank ^ t) for t in range(ts)])

    flat = lambda w: w.reshape(w.shape[0], -1)
    side = merger_weight.shape[1] * merger_weight.shape[2]
    heads_width = output_weight.shape[1]

    def pack_att(m, o, a):
        return jnp.concatenate([flat(m), o, flat(a)], axis=1)

    def split_rows(one, two):
        array = jnp.concatenate([one, two], axis=-1)
        array = array.reshape(slots, ts, share, fine, -1).transpose(0, 2, 1, 3, 4)
        return array.reshape(group * ts * fine, -1)

    small = merger_bias.shape[0]
    att = gather_ctx(line.plain(pack_att, merger_weight, output_weight, attend_weight))
    packed = line.plain(
        lambda *v: jnp.broadcast_to(jnp.concatenate(v), (devices, sum(x.shape[0] for x in v))),
        merger_bias, first_gain, first_shift, output_bias, second_gain, second_shift, shrink_bias, widen_bias,
    )
    packed = lax.all_to_all(packed, ALL, 0, 0, tiled=True)
    both = line.plain(split_rows, tokens, skip_tokens)
    ffn = line.plain(lambda a, b: jnp.concatenate([a, b], axis=1), expand_weight, shrink_weight)
    packed = line.gate(packed)
    cot = to_group(line.gate(cotangent).reshape(group * fine, width))
    att = gather_one(att)
    ffn = ring_start(line.gate(ffn))
    ffn = ring_step(ffn)
    att = gather_near(*gather_two(*att))
    for _ in range(3, cs):
        ffn = ring_step(ffn)
    cot = line.gate(cot)
    both = to_group(line.gate(both))
    ffn = gather_one(ring_step(ffn))

    live = pick(live_slots.reshape(slots), (c_rank * ts + t_rank) // share).astype(F32)
    branch_low, branch_low_t = line(arrived, cot.reshape(count, width), permute, live)

    def vectors_of(packed):
        vectors = packed[:, : 7 * small].reshape(fs * cs, ts, 7, small).transpose(0, 2, 1, 3)
        vectors = vectors.reshape(fs * cs, 7, rows)
        vectors = jnp.stack([pick(vectors, owner[i]) for i in range(fs * cs)], axis=1).reshape(7, width)
        return vectors, relative(packed[:, 7 * small :].reshape(ts, 1, hidden))

    def blocks_of(both):
        both = relative(both.reshape(cs, ts, ts * fine, side), 1)
        return [b.reshape(2, count, side) for b in both]

    vectors, widen = line.plain(vectors_of, packed)
    att = gather_three(*att)
    both = line.plain(blocks_of, both)
    act = (count, width)
    turned = (width, count)
    flows = [(count, BF16)] * 2

    joined, normed, normed_t, *project = line(
        lambda *o: down(
            *o[:2], "joined", o[2], o[3], side, 0, functools.partial(norm_finish, False), [o[4][0:3]],
            [(act, F32), (act, BF16), (turned, BF16)],
            then_up(1, o[3], 3 * heads_width, 1, heads_width)(count),
        ),
        both, att, vectors,
    )
    def halves(own, moved):
        cuts = [slice(0, hidden), slice(hidden, None)]
        return [jnp.stack([p[:, cc] for p in (own, *moved)]) for cc in cuts]

    expand, shrink = [(p, second_move(p)) for p in line.plain(halves, *ffn)]
    others = [[over_tp(project[k ^ (d & 1)], d) for d in range(1, share)] for k in range(2)]
    others = line.gate(others)
    inner = [line(attend_forward, project[0], others[0])]
    expand = gather_near(*expand)
    inner.append(line(attend_forward, project[1], others[1]))
    shrink = gather_near(*shrink)
    probs, attended = zip(*inner)

    expand = gather_three(*expand)
    second, normed_two, normed_two_t = line(
        lambda *o: down(
            *o[:2], "second", o[2], o[3], heads_width, side // heads_width, functools.partial(norm_finish, True),
            [o[4], o[5][3:6]], [(act, F32), (act, BF16), (turned, BF16)],
        ),
        attended, att, joined, vectors,
    )

    def grads(k):
        return lambda roles, after, lefts, rights, more=(): weight_grad(roles, after, lefts, rights, fs, k, more)

    def other_grads(lefts, rights):
        return over_tp(line(grads(1), lefts, rights)[0], 1)

    def hidden_step(k):
        return lambda *o: up_grad(*o[:2], "hidden", *o[2:5], k, 0, gelu_step, [o[5]], flows, *o[6:])

    def hidden_back(k):
        return lambda *o: up_grad(
            *o[:2], "hidden_back", *o[2:5], k, 0, slope_step, [o[5]], [(count, BF16), (1, F32)], *o[6:]
        )

    shrink = gather_three(*shrink)
    activated, slope, grad_expanded, wide = ([None, None] for _ in range(4))
    activated[1], slope[1], other = line(hidden_step(1), normed_two, branch_low_t, expand[1], widen[1])
    other = over_tp(other, 1)
    grad_expanded[1], wide[1], other_two = line(hidden_back(1), branch_low, normed_two_t, shrink[1], slope[1])
    other_two = over_tp(other_two, 1)
    activated[0], slope[0], *sums = line(hidden_step(0), normed_two, branch_low_t, expand[0], widen[0], [other])
    shrink_sums = reduce_one(sums)
    grad_expanded[0], wide[0], *sums = line(hidden_back(0), branch_low, normed_two_t, shrink[0], slope[0], [other_two])
    expand_sums = reduce_one(sums)
    grad_second, attn_low, attn_low_t, sums_two, *grad_attended = line(
        lambda *o: down(
            *o[:2], "second_back", o[2], o[3], hidden, 0, functools.partial(norm_back_finish, True),
            [o[4], o[5], o[6][4:5]], [(act, F32), (act, BF16), (turned, BF16), ((4, width), F32)],
            then_up(1, o[7], heads_width, side // heads_width, heads_width // 2)(count),
        ),
        grad_expanded, expand, second, branch_low, vectors, att,
    )
    shrink_sums = reduce_two(*shrink_sums)
    inner = [None, None]
    inner[1] = line(attend_backward, project[1], others[1], probs[1], attended[1], grad_attended[1])

    def layer_end(roles, after, a, w, t, v):
        ends = jnp.stack([v[6], jnp.full((width,), live)])
        return down(roles, after, "layer_out", a, w, hidden, 0, out_finish, [t, ends], [(act, BF16)])

    (layer_out,) = line(layer_end, activated, shrink, second, vectors)
    layer_out = line.plain(lambda a, p: mxu(a, p, 1, 1).astype(BF16), layer_out, permute)
    layer_out = to_group(layer_out.reshape(group * fine, width))
    expand_sums = reduce_two(*expand_sums)
    inner[0] = line(attend_backward, project[0], others[0], probs[0], attended[0], grad_attended[0])
    ffn_sums = reduce_three(shrink_sums, expand_sums)

    def close(k):
        def total(own, *moves):
            third = own.shape[2] // 3
            return jnp.concatenate([own[:, :, :third], add(own[:, :, third:], *moves)], axis=-1)

        moves = [over_tp(inner[k ^ (d & 1)][d], d) for d in range(1, share)]
        return line.plain(total, inner[k][0], *moves)

    grad_project = [None, None]
    grad_project[1] = close(1)
    attend_other = other_grads([attn_low_t, normed_t], [attended[1], grad_project[1]])
    grad_project[0] = close(0)
    joined_low, joined_low_t, sums_one, merger_other = line(
        lambda *o: down(
            *o[:2], "first_back", o[2], o[3], 3 * heads_width, 1, functools.partial(norm_back_finish, False),
            [o[4], o[5], o[6][1:2]], [(act, BF16), (turned, BF16), ((4, width), F32)],
            then_grad(1, o[7], fs)(width),
        ),
        grad_project, att, joined, grad_second, vectors, both[1],
    )
    merger_other = over_tp(merger_other, 1)
    out = line(
        lambda *o: up(*o[:2], "inputs_back", *o[2:], (0, 1), side, 0, plain_step, flows, 256),
        joined_low, att,
    )
    att_sums = reduce_one(
        line(
            grads(0), [joined_low_t, attn_low_t, normed_t], [both[0], attended[0], grad_project[0]],
            [merger_other, attend_other],
        )
    )
    layer_out = line.gate(layer_out)
    def turn_back(out):
        out = absolute(out).reshape(ts, cs, ts * fine, side)
        return out.transpose(1, 0, 2, 3).reshape(group * ts * fine, side)

    out = to_group(line.plain(turn_back, out))
    ffn_sums = reduce_step(*ffn_sums)
    def vector_sums(one, two, wide):
        sums = jnp.concatenate([one[0:3], two]).reshape(7, fs * cs, rows)
        place = jnp.asarray([ring.index(i) for i in range(cs)], jnp.int32)[c_rank]
        places = [(f_rank - f) % fs * cs + (place - ring.index(c)) % cs for f in range(fs) for c in range(cs)]
        sums = jnp.stack([pick(sums, p, 1) for p in places])
        sums = sums.reshape(fs * cs, 7, ts, small).transpose(0, 2, 1, 3).reshape(devices, 7 * small)
        return jnp.concatenate([sums, absolute(wide).reshape(devices, -1)], axis=1)

    vec = line.plain(vector_sums, sums_one, sums_two, wide).reshape(fs, cs, 2, 2, -1)
    moved = over_tp(pick(vec, 1 - t_rank % 2, 3), 1)
    ffn_sums = reduce_step(*ffn_sums)
    vec = line.plain(lambda v, m: pick(v, t_rank % 2, 3) + m, vec, moved)
    moved = over_tp(pick(vec, 1 - t_rank // 2, 2), 2)
    out = line.gate(out)
    att_sums = reduce_two(*att_sums)
    vec = line.plain(lambda v, m: pick(v, t_rank // 2, 2) + m, vec, moved)
    moved = [over_fsdp(pick(vec, (f_rank - h) % fs), -h) for h in range(1, fs)]
    grad_ffn = reduce_last(*ffn_sums)

    def unpack(out, layer_out):
        out = out.reshape(slots, share, ts, fine, side).transpose(0, 2, 1, 3, 4)
        out = out.reshape(batches, local_seqs, local_len, side).astype(F32)
        layer_out = layer_out.reshape(batches, local_seqs, share * fine, width)
        return out[..., :part_width], out[..., part_width:], layer_out

    grad_tokens, grad_skip, layer_out = line.plain(unpack, out, layer_out)
    att_sums = reduce_three(att_sums)
    vec = line.plain(lambda v, m: sum(m, pick(v, f_rank)), vec, moved)
    moved = [over_ctx(pick(vec, ctx_behind(d)), -d) for d in range(1, cs)]
    att_sums = reduce_step(*att_sums)
    vec = line.plain(lambda v, m: sum(m, pick(v, c_rank)), vec, moved)
    grad_att = reduce_last(*att_sums)
    cut = side + heads_width
    vec_out = [vec[i * small : (i + 1) * small] for i in range(7)] + [vec[7 * small :]]
    return (
        layer_out,
        grad_tokens,
        grad_skip,
        grad_att[:, :side].reshape(merger_weight.shape),
        vec_out[0],
        vec_out[1],
        vec_out[2],
        grad_att[:, cut:].reshape(attend_weight.shape),
        grad_att[:, side:cut],
        vec_out[3],
        vec_out[4],
        vec_out[5],
        grad_ffn[:, hidden:],
        vec_out[7],
        grad_ffn[:, :hidden],
        vec_out[6],
    )


def solution(mesh):
    sizes = tuple(mesh.shape[a] for a in ALL)
    act = P(None, "fsdp", "ctx", "tp")
    vec = P(ALL)
    flat = P(None, "fsdp", ("ctx", "tp"), None)
    w_three = P(("fsdp", "ctx"), None, "tp")
    w_two = P(("fsdp", "ctx"), "tp")
    return jax.shard_map(
        functools.partial(on_device, sizes),
        mesh=mesh,
        in_specs=(
            act, act, w_three, vec, vec, vec, w_three, w_two, vec, vec, vec, w_two, vec, w_two, vec,
            P(None, "fsdp"), flat,
        ),
        out_specs=(
            flat, act, act, w_three, vec, vec, vec, w_three, w_two, vec, vec, vec, w_two, vec, w_two, vec,
        ),
        check_vma=False,
    )
```

```python
import functools

import jax
import jax.numpy as jnp
from jax import lax
from jax.experimental import pallas as pl
from jax.experimental.pallas import tpu as pltpu
from jax.sharding import PartitionSpec as P

HD = 64
EPSILON = 1e-05
F32 = jnp.float32
BF16 = jnp.bfloat16
ALL = ("fsdp", "ctx", "tp")
PARAMS = pltpu.CompilerParams(vmem_limit_bytes=56 * 1024 * 1024)
CHUNK = 128


def mxu(a, b, a_dim, b_dim):
    return lax.dot_general(a, b, (((a_dim,), (b_dim,)), ((), ())), preferred_element_type=F32)


def whole(shape):
    return pl.BlockSpec(shape, lambda *_: (0,) * len(shape))


def call(body, roles, after, *, in_specs, out_specs, out_shape, grid, name, scratch_shapes=()):
    n_in, n_after, n_out = len(in_specs), len(after), len(out_specs)

    def run(roles_ref, *refs):
        outs = refs[n_in + n_after :]
        outs[n_out][...] = jnp.zeros((8, 128), F32)
        body(roles_ref, *refs[:n_in], *outs[:n_out], *outs[n_out + 1 :])

    def apply(*args):
        outs = pl.pallas_call(
            run,
            grid_spec=pltpu.PrefetchScalarGridSpec(
                num_scalar_prefetch=1,
                grid=grid,
                in_specs=[*in_specs, *[pl.BlockSpec(memory_space=pl.ANY)] * n_after],
                out_specs=[*out_specs, whole((8, 128))],
                scratch_shapes=scratch_shapes,
            ),
            out_shape=[*out_shape, jax.ShapeDtypeStruct((8, 128), F32)],
            compiler_params=PARAMS,
            cost_estimate=pl.CostEstimate(flops=1, bytes_accessed=1, transcendentals=0),
            name=name,
        )(roles, *args, *after)
        return outs[:-1], outs[-1]

    return apply


def attend_forward_body(share, heads, roles, *refs):
    own, others = refs[0], refs[1:share]
    p_ref, o_ref = refs[share:]
    part = heads * HD
    rows = lax.broadcasted_iota(jnp.int32, (part, own.shape[1]), 0) // HD
    lanes = lax.broadcasted_iota(jnp.int32, (own.shape[1], part), 1) // HD
    q = own[0, :, :part] * jnp.asarray(HD**-0.5, BF16)
    k = jnp.concatenate([r[0, :, part : 2 * part] for r in (own, *others)], axis=0)
    v = jnp.concatenate([r[0, :, 2 * part :] for r in (own, *others)], axis=0)
    total = jnp.zeros((part, q.shape[0]), F32)
    for h in range(heads):
        s = mxu(k, jnp.where(lanes == h, q, jnp.zeros_like(q)), 1, 1)
        p = jnp.exp(s - jnp.max(s, axis=0, keepdims=True))
        low = (p * (1.0 / jnp.sum(p, axis=0, keepdims=True))).astype(BF16)
        p_ref[0, h] = low
        total = total + jnp.where(rows == h, mxu(v, low, 0, 0), 0.0)
    o_ref[0] = total.T.astype(BF16)


def other_specs(share, shape):
    return [pl.BlockSpec(shape, lambda x, _, d=d: (x ^ (d >> 1), 0, 0)) for d in range(1, share)]


def attend_forward(roles, after, own, others):
    blocks, count, cols = own.shape
    share = 1 + len(others)
    part = cols // 3
    heads = part // HD
    return call(
        functools.partial(attend_forward_body, share, heads),
        roles,
        after,
        grid=(blocks,),
        in_specs=[pl.BlockSpec((1, count, cols), lambda x, _: (x, 0, 0))] + other_specs(share, (1, count, cols)),
        out_specs=[
            pl.BlockSpec((1, heads, share * count, count), lambda x, _: (x, 0, 0, 0)),
            pl.BlockSpec((1, count, part), lambda x, _: (x, 0, 0)),
        ],
        out_shape=[
            jax.ShapeDtypeStruct((blocks, heads, share * count, count), BF16),
            jax.ShapeDtypeStruct((blocks, count, part), BF16),
        ],
        name="attend_forward",
    )(own, *others)


def attend_backward_body(share, heads, roles, *refs):
    own, others = refs[0], refs[1:share]
    p_ref, o_ref, g_ref = refs[share : share + 3]
    outs = refs[share + 3 :]
    part = heads * HD
    count = own.shape[1]
    q = own[0, :, :part] * jnp.asarray(HD**-0.5, BF16)
    k = jnp.concatenate([r[0, :, part : 2 * part] for r in (own, *others)], axis=0)
    v = jnp.concatenate([r[0, :, 2 * part :] for r in (own, *others)], axis=0)
    g = g_ref[0]
    rows = lax.broadcasted_iota(jnp.int32, (part, count), 0) // HD
    lanes = lax.broadcasted_iota(jnp.int32, (count, part), 1) // HD
    prod = (g.astype(F32) * o_ref[0].astype(F32)).T
    dq = jnp.zeros((part, count), F32)
    dk = jnp.zeros((share * count, part), F32)
    dv = jnp.zeros((share * count, part), F32)
    for h in range(heads):
        q_h = jnp.where(lanes == h, q, jnp.zeros_like(q))
        g_h = jnp.where(lanes == h, g, jnp.zeros_like(g))
        p = p_ref[0, h]
        delta = jnp.sum(prod[h * HD : (h + 1) * HD], axis=0, keepdims=True)
        ds = (p.astype(F32) * (mxu(v, g_h, 1, 1) - delta)).astype(BF16)
        dq = dq + jnp.where(rows == h, mxu(k, ds, 0, 0), 0.0)
        dk = dk + mxu(ds, q_h, 1, 0)
        dv = dv + mxu(p, g_h, 1, 0)
    outs[0][0, :, :part] = (dq.T * (HD**-0.5)).astype(BF16)
    outs[0][0, :, part : 2 * part] = dk[:count].astype(BF16)
    outs[0][0, :, 2 * part :] = dv[:count].astype(BF16)
    for d in range(1, share):
        outs[d][0, :, :part] = dk[d * count : (d + 1) * count].astype(BF16)
        outs[d][0, :, part:] = dv[d * count : (d + 1) * count].astype(BF16)


def attend_backward(roles, after, own, others, probs, attended, grad):
    blocks, count, cols = own.shape
    share = 1 + len(others)
    part = cols // 3
    heads = part // HD
    spec = pl.BlockSpec((1, count, cols), lambda x, _: (x, 0, 0))
    o_spec = pl.BlockSpec((1, count, part), lambda x, _: (x, 0, 0))
    p_spec = pl.BlockSpec((1, heads, share * count, count), lambda x, _: (x, 0, 0, 0))
    return call(
        functools.partial(attend_backward_body, share, heads),
        roles,
        after,
        grid=(blocks,),
        in_specs=[spec] + other_specs(share, (1, count, cols)) + [p_spec, o_spec, o_spec],
        out_specs=[spec] + other_specs(share, (1, count, 2 * part)),
        out_shape=[jax.ShapeDtypeStruct((blocks, count, cols), BF16)]
        + [jax.ShapeDtypeStruct((blocks, count, 2 * part), BF16)] * (share - 1),
        name="attend_backward",
    )(own, *others, probs, attended, grad)


def up_tiles(left, w, k, parts, roles):
    rows = left.shape[1] // parts

    def term(x, h, at):
        return mxu(left[:, pl.ds(at * rows, rows)], w[x][h], 1, 0)

    if parts != 2:
        return [sum(term(x, h, h) for h in range(parts)) for x in range(2)]
    role = roles[k]
    one, two = term(0, 1, 1 - role), term(1, 0, role)
    return [
        term(0, 0, 0) + jnp.where(role == 0, one, two),
        term(1, 1, 1) + jnp.where(role == 0, two, one),
    ]


def up_body(ks, parts, step, roles, *refs):
    left = refs[0]
    for i, k in enumerate(ks):
        for x, tile in enumerate(up_tiles(left, refs[1 + 2 * i : 3 + 2 * i], k, parts, roles)):
            step(i, x, tile, refs[1 + 2 * len(ks) :])


def up(roles, after, name, left, weights, ks, width, col, step, outs, tile):
    parts, rows, _ = weights[0][0].shape
    per = width // tile
    count = left.shape[0]
    return call(
        functools.partial(up_body, ks, parts, step),
        roles,
        after,
        grid=(per,),
        in_specs=[whole((count, parts * rows))]
        + [pl.BlockSpec((parts, rows, tile), lambda n, _: (0, 0, col * per + n))] * (2 * len(ks)),
        out_specs=[pl.BlockSpec((2, o[0], tile), lambda n, _: (0, 0, n)) for o in outs],
        out_shape=[jax.ShapeDtypeStruct((2, o[0], width), o[1]) for o in outs],
        name=name,
    )(left, *[a for w in weights for a in w])


def up_grad_body(k, parts, step, n_extra, n_out, n_more, roles, left, left_t, *refs):
    w, extras, more = refs[:2], refs[2 : 2 + n_extra], refs[2 + n_extra : 2 + n_extra + n_more]
    outs = refs[2 + n_extra + n_more : 2 + n_extra + n_more + n_out]
    ends, kept = refs[2 + n_extra + n_more + n_out : -1], refs[-1]
    for x, tile in enumerate(up_tiles(left, w, k, parts, roles)):
        kept[x] = step(x, tile, extras, outs)
    rows = left_t.shape[0] // parts
    role = roles[k]
    for a in range(2):
        for b in range(parts):
            total = mxu(left_t[pl.ds((b + role * (a - b)) * rows, rows), :], kept[a + role * (b - a)], 1, 0)
            if n_more:
                ends[a][b] = (total + more[0][a, b].astype(F32)).astype(BF16)
            else:
                ends[0][a, b] = total.astype(BF16)


def up_grad(roles, after, name, left, left_t, weights, k, col, step, extras, outs, more=()):
    parts, rows, _ = weights[0].shape
    tile = 512
    width = extras[0].shape[2]
    per = width // tile
    count = left.shape[0]
    thin = lambda r: pl.BlockSpec((2, r, tile), lambda n, _: (0, 0, n))
    pair = pl.BlockSpec((2, parts, rows, tile), lambda n, _: (0, 0, 0, n))
    single = pl.BlockSpec((parts, rows, tile), lambda n, _: (0, 0, n))
    ends = [(single, (parts, rows, width))] * 2 if more else [(pair, (2, parts, rows, width))]
    return call(
        functools.partial(up_grad_body, k, parts, step, len(extras), len(outs), len(more)),
        roles,
        after,
        grid=(per,),
        in_specs=[whole(left.shape), whole(left_t.shape)]
        + [pl.BlockSpec((parts, rows, tile), lambda n, _: (0, 0, col * per + n))] * 2
        + [thin(e.shape[1]) for e in extras]
        + [pair] * len(more),
        out_specs=[thin(o[0]) for o in outs] + [e[0] for e in ends],
        out_shape=[jax.ShapeDtypeStruct((2, o[0], width), o[1]) for o in outs]
        + [jax.ShapeDtypeStruct(e[1], BF16) for e in ends],
        scratch_shapes=[pltpu.VMEM((2, count, tile), BF16)],
        name=name,
    )(left, left_t, *weights, *extras, *more)


def plain_step(i, x, total, refs):
    refs[i][x] = total.astype(BF16)


def gelu_step(x, total, extras, outs):
    act, slope = outs
    v = total + extras[0][x]
    half = 0.5 * (1.0 + lax.erf(v * (0.5**0.5)))
    low = (v * half).astype(BF16)
    act[x] = low
    slope[x] = (half + v * jnp.exp(-0.5 * v * v) * 0.3989422804014327).astype(BF16)
    return low


def slope_step(x, total, extras, outs):
    grad, sums = outs
    low = (total * extras[0][x].astype(F32)).astype(BF16)
    grad[x] = low
    sums[x] = jnp.sum(low.astype(F32), axis=0, keepdims=True)
    return low


def down_body(parts, per, finish, n_extra, n_out, n_in, body, roles, *refs):
    extras = refs[6 : 6 + n_extra]
    outs = refs[6 + n_extra + n_in : 6 + n_extra + n_in + n_out]
    acc = refs[-1]
    n = pl.program_id(0)

    @pl.when(n < per)
    def _():
        total = [0] * parts
        for k in range(2):
            left, w = refs[k], refs[2 + 2 * k : 4 + 2 * k]

            def term(x, h, at):
                return mxu(left[at], w[x][h], 1, 1)

            if parts == 2:
                role = roles[k]
                one, two = term(0, 1, role), term(1, 0, 1 - role)
                total[0] = total[0] + term(0, 0, 0) + jnp.where(role == 0, two, one)
                total[1] = total[1] + term(1, 1, 1) + jnp.where(role == 0, one, two)
            else:
                for h in range(parts):
                    total[h] = total[h] + term(0, h, 0) + term(1, h, 1)
        for h in range(parts):
            acc[h * per + n] = total[h]

    @pl.when(n == per - 1)
    def _():
        finish(acc, [*extras, *outs])

    if body is not None:

        @pl.when(n >= per)
        def _():
            body(roles, outs, refs[6 + n_extra : 6 + n_extra + n_in], refs[6 + n_extra + n_in + n_out : -1])


def down(roles, after, name, lefts, weights, width, col, finish, extras, outs, then=(0, None, [], [])):
    parts, rows, _ = weights[0][0].shape
    tile = min(256, rows)
    per = rows // tile
    count = lefts[0].shape[1]
    steps, body, ins, more = then

    def late(block, index):
        return pl.BlockSpec(block, lambda n, _: index(jnp.maximum(n - per, 0)))

    return call(
        functools.partial(down_body, parts, per, finish, len(extras), len(outs), len(ins), body),
        roles,
        after,
        grid=(per + steps,),
        in_specs=[whole((2, count, width))] * 2
        + [pl.BlockSpec((parts, tile, width), lambda n, _: (0, jnp.minimum(n, per - 1), col))] * 4
        + [whole(e.shape) for e in extras]
        + [late(*i[1:]) for i in ins],
        out_specs=[whole(o[0]) for o in outs] + [late(*m[2:]) for m in more],
        out_shape=[jax.ShapeDtypeStruct(*o) for o in outs] + [jax.ShapeDtypeStruct(*m[:2]) for m in more],
        scratch_shapes=[pltpu.VMEM((parts * rows // tile, count, tile), F32)],
        name=name,
    )(*lefts, *weights[0], *weights[1], *extras, *[i[0] for i in ins])


def then_up(place, weights, width, col, tile):
    parts, rows, _ = weights[0][0].shape
    per = width // tile

    def body(roles, outs, ins, ends):
        for k in range(2):
            for x, total in enumerate(up_tiles(outs[place], ins[2 * k : 2 * k + 2], k, parts, roles)):
                ends[k][x] = total.astype(BF16)

    def of(count):
        return (
            per,
            body,
            [(a, (parts, rows, tile), lambda m: (0, 0, col * per + m)) for w in weights for a in w],
            [((2, count, width), BF16, (2, count, tile), lambda m: (0, 0, m))] * 2,
        )

    return of


def then_grad(place, right, parts):
    _, count, cols = right.shape

    def body(roles, outs, ins, ends):
        b = pl.program_id(0) - pl.num_programs(0) + parts
        rows = outs[place].shape[0] // parts
        role = roles[1]
        for a in range(2):
            left = outs[place][pl.ds((b + role * (a - b)) * rows, rows), :]
            ends[0][a] = mxu(left, ins[0][a + role * (b - a)], 1, 0).astype(BF16)

    def of(depth):
        rows = depth // parts
        return (
            parts,
            body,
            [(right, right.shape, lambda m: (0, 0, 0))],
            [((2, parts, rows, cols), BF16, (2, None, rows, cols), lambda m: (0, m, 0, 0))],
        )

    return of


def row_mean(tiles):
    total = sum(jnp.sum(t, axis=-1, keepdims=True) for t in tiles)
    return total / sum(t.shape[-1] for t in tiles)


def norm_finish(has_residual, acc, refs):
    refs = list(refs)
    residual = refs.pop(0) if has_residual else None
    rows, total_ref, low_ref, low_t_ref = refs
    tiles, count, width = acc.shape
    for r in range(0, count, CHUNK):
        rr = pl.ds(r, CHUNK)
        total = []
        for i in range(tiles):
            cc = slice(i * width, (i + 1) * width)
            v = acc[i, rr, :] + rows[0:1, cc]
            if residual is not None:
                v = v + residual[rr, cc]
            total_ref[rr, cc] = v
            total.append(v)
        mean = row_mean(total)
        center = [t - mean for t in total]
        scale = lax.rsqrt(row_mean([c * c for c in center]) + EPSILON)
        for i in range(tiles):
            cc = slice(i * width, (i + 1) * width)
            v = center[i] * scale * rows[1:2, cc] + rows[2:3, cc]
            low_ref[rr, cc] = v.astype(BF16)
            low_t_ref[cc, rr] = v.T.astype(BF16)


def norm_back_finish(keep, acc, refs):
    total_ref, up_ref, rows, *outs = refs
    full_ref = outs.pop(0) if keep else None
    low_ref, low_t_ref, sums_ref = outs
    tiles, count, width = acc.shape
    zero = jnp.zeros((1, width), F32)
    sums = [[zero] * tiles for _ in range(4)]
    for r in range(0, count, CHUNK):
        rr = pl.ds(r, CHUNK)
        cuts = [slice(i * width, (i + 1) * width) for i in range(tiles)]
        total = [total_ref[rr, cc] for cc in cuts]
        mean = row_mean(total)
        center = [t - mean for t in total]
        scale = lax.rsqrt(row_mean([c * c for c in center]) + EPSILON)
        unit = [c * scale for c in center]
        grad = [acc[i, rr, :] for i in range(tiles)]
        z = [g * rows[0:1, cc] for g, cc in zip(grad, cuts)]
        z_mean = row_mean(z)
        zu_mean = row_mean([a * b for a, b in zip(z, unit)])
        for i, cc in enumerate(cuts):
            up_now = up_ref[rr, cc].astype(F32)
            v = up_now + scale * (z[i] - z_mean - unit[i] * zu_mean)
            if keep:
                full_ref[rr, cc] = v
            low_ref[rr, cc] = v.astype(BF16)
            low_t_ref[cc, rr] = v.T.astype(BF16)
            for j, s in enumerate((v, grad[i] * unit[i], grad[i], up_now)):
                sums[j][i] = sums[j][i] + jnp.sum(s, axis=0, keepdims=True)
    for j in range(4):
        for i in range(tiles):
            sums_ref[j : j + 1, i * width : (i + 1) * width] = sums[j][i]


def out_finish(acc, refs):
    total_ref, rows, low_ref = refs
    tiles, count, width = acc.shape
    for i in range(tiles):
        cc = slice(i * width, (i + 1) * width)
        v = (acc[i] + total_ref[:, cc] + rows[0:1, cc]) * rows[1:2, cc]
        low_ref[:, cc] = v.astype(BF16)


def arrived_body(roles, cot, permute, live, low_ref, low_t_ref):
    low = mxu(cot[...], permute[...], 1, 0) * live[...]
    low_ref[...] = low.astype(BF16)
    low_t_ref[...] = low.T.astype(BF16)


def arrived(roles, after, cot, permute, live):
    count, width = cot.shape
    tile = min(256, width)
    return call(
        arrived_body,
        roles,
        after,
        grid=(width // tile,),
        in_specs=[whole(cot.shape), pl.BlockSpec((width, tile), lambda n, _: (0, n)), whole((1, 1))],
        out_specs=[pl.BlockSpec((count, tile), lambda n, _: (0, n)), pl.BlockSpec((tile, count), lambda n, _: (n, 0))],
        out_shape=[jax.ShapeDtypeStruct((count, width), BF16), jax.ShapeDtypeStruct((width, count), BF16)],
        name="arrived",
    )(cot, permute, live.reshape(1, 1))


def weight_grad_body(n_parts, n_more, own, roles, *refs):
    ends = refs[4 * n_parts + n_more :]
    for a in range(2):
        at = 0
        more = [m[a].astype(F32) for m in refs[4 * n_parts : 4 * n_parts + n_more]]
        for p in range(n_parts):
            left, right = refs[4 * p + 2 * a : 4 * p + 2 * a + 2]
            total = mxu(left[...], right[...], 1, 0)
            cc = slice(at, at + total.shape[1])
            at = cc.stop
            if own:
                start = 0
                for m in more:
                    if start <= cc.start and cc.stop <= start + m.shape[1]:
                        total = total + m[:, cc.start - start : cc.stop - start]
                    start += m.shape[1]
                ends[a][:, cc] = total.astype(BF16)
            else:
                ends[0][a, :, cc] = total.astype(BF16)


def weight_grad(roles, after, lefts, rights, parts, k, more=()):
    depth, count = lefts[0].shape
    rows = depth // parts
    tile = rows
    per = rows // tile
    cols = sum(r.shape[2] for r in rights)
    own = k == 0
    specs, args = [], []
    for left, right in zip(lefts, rights):
        for a in range(2):
            specs += [
                pl.BlockSpec((tile, count), lambda b, n, p, a=a: ((b + p[k] * (a - b)) * per + n, 0)),
                pl.BlockSpec((None, count, right.shape[2]), lambda b, n, p, a=a: (a + p[k] * (b - a), 0, 0)),
            ]
            args += [left, right]
    pair = lambda width: pl.BlockSpec((2, None, tile, width), lambda b, n, _: (0, b, n, 0))
    if own:
        out_specs = [pl.BlockSpec((None, tile, cols), lambda b, n, _: (b, n, 0))] * 2
        out_shape = [jax.ShapeDtypeStruct((parts, rows, cols), BF16)] * 2
    else:
        out_specs = [pair(cols)]
        out_shape = [jax.ShapeDtypeStruct((2, parts, rows, cols), BF16)]
    return call(
        functools.partial(weight_grad_body, len(lefts), len(more), own),
        roles,
        after,
        grid=(parts, per),
        in_specs=specs + [pair(m.shape[3]) for m in more],
        out_specs=out_specs,
        out_shape=out_shape,
        name="weight_grad",
    )(*args, *more)


def pick(array, index, axis=0):
    return lax.dynamic_index_in_dim(array, index, axis, keepdims=False)


def add(*terms):
    return sum(t.astype(F32) for t in terms).astype(BF16)


class Line:
    def __init__(self, roles):
        self.roles, self.marks = roles, []

    def gate(self, *arrays):
        leaves, form = jax.tree.flatten(arrays)
        places = [i for i, leaf in enumerate(leaves) if isinstance(leaf, jax.Array)]
        held, self.marks = lax.optimization_barrier(([leaves[i] for i in places], self.marks))
        for i, array in zip(places, held):
            leaves[i] = array
        arrays = jax.tree.unflatten(form, leaves)
        return arrays[0] if len(arrays) == 1 else arrays

    def plain(self, step, *args):
        out = step(*self.gate(args, ())[0])
        self.marks = self.marks + jax.tree.leaves(out)
        return out

    def __call__(self, step, *args):
        args = self.gate(args, ())[0]
        out, mark = step(self.roles, self.marks, *args)
        self.marks = [mark]
        return out


def on_device(
    sizes,
    tokens,
    skip_tokens,
    merger_weight,
    merger_bias,
    first_gain,
    first_shift,
    attend_weight,
    output_weight,
    output_bias,
    second_gain,
    second_shift,
    expand_weight,
    widen_bias,
    shrink_weight,
    shrink_bias,
    live_slots,
    cotangent,
):
    fs, cs, ts = sizes
    assert ts == 4
    f_rank, c_rank, t_rank = (lax.axis_index(a) for a in ALL)
    group = cs * ts
    devices = fs * group
    batches, local_seqs, local_len, part_width = tokens.shape
    slots = batches * local_seqs
    share = group // slots
    assert share in (1, 2, 4)
    fine = cotangent.shape[2] // share
    width = cotangent.shape[3]
    count = group * fine
    hidden = expand_weight.shape[1]
    rows = width // (fs * cs)
    role = t_rank % 2 if fs == 2 else 0 * t_rank
    line = Line(jnp.stack([role, (1 - role) if fs == 2 else role]).astype(jnp.int32))

    def to_group(array):
        return lax.all_to_all(array, ("ctx", "tp"), 0, 0, tiled=True)

    def over_tp(array, flip):
        return lax.ppermute(array, "tp", [(i, i ^ flip) for i in range(ts)])

    ring = list(range(0, cs, 2)) + list(range(cs - 1 - cs % 2, 0, -2))

    def over_ctx(array, d):
        return lax.ppermute(array, "ctx", [(ring[i], ring[(i + d) % cs]) for i in range(cs)])

    def ctx_behind(d):
        return jnp.asarray([ring[(ring.index(i) - d) % cs] for i in range(cs)], jnp.int32)[c_rank]

    def over_fsdp(array, d):
        return lax.ppermute(array, "fsdp", [(i, (i + d) % fs) for i in range(fs)])

    def first_pairs(i):
        f, c, t = i // (cs * ts), i // ts % cs, i % ts
        f, t = (f, t ^ 2) if t % 2 else (1 - f, t)
        return (f * cs + c) * ts + t

    def second_pairs(i):
        f, c, t = i // (cs * ts), i // ts % cs, i % ts
        f, t = (1 - f, t) if t % 2 else (f, t ^ 2)
        return (f * cs + c) * ts + t

    def over(array, target):
        return lax.ppermute(array, ALL, [(i, target(i)) for i in range(devices)])

    def gather_ctx(piece):
        return [piece] + [over_ctx(piece, d) for d in range(1, cs)]

    def ring_start(piece):
        return [piece, over_ctx(piece, 1)]

    def ring_step(moved):
        *kept, last = moved
        last = line.gate(last)
        return [*kept, last, over_ctx(last, 1)] if len(moved) < cs else [*kept, last]

    def gather_one(moved):
        own = line.plain(lambda *m: jnp.concatenate(m, axis=0), *moved)
        return own, [over(own, first_pairs)] if fs == 2 else [over_fsdp(own, h) for h in range(1, fs)]

    def gather_two(own, moved):
        first = line.plain(lambda a, m: jnp.stack([a, *m]), own, moved)
        return first, second_move(first)

    def second_move(first):
        return over(first, second_pairs) if fs == 2 else over_tp(first, 2)

    def gather_near(first, second):
        first = line.gate(first)
        return first, second, over_tp(first, 1)

    def gather_three(first, second, other):
        first, second, other = line.gate(first, second, other)
        return [[first, second], [other, over_tp(second, 1)]]

    def reduce_one(sums):
        keep, send = sums
        return keep, over(send, second_pairs) if fs == 2 else over_tp(send, 2)

    def reduce_two(keep, moved):
        sums = line.plain(lambda a, m: [add(a[h], m[h]) for h in range(fs)], keep, moved)
        if fs == 2:
            return sums[0], [over(sums[1], first_pairs)]
        return sums[0], [over_fsdp(sums[h], -h) for h in range(1, fs)]

    def reduce_three(*sums):
        def pieces(*sums):
            total = jnp.concatenate([add(own, *moved) for own, moved in sums], axis=1).reshape(cs, rows, -1)
            return [total[d] for d in range(cs)]

        parts = line.plain(pieces, *sums)
        return parts, over_ctx(parts[-1], -1)

    def reduce_step(parts, moving):
        *parts, last = line.plain(lambda p, m: [*p[:-2], add(p[-2], m)], parts, moving)
        return [*parts, last], over_ctx(last, -1)

    def reduce_last(parts, moving):
        while len(parts) > 2:
            parts, moving = reduce_step(parts, moving)
        return line.plain(lambda p, m: p.astype(F32) + m.astype(F32), parts[0], moving)

    spread = lambda blocks: [blocks[0][0], blocks[1][0], blocks[0][1], blocks[1][1]]
    owner = jnp.stack(
        [(f_rank - h) % fs * cs + ctx_behind(d) for h in range(fs) for d in range(cs)]
    )
    features = lax.broadcasted_iota(jnp.int32, (width, width), 0)
    places = (owner[:, None] * rows + jnp.arange(rows)[None, :]).reshape(1, width)
    permute = (features == places).astype(BF16)

    def relative(array, axis=0):
        return [
            jnp.stack([pick(array, t_rank ^ (2 * x + k), axis) for x in range(2)]) for k in range(2)
        ]

    def absolute(blocks):
        blocks = jnp.stack(spread(blocks))
        return jnp.stack([pick(blocks, t_rank ^ t) for t in range(ts)])

    flat = lambda w: w.reshape(w.shape[0], -1)
    side = merger_weight.shape[1] * merger_weight.shape[2]
    heads_width = output_weight.shape[1]

    def pack_att(m, o, a):
        return jnp.concatenate([flat(m), o, flat(a)], axis=1)

    def split_rows(one, two):
        array = jnp.concatenate([one, two], axis=-1)
        array = array.reshape(slots, ts, share, fine, -1).transpose(0, 2, 1, 3, 4)
        return array.reshape(group * ts * fine, -1)

    small = merger_bias.shape[0]
    att = gather_ctx(line.plain(pack_att, merger_weight, output_weight, attend_weight))
    packed = line.plain(
        lambda *v: jnp.broadcast_to(jnp.concatenate(v), (devices, sum(x.shape[0] for x in v))),
        merger_bias, first_gain, first_shift, output_bias, second_gain, second_shift, shrink_bias, widen_bias,
    )
    packed = lax.all_to_all(packed, ALL, 0, 0, tiled=True)
    both = line.plain(split_rows, tokens, skip_tokens)
    ffn = line.plain(lambda a, b: jnp.concatenate([a, b], axis=1), expand_weight, shrink_weight)
    packed = line.gate(packed)
    cot = to_group(line.gate(cotangent).reshape(group * fine, width))
    att = gather_one(att)
    ffn = ring_start(line.gate(ffn))
    ffn = ring_step(ffn)
    att = gather_near(*gather_two(*att))
    for _ in range(3, cs):
        ffn = ring_step(ffn)
    cot = line.gate(cot)
    both = to_group(line.gate(both))
    ffn = gather_one(ring_step(ffn))

    live = pick(live_slots.reshape(slots), (c_rank * ts + t_rank) // share).astype(F32)
    branch_low, branch_low_t = line(arrived, cot.reshape(count, width), permute, live)

    def vectors_of(packed):
        vectors = packed[:, : 7 * small].reshape(fs * cs, ts, 7, small).transpose(0, 2, 1, 3)
        vectors = vectors.reshape(fs * cs, 7, rows)
        vectors = jnp.stack([pick(vectors, owner[i]) for i in range(fs * cs)], axis=1).reshape(7, width)
        return vectors, relative(packed[:, 7 * small :].reshape(ts, 1, hidden))

    def blocks_of(both):
        both = relative(both.reshape(cs, ts, ts * fine, side), 1)
        return [b.reshape(2, count, side) for b in both]

    vectors, widen = line.plain(vectors_of, packed)
    att = gather_three(*att)
    both = line.plain(blocks_of, both)
    act = (count, width)
    turned = (width, count)
    flows = [(count, BF16)] * 2

    joined, normed, normed_t, *project = line(
        lambda *o: down(
            *o[:2], "joined", o[2], o[3], side, 0, functools.partial(norm_finish, False), [o[4][0:3]],
            [(act, F32), (act, BF16), (turned, BF16)],
            then_up(1, o[3], 3 * heads_width, 1, heads_width)(count),
        ),
        both, att, vectors,
    )
    def halves(own, moved):
        cuts = [slice(0, hidden), slice(hidden, None)]
        return [jnp.stack([p[:, cc] for p in (own, *moved)]) for cc in cuts]

    expand, shrink = [(p, second_move(p)) for p in line.plain(halves, *ffn)]
    others = [[over_tp(project[k ^ (d & 1)], d) for d in range(1, share)] for k in range(2)]
    others = line.gate(others)
    inner = [line(attend_forward, project[0], others[0])]
    expand = gather_near(*expand)
    inner.append(line(attend_forward, project[1], others[1]))
    shrink = gather_near(*shrink)
    probs, attended = zip(*inner)

    expand = gather_three(*expand)
    second, normed_two, normed_two_t = line(
        lambda *o: down(
            *o[:2], "second", o[2], o[3], heads_width, side // heads_width, functools.partial(norm_finish, True),
            [o[4], o[5][3:6]], [(act, F32), (act, BF16), (turned, BF16)],
        ),
        attended, att, joined, vectors,
    )

    def grads(k):
        return lambda roles, after, lefts, rights, more=(): weight_grad(roles, after, lefts, rights, fs, k, more)

    def other_grads(lefts, rights):
        return over_tp(line(grads(1), lefts, rights)[0], 1)

    def hidden_step(k):
        return lambda *o: up_grad(*o[:2], "hidden", *o[2:5], k, 0, gelu_step, [o[5]], flows, *o[6:])

    def hidden_back(k):
        return lambda *o: up_grad(
            *o[:2], "hidden_back", *o[2:5], k, 0, slope_step, [o[5]], [(count, BF16), (1, F32)], *o[6:]
        )

    shrink = gather_three(*shrink)
    activated, slope, grad_expanded, wide = ([None, None] for _ in range(4))
    activated[1], slope[1], other = line(hidden_step(1), normed_two, branch_low_t, expand[1], widen[1])
    other = over_tp(other, 1)
    grad_expanded[1], wide[1], other_two = line(hidden_back(1), branch_low, normed_two_t, shrink[1], slope[1])
    other_two = over_tp(other_two, 1)
    activated[0], slope[0], *sums = line(hidden_step(0), normed_two, branch_low_t, expand[0], widen[0], [other])
    shrink_sums = reduce_one(sums)
    grad_expanded[0], wide[0], *sums = line(hidden_back(0), branch_low, normed_two_t, shrink[0], slope[0], [other_two])
    expand_sums = reduce_one(sums)
    grad_second, attn_low, attn_low_t, sums_two, *grad_attended = line(
        lambda *o: down(
            *o[:2], "second_back", o[2], o[3], hidden, 0, functools.partial(norm_back_finish, True),
            [o[4], o[5], o[6][4:5]], [(act, F32), (act, BF16), (turned, BF16), ((4, width), F32)],
            then_up(1, o[7], heads_width, side // heads_width, heads_width // 2)(count),
        ),
        grad_expanded, expand, second, branch_low, vectors, att,
    )
    shrink_sums = reduce_two(*shrink_sums)
    inner = [None, None]
    inner[1] = line(attend_backward, project[1], others[1], probs[1], attended[1], grad_attended[1])

    def layer_end(roles, after, a, w, t, v):
        ends = jnp.stack([v[6], jnp.full((width,), live)])
        return down(roles, after, "layer_out", a, w, hidden, 0, out_finish, [t, ends], [(act, BF16)])

    (layer_out,) = line(layer_end, activated, shrink, second, vectors)
    layer_out = line.plain(lambda a, p: mxu(a, p, 1, 1).astype(BF16), layer_out, permute)
    layer_out = to_group(layer_out.reshape(group * fine, width))
    expand_sums = reduce_two(*expand_sums)
    inner[0] = line(attend_backward, project[0], others[0], probs[0], attended[0], grad_attended[0])
    ffn_sums = reduce_three(shrink_sums, expand_sums)

    def close(k):
        def total(own, *moves):
            third = own.shape[2] // 3
            return jnp.concatenate([own[:, :, :third], add(own[:, :, third:], *moves)], axis=-1)

        moves = [over_tp(inner[k ^ (d & 1)][d], d) for d in range(1, share)]
        return line.plain(total, inner[k][0], *moves)

    grad_project = [None, None]
    grad_project[1] = close(1)
    attend_other = other_grads([attn_low_t, normed_t], [attended[1], grad_project[1]])
    grad_project[0] = close(0)
    joined_low, joined_low_t, sums_one, merger_other = line(
        lambda *o: down(
            *o[:2], "first_back", o[2], o[3], 3 * heads_width, 1, functools.partial(norm_back_finish, False),
            [o[4], o[5], o[6][1:2]], [(act, BF16), (turned, BF16), ((4, width), F32)],
            then_grad(1, o[7], fs)(width),
        ),
        grad_project, att, joined, grad_second, vectors, both[1],
    )
    merger_other = over_tp(merger_other, 1)
    out = line(
        lambda *o: up(*o[:2], "inputs_back", *o[2:], (0, 1), side, 0, plain_step, flows, 256),
        joined_low, att,
    )
    att_sums = reduce_one(
        line(
            grads(0), [joined_low_t, attn_low_t, normed_t], [both[0], attended[0], grad_project[0]],
            [merger_other, attend_other],
        )
    )
    layer_out = line.gate(layer_out)
    def turn_back(out):
        out = absolute(out).reshape(ts, cs, ts * fine, side)
        return out.transpose(1, 0, 2, 3).reshape(group * ts * fine, side)

    out = to_group(line.plain(turn_back, out))
    ffn_sums = reduce_step(*ffn_sums)
    def vector_sums(one, two, wide):
        sums = jnp.concatenate([one[0:3], two]).reshape(7, fs * cs, rows)
        place = jnp.asarray([ring.index(i) for i in range(cs)], jnp.int32)[c_rank]
        places = [(f_rank - f) % fs * cs + (place - ring.index(c)) % cs for f in range(fs) for c in range(cs)]
        sums = jnp.stack([pick(sums, p, 1) for p in places])
        sums = sums.reshape(fs * cs, 7, ts, small).transpose(0, 2, 1, 3).reshape(devices, 7 * small)
        return jnp.concatenate([sums, absolute(wide).reshape(devices, -1)], axis=1)

    vec = line.plain(vector_sums, sums_one, sums_two, wide).reshape(fs, cs, 2, 2, -1)
    moved = over_tp(pick(vec, 1 - t_rank % 2, 3), 1)
    ffn_sums = reduce_step(*ffn_sums)
    vec = line.plain(lambda v, m: pick(v, t_rank % 2, 3) + m, vec, moved)
    moved = over_tp(pick(vec, 1 - t_rank // 2, 2), 2)
    out = line.gate(out)
    att_sums = reduce_two(*att_sums)
    vec = line.plain(lambda v, m: pick(v, t_rank // 2, 2) + m, vec, moved)
    moved = [over_fsdp(pick(vec, (f_rank - h) % fs), -h) for h in range(1, fs)]
    grad_ffn = reduce_last(*ffn_sums)

    def unpack(out, layer_out):
        out = out.reshape(slots, share, ts, fine, side).transpose(0, 2, 1, 3, 4)
        out = out.reshape(batches, local_seqs, local_len, side).astype(F32)
        layer_out = layer_out.reshape(batches, local_seqs, share * fine, width)
        return out[..., :part_width], out[..., part_width:], layer_out

    grad_tokens, grad_skip, layer_out = line.plain(unpack, out, layer_out)
    att_sums = reduce_three(att_sums)
    vec = line.plain(lambda v, m: sum(m, pick(v, f_rank)), vec, moved)
    moved = [over_ctx(pick(vec, ctx_behind(d)), -d) for d in range(1, cs)]
    att_sums = reduce_step(*att_sums)
    vec = line.plain(lambda v, m: sum(m, pick(v, c_rank)), vec, moved)
    grad_att = reduce_last(*att_sums)
    cut = side + heads_width
    vec_out = [vec[i * small : (i + 1) * small] for i in range(7)] + [vec[7 * small :]]
    return (
        layer_out,
        grad_tokens,
        grad_skip,
        grad_att[:, :side].reshape(merger_weight.shape),
        vec_out[0],
        vec_out[1],
        vec_out[2],
        grad_att[:, cut:].reshape(attend_weight.shape),
        grad_att[:, side:cut],
        vec_out[3],
        vec_out[4],
        vec_out[5],
        grad_ffn[:, hidden:],
        vec_out[7],
        grad_ffn[:, :hidden],
        vec_out[6],
    )


def solution(mesh):
    sizes = tuple(mesh.shape[a] for a in ALL)
    act = P(None, "fsdp", "ctx", "tp")
    vec = P(ALL)
    flat = P(None, "fsdp", ("ctx", "tp"), None)
    w_three = P(("fsdp", "ctx"), None, "tp")
    w_two = P(("fsdp", "ctx"), "tp")
    return jax.shard_map(
        functools.partial(on_device, sizes),
        mesh=mesh,
        in_specs=(
            act, act, w_three, vec, vec, vec, w_three, w_two, vec, vec, vec, w_two, vec, w_two, vec,
            P(None, "fsdp"), flat,
        ),
        out_specs=(
            flat, act, act, w_three, vec, vec, vec, w_three, w_two, vec, vec, vec, w_two, vec, w_two, vec,
        ),
        check_vma=False,
    )
```
